32 devices in a mesh: dp: 2 (over x), ctx: 4 (over z), tp: 4 (over y, core).
Axes of the slice: x: 2, y: 2, z: 4, core: 2. Of those that a mesh axis runs over, the one named last changes fastest.
Arguments:
- hidden_in: bfloat16 [2, 2, 2048, 768], P(None, 'dp', 'ctx'), may hold values from -6 to 6
- prefix: int32 [2, 2], P(None, 'dp'), may hold values from 204 to 1024
- block_order: int32 [8], replicated, may hold values from 0 to 7, each once
- qkv_weight: bfloat16 [3, 768, 768], P(None, 'dp', 'tp'), may hold values from -0.3125 to 0.3125
- out_weight: bfloat16 [768, 768], P('tp', 'dp'), may hold values from -2.5 to 2.5
- up_weight: bfloat16 [768, 3072], P('dp', 'tp'), may hold values from -0.21875 to 0.21875
- down_weight: bfloat16 [3072, 768], P('tp', 'dp'), may hold values from -0.4375 to 0.4375
- ln_gains: bfloat16 [2, 768], P(None, 'dp'), may hold values from 0.5 to 1.5
- ln_shifts: bfloat16 [2, 768], P(None, 'dp'), may hold values from -2 to 2
- cotangent: bfloat16 [2, 2, 2048, 768], P(None, 'dp', 'ctx'), may hold values from -6 to 6
Outputs:
- block_out: bfloat16 [2, 2, 2048, 768], P(None, 'dp', 'ctx')
- grad_in: float32 [2, 2, 2048, 768], P(None, 'dp', 'ctx')
- grad_qkv: float32 [3, 768, 768], P(None, 'dp', 'tp')
- grad_out: float32 [768, 768], P('tp', 'dp')
- grad_up: float32 [768, 3072], P('dp', 'tp')
- grad_down: float32 [3072, 768], P('tp', 'dp')
- grad_gains: float32 [2, 768], P(None, 'dp')
- grad_shifts: float32 [2, 768], P(None, 'dp')
The draws below stay inside these ranges and needn't reach their ends.
Inputs may be any that keep to these rules, and one draw needn't show every extreme that they name: `prefix`: leading positions of each sequence that all of its queries see. `block_order`: each of the 2 * 4 block numbers appears once.
All inputs are finite; a program needn't handle non-finite values.
Results may differ from the reference program's by a relative error of at most 0.012.
The reference program's roundings to bfloat16 on the way count: a program that leaves them out, or rounds other values in their place, can miss the bound.
Values may be sent and summed in bfloat16 or wider, within the bound.
A program may use at most 128 MiB of HBM per device.

```python
import jax
import jax.numpy as jnp
from jax import lax

D = 768
HEADS = 12
HEAD_DIM = 64
FF = 3072
MICRO = 2
DEPTH = 12
LEN = 2048
SEQS = 2
N_CTX = 4


def set_ends(drawn, key, smallest, top_value):
    spot = [jax.random.randint(jax.random.fold_in(key, axis), (), 0, length) for axis, length in enumerate(drawn.shape)]
    longest = drawn.shape.index(max(drawn.shape))
    beside = spot[:longest] + [(spot[longest] + 1) % drawn.shape[longest]] + spot[longest + 1:]
    return drawn.at[tuple(spot)].set(smallest).at[tuple(beside)].set(top_value)


def shard_levels(rng, shape, split, least, largest):
    def one(axis_at, blocks):
        draws = jax.random.uniform(jax.random.fold_in(jax.random.fold_in(rng, 6), axis_at), (blocks,), jnp.float32, least / len(split), largest / len(split))
        return jnp.repeat(jnp.exp(draws), shape[axis_at] // blocks).reshape((-1,) + (1,) * (len(shape) - axis_at - 1))

    gain = one(*split[0])
    for cut in split[1:]:
        gain = gain * one(*cut)
    return gain


def scatter_about(rng, shape, spread, bound, shards=(), kind=jnp.bfloat16):
    drawn = spread * jax.random.normal(rng, shape, jnp.float32)
    if shards:
        drawn = drawn * shard_levels(rng, shape, shards, -0.22, 0.18)
    return jnp.clip(drawn, -bound, bound).astype(kind)


def setup_inputs(seed: int = 0) -> dict:
    arg_keys = jax.random.split(jax.random.key(seed), 11)
    return {
        "hidden_in": scatter_about(arg_keys[0], (MICRO, SEQS, LEN, D), 1.0, 6.0, ((1, 2), (2, 4))),
        "prefix": set_ends(jax.random.randint(arg_keys[1], (MICRO, SEQS), LEN // 10, LEN // 2 + 1), jax.random.fold_in(arg_keys[1], 1), LEN // 10, (LEN // 2 + 1) - 1).astype(jnp.int32),
        "block_order": jax.random.permutation(arg_keys[2], 2 * N_CTX).astype(jnp.int32),
        "qkv_weight": scatter_about(arg_keys[3], (3, D, D), (D // 2) ** -0.5, 0.3125, ((1, 2), (2, 4))),
        "out_weight": scatter_about(arg_keys[4], (D, D), (max(D // 128, 2)) ** -0.5, 2.5, ((0, 4), (1, 2))),
        "up_weight": scatter_about(arg_keys[5], (D, FF), D ** -0.5, 0.21875, ((0, 2), (1, 4))),
        "down_weight": scatter_about(arg_keys[6], (FF, D), (FF // 16) ** -0.5, 0.4375, ((0, 4), (1, 2))),
        "ln_gains": jnp.clip(1.0 + 0.1 * jax.random.normal(arg_keys[7], (2, D), jnp.float32), 0.5, 1.5).astype(jnp.bfloat16),
        "ln_shifts": scatter_about(arg_keys[8], (2, D), 0.3, 2.0, ((1, 2),)),
        "cotangent": scatter_about(arg_keys[9], (MICRO, SEQS, LEN, D), 1.0, 6.0, ((1, 2), (2, 4))),
    }


@jax.custom_vjp
def low(v):
    return lax.optimization_barrier(v.astype(jnp.bfloat16)).astype(jnp.float32)

@jax.custom_vjp
def low_back(v):
    return v

def low_keep(v):
    return (low(v), None)

def low_pass(kept, grad):
    return (grad,)

def back_keep(v):
    return (v, None)

def back_low(kept, grad):
    return (low(grad),)
low.defvjp(low_keep, low_pass)
low_back.defvjp(back_keep, back_low)
EPS = 1e-05
HIGH = lax.Precision.HIGHEST

def mult(left, right):
    return jnp.dot(left, right, precision=HIGH, preferred_element_type=jnp.float32)

def apply_layer_norm(values, norm_gain, norm_shift):
    row_mean = lax.optimization_barrier(jnp.mean(values, axis=-1, keepdims=True))
    centered_input = values - row_mean
    var = lax.optimization_barrier(jnp.mean(centered_input * centered_input, axis=-1, keepdims=True))
    return centered_input * lax.rsqrt(var + EPS) * norm_gain + norm_shift

def gelu_tanh(u):
    return 0.5 * u * (1.0 + jnp.tanh(0.7978845608028654 * (u + 0.044715 * u * u * u)))

def positions(block_order):
    half = LEN // (2 * N_CTX)
    rows = jnp.arange(LEN, dtype=jnp.int32)
    return block_order[rows // half] * half + rows % half

def attend_head(query, keys, values, allowed):
    scores = low_back(mult(query, keys.T) * HEAD_DIM ** (-0.5))
    scores = jnp.where(allowed, scores, -1e+30)
    top = lax.optimization_barrier(jnp.max(scores, axis=1, keepdims=True))
    expd = jnp.exp(scores - top)
    prob = low(expd / lax.optimization_barrier(jnp.sum(expd, axis=1, keepdims=True)))
    return mult(prob, values)

def layer(input_rows, allowed, qkv_w, out_w, up_w, down_w, norm_gains, norm_shifts):
    branch = DEPTH ** (-0.5)
    h1 = low(apply_layer_norm(input_rows, norm_gains[0], norm_shifts[0]))
    query = low(low_back(mult(h1, qkv_w[0])))
    keys = low(low_back(mult(h1, qkv_w[1])))
    values = low(low_back(mult(h1, qkv_w[2])))

    def one_head(index):
        start = (index * HEAD_DIM).astype(jnp.int32)
        return attend_head(lax.dynamic_slice_in_dim(query, start, HEAD_DIM, 1), lax.dynamic_slice_in_dim(keys, start, HEAD_DIM, 1), lax.dynamic_slice_in_dim(values, start, HEAD_DIM, 1), allowed)
    heads = lax.map(jax.checkpoint(one_head), jnp.arange(HEADS, dtype=jnp.int32))
    heads = jnp.transpose(heads, (1, 0, 2)).reshape(LEN, D)
    heads = low(low_back(heads))
    attn = low_back(mult(heads, out_w))
    middle_state = input_rows + branch * attn
    h2 = low(apply_layer_norm(middle_state, norm_gains[1], norm_shifts[1]))
    up = low_back(mult(h2, up_w))
    act = low(gelu_tanh(up))
    mlp = low_back(mult(act, down_w))
    return middle_state + branch * mlp

def reference(hidden_in, prefix, block_order, qkv_weight, out_weight, up_weight, down_weight, ln_gains, ln_shifts, cotangent):
    pos = positions(block_order)
    count = MICRO * SEQS
    flat_x = hidden_in.astype(jnp.float32).reshape(count, LEN, D)
    flat_pre = prefix.reshape(count).astype(jnp.int32)
    params = (qkv_weight.astype(jnp.float32), out_weight.astype(jnp.float32), up_weight.astype(jnp.float32), down_weight.astype(jnp.float32), ln_gains.astype(jnp.float32), ln_shifts.astype(jnp.float32))

    def forward(weights, inputs):

        def one_seq(item):
            input_rows, start = item
            allowed = (pos[None, :] <= pos[:, None]) | (pos[None, :] < start)
            return layer(input_rows, allowed, *weights)
        return lax.map(jax.checkpoint(one_seq), (inputs, flat_pre))
    result, pull = jax.vjp(forward, params, flat_x)
    grads, grad_x = pull(cotangent.astype(jnp.float32).reshape(count, LEN, D))
    shape = (MICRO, SEQS, LEN, D)
    return (result.reshape(shape).astype(jnp.bfloat16), grad_x.reshape(shape), grads[0], grads[1], grads[2], grads[3], grads[4], grads[5])
```

```python
import functools

import jax
import jax.numpy as jnp
from jax import lax
from jax.experimental import pallas as pl
from jax.experimental.pallas import tpu as pltpu
from jax.sharding import PartitionSpec as P

HEAD_DIM = 64
DEPTH = 12
EPS = 1e-05
GELU_C = 0.7978845608028654
GELU_A = 0.044715
NEG = -1e30
BRANCH = DEPTH ** (-0.5)
MESH = pl.DeviceIdType.MESH
F32 = jnp.float32
BF16 = jnp.bfloat16
VMEM_LIMIT = 60 * 1024 * 1024


def gelu_value(u):
    return 0.5 * u * (1.0 + jnp.tanh(GELU_C * (u + GELU_A * u * u * u)))


def gelu_slope(u):
    inner = jnp.tanh(GELU_C * (u + GELU_A * u * u * u))
    return 0.5 * (1.0 + inner) + 0.5 * u * (1.0 - inner * inner) * GELU_C * (
        1.0 + 3.0 * GELU_A * u * u
    )


def normalize(x):
    centered = x - jnp.mean(x, axis=1, keepdims=True)
    inv = lax.rsqrt(jnp.mean(centered * centered, axis=1, keepdims=True) + EPS)
    return centered * inv, inv


def dot_nn(a, b):
    return lax.dot_general(a, b, (((1,), (0,)), ((), ())), preferred_element_type=F32)


def dot_nt(a, b):
    return lax.dot_general(a, b, (((1,), (1,)), ((), ())), preferred_element_type=F32)


def dot_tn(a, b):
    return lax.dot_general(a, b, (((0,), (0,)), ((), ())), preferred_element_type=F32)


def remote(src, dst, send, recv, **ids):
    return pltpu.make_async_remote_copy(
        src_ref=src, dst_ref=dst, send_sem=send, recv_sem=recv, device_id=ids, device_id_type=MESH
    )


class Place:
    def __init__(self, n_ctx):
        self.n = n_ctx
        self.c = lax.axis_index("ctx")
        self.d = lax.axis_index("dp")
        tp = lax.axis_index("tp")
        self.core = lax.rem(tp, 2)
        self.mate = tp + 1 - 2 * self.core
        chip = lax.div(tp, 2)
        self.across = (1 - chip) * 2 + self.core

    def barrier(self, dp, tp, ctx):
        sem = pltpu.get_barrier_semaphore()

        def hello(**ids):
            pl.semaphore_signal(sem, inc=1, device_id=ids, device_id_type=MESH)

        count = 0
        if dp:
            hello(dp=1 - self.d)
            count += 1
        if tp:
            hello(tp=self.mate)
            hello(tp=self.across)
            count += 2
        if ctx:
            pl.when(self.c > 0)(lambda: hello(ctx=self.c - 1))
            pl.when(self.c < self.n - 1)(lambda: hello(ctx=self.c + 1))
        if ctx:
            count = count + jnp.minimum(self.c, 1) + jnp.minimum(self.n - 1 - self.c, 1)
        pl.semaphore_wait(sem, count)


class TpSum:
    def __init__(self, place, half, mine, out_half, in_half, out_sum, in_sum, total, send, recv):
        self.p, self.half = place, half
        self.mine, self.out_half, self.in_half = mine, out_half, in_half
        self.out_sum, self.in_sum, self.total = out_sum, in_sum, total
        self.send, self.recv = send, recv

    def rows(self, core):
        return pl.ds(pl.multiple_of(core * self.half, self.half), self.half)

    def c1(self):
        return remote(self.out_half, self.in_half, self.send.at[0], self.recv.at[0], tp=self.p.mate)

    def c2(self):
        return remote(self.out_sum, self.in_sum, self.send.at[1], self.recv.at[1], tp=self.p.across)

    def c3(self, core):
        part = self.total.at[self.rows(core)]
        return remote(part, part, self.send.at[2], self.recv.at[2], tp=self.p.mate)

    def start(self, partial):
        self.out_half[...] = partial(self.rows(1 - self.p.core)).astype(BF16)
        self.c1().start()
        self.mine[...] = partial(self.rows(self.p.core))

    def step2(self):
        self.c1().wait_recv()
        self.out_sum[...] = (self.mine[...] + self.in_half[...].astype(F32)).astype(BF16)
        self.c2().start()

    def step3(self):
        self.c2().wait_recv()
        both = self.out_sum[...].astype(F32) + self.in_sum[...].astype(F32)
        self.total[self.rows(self.p.core), :] = both.astype(BF16)
        self.c3(self.p.core).start()

    def finish(self):
        self.c3(1 - self.p.core).wait_recv()

    def drain(self):
        self.c1().wait_send()
        self.c2().wait_send()
        self.c3(self.p.core).wait_send()


def tp_scratch(sets, half, width):
    return [
        pltpu.VMEM((sets, half, width), F32),
        pltpu.VMEM((sets, half, width), BF16),
        pltpu.VMEM((sets, half, width), BF16),
        pltpu.VMEM((sets, half, width), BF16),
        pltpu.VMEM((sets, half, width), BF16),
        pltpu.SemaphoreType.DMA((sets, 3)),
        pltpu.SemaphoreType.DMA((sets, 3)),
    ]


def tp_set(place, half, scratch, index, total):
    mine, out_half, in_half, out_sum, in_sum, send, recv = scratch
    return TpSum(
        place, half, mine.at[index], out_half.at[index], in_half.at[index], out_sum.at[index],
        in_sum.at[index], total, send.at[index], recv.at[index],
    )


def query_limits(border, prefix, m, c, rows):
    half = rows // 2
    lane = lax.broadcasted_iota(jnp.int32, (1, rows), 1)
    pos = jnp.where(lane < half, border[2 * c] * half + lane, border[2 * c + 1] * half + lane - half)
    return jnp.maximum(pos, prefix[m, 0] - 1)


def key_positions(border, block, half):
    return border[block] * half + lax.broadcasted_iota(jnp.int32, (half, 1), 0)


def forward_kernel(
    n_ctx, exchange, prefix, border, hid, *refs
):
    if exchange:
        (wp_s, wo_s, wu_s, wd_s, ln_s) = refs[:5]
        refs = refs[5:]
        (attn, heads, lse, o_t, qs, kv, h1, wp, wo, wu, wd, ln) = refs[:12]
        refs = refs[12:]
    else:
        (wp, wo, wu, wd, ln) = refs[:5]
        refs = refs[5:]
        (attn, heads, lse, o_t, qs, kv, h1) = refs[:7]
        refs = refs[7:]
    (m_row, l_row, o_acc, heads_t, ks, kr, ws, wr) = refs[:8]
    tp_refs = refs[8:15]
    p = Place(n_ctx)
    c, n = p.c, n_ctx
    micro, rows, width = hid.shape
    half = rows // 2
    p.barrier(exchange, True, True)

    def pairs():
        size = wp_s.shape[0]
        span = pl.ds(pl.multiple_of(p.d * size, size), size)
        usize = wu_s.shape[0]
        uspan = pl.ds(pl.multiple_of(p.d * usize, usize), usize)
        return (
            (ln_s, ln.at[p.d]), (wp_s, wp.at[span]), (wo_s, wo.at[p.d]),
            (wu_s, wu.at[uspan]), (wd_s, wd.at[p.d]),
        )

    def weight_copy(i, src, dst):
        return remote(src, dst, ws.at[i], wr.at[i], dp=1 - p.d)

    if exchange:
        for i, (src, dst) in enumerate(pairs()):
            weight_copy(i, src, dst).start()
        for i, (src, dst) in enumerate(pairs()):
            dst[...] = src[...]
        weight_copy(0, *pairs()[0]).wait_recv()
    gain = jnp.concatenate([ln[i, 0:1, :] for i in range(ln.shape[0])], axis=1)
    shift = jnp.concatenate([ln[i, 2:3, :] for i in range(ln.shape[0])], axis=1)

    for m in range(micro):
        @pl.loop(0, rows // 128)
        def _(i):
            span = pl.ds(pl.multiple_of(i * 128, 128), 128)
            xhat, _ = normalize(hid[m, span, :].astype(F32))
            h1[m, span, :] = (xhat * gain + shift).astype(BF16)

    def kv_copy(m, way, s):
        j, to = (c - s, c + 1) if way == 0 else (c + s, c - 1)
        block = kv.at[m, j]
        return remote(block, block, ks.at[m, way, s], kr.at[m, way, s + 1], ctx=to)

    def kv_arrival(m, way, s):
        j = c - s if way == 0 else c + s
        to = c - 1 if way == 0 else c + 1
        block = kv.at[m, j]
        return remote(block, block, ks.at[m, way, s], kr.at[m, way, s], ctx=to)

    def has(way, s):
        return c - s >= 0 if way == 0 else c + s < n

    def sends(way, s):
        if way == 0:
            return jnp.logical_and(c - s >= 0, c + 1 < n)
        return jnp.logical_and(c + s < n, c - 1 >= 0)

    if exchange:
        weight_copy(1, *pairs()[1]).wait_recv()
    for m in range(micro):
        @pl.loop(0, rows // 128)
        def _(i):
            span = pl.ds(pl.multiple_of(i * 128, 128), 128)
            packed = dot_nn(h1[m, span, :], wp[...])
            qs[m, span, :] = (packed[:, 0:256].astype(BF16).astype(F32) * HEAD_DIM ** (-0.5)).astype(BF16)
            kv[m, c, span, :] = packed[:, 256:640].astype(BF16)

        if m == 0:
            for way in range(2):
                pl.when(sends(way, 0))(lambda way=way: kv_copy(0, way, 0).start())
    pl.when(c == 0)(lambda: kv_copy(1, 0, 0).start())
    pl.when(c == n - 1)(lambda: kv_copy(1, 1, 0).start())

    def attend(m, j, limits):
        lanes = lax.broadcasted_iota(jnp.int32, (rows, 128), 1)
        q01 = qs[m, :, 0:128]
        zero = jnp.zeros_like(q01)
        q_heads = (
            jnp.where(lanes < 64, q01, zero), jnp.where(lanes < 64, zero, q01), qs[m, :, 128:256]
        )
        for b in range(2):
            span = pl.ds(b * half, half)
            k01 = kv[m, j, span, 0:128]
            k2v0 = kv[m, j, span, 128:256]
            v12 = kv[m, j, span, 256:384]
            t0 = k2v0.T
            t12 = v12.T
            allowed = key_positions(border, 2 * j + b, half) <= limits
            for h in range(3):
                scores = dot_nt(k2v0 if h == 2 else k01, q_heads[h])
                scores = jnp.where(allowed, scores, NEG)
                old = m_row[h]
                top = jnp.maximum(old, jnp.max(scores, axis=0, keepdims=True))
                prob = jnp.exp(scores - top)
                fade = jnp.exp(old - top)
                m_row[h] = top
                l_row[h] = l_row[h] * fade + jnp.sum(prob, axis=0, keepdims=True)
                v_t = t0[64:128] if h == 0 else t12[(h - 1) * 64 : h * 64]
                o_acc[h] = o_acc[h] * fade + dot_nn(v_t, prob.astype(BF16))

    tops = [tp_set(p, half, tp_refs, m, attn.at[m]) for m in range(micro)]
    for m in range(micro):
        limits = query_limits(border, prefix, m, c, rows)
        m_row[...] = jnp.full(m_row.shape, NEG, F32)
        l_row[...] = jnp.zeros(l_row.shape, F32)
        o_acc[...] = jnp.zeros(o_acc.shape, F32)

        @pl.loop(0, 2 * n - 1)
        def _(t, m=m, limits=limits):
            s = lax.div(t + 1, 2)
            right = lax.rem(t, 2) == 1
            left = jnp.logical_and(lax.rem(t, 2) == 0, t > 0)

            def arrive(way):
                kv_arrival(m, way, s).wait_recv()
                pl.when(sends(way, s))(lambda: kv_copy(m, way, s).start())
                if m == 0:
                    last = c if way == 0 else n - 1 - c
                    pl.when(jnp.logical_and(s == last, sends(way, 0)))(
                        lambda: kv_copy(1, way, 0).start()
                    )

            pl.when(jnp.logical_and(right, has(0, s)))(lambda: arrive(0))
            pl.when(jnp.logical_and(left, has(1, s)))(lambda: arrive(1))
            j = jnp.where(right, c - s, c + s)

            @pl.when(jnp.logical_and(j >= 0, j < n))
            def _():
                attend(m, j, limits)

            if m == 1:
                pl.when(t == 0)(tops[0].step2)
                pl.when(t == 3)(tops[0].step3)

        for h in range(3):
            norm = o_acc[h] / l_row[h]
            o_t[m, h] = norm
            lse[m, h : h + 1, :] = m_row[h] + jnp.log(l_row[h])
            at = 192 if h == 0 else (h - 1) * 64
            heads_t[at : at + 64, :] = norm
        heads_t[128:192, :] = jnp.zeros((64, rows), F32)
        heads[m] = heads_t[...].T.astype(BF16)
        if exchange and m == 0:
            weight_copy(2, *pairs()[2]).wait_recv()

        def project(span, m=m):
            left = heads[m, span, :]
            return jnp.concatenate([dot_nn(left, wo[i]) for i in range(wo.shape[0])], axis=1)

        tops[m].start(project)
    tops[0].finish()
    tops[1].step2()
    tops[1].step3()
    tops[1].finish()
    if exchange:
        for i in range(3, 5):
            weight_copy(i, *pairs()[i]).wait_recv()
        for i in range(5):
            weight_copy(i, *pairs()[i]).wait_send()
    for m in range(micro):
        for way in range(2):
            for s in range(n - 1):
                pl.when(sends(way, s))(lambda m=m, way=way, s=s: kv_copy(m, way, s).wait_send())
        tops[m].drain()


def vmem_specs(k):
    return [pl.BlockSpec(memory_space=pltpu.VMEM)] * k


def run_forward(n_ctx, exchange, prefix, border, hid, weights):
    micro, rows, width = hid.shape
    half = rows // 2
    sds = jax.ShapeDtypeStruct
    outs = [
        sds((micro, rows, width), BF16),
        sds((micro, rows, 256), BF16),
        sds((micro, 8, rows), F32),
        sds((micro, 3, 64, rows), F32),
        sds((micro, rows, 256), BF16),
        sds((micro, n_ctx, rows, 384), BF16),
        sds((micro, rows, width), BF16),
    ]
    if exchange:
        wp, wo, wu, wd, ln = weights
        outs += [
            sds((2 * wp.shape[0], wp.shape[1]), BF16),
            sds((2,) + wo.shape, BF16),
            sds((2 * wu.shape[0], wu.shape[1]), BF16),
            sds((2,) + wd.shape, BF16),
            sds((2,) + ln.shape, F32),
        ]
    scratch = [
        pltpu.VMEM((3, 1, rows), F32),
        pltpu.VMEM((3, 1, rows), F32),
        pltpu.VMEM((3, 64, rows), F32),
        pltpu.VMEM((256, rows), F32),
        pltpu.SemaphoreType.DMA((micro, 2, n_ctx + 1)),
        pltpu.SemaphoreType.DMA((micro, 2, n_ctx + 1)),
        pltpu.SemaphoreType.DMA((5,)),
        pltpu.SemaphoreType.DMA((5,)),
    ] + tp_scratch(micro, half, width)
    smem = pl.BlockSpec(memory_space=pltpu.SMEM)
    out = pl.pallas_call(
        functools.partial(forward_kernel, n_ctx, exchange),
        out_shape=outs,
        in_specs=[smem, smem] + vmem_specs(1 + len(weights)),
        out_specs=vmem_specs(len(outs)),
        scratch_shapes=scratch,
        compiler_params=pltpu.CompilerParams(
            collective_id=0, has_side_effects=True, vmem_limit_bytes=VMEM_LIMIT
        ),
        name="attention_forward",
    )(prefix, border, hid, *weights)
    return out if exchange else list(out) + list(weights)


def apply_layer_norm(values, norm_gain, norm_shift):
    normalized, inv = normalize(values)
    return (normalized * norm_gain + norm_shift, normalized, inv)


def norm_backward(normed_gradient, normalized_input, inverse_deviation, norm_gain):
    scaled_gradient = normed_gradient * norm_gain
    return inverse_deviation * (
        scaled_gradient
        - jnp.mean(scaled_gradient, axis=1, keepdims=True)
        - normalized_input * jnp.mean(scaled_gradient * normalized_input, axis=1, keepdims=True)
    )


def pack_weights(qkv_weight, out_weight, up_weight, down_weight, ln_gains, ln_shifts, exchange):
    q, k, v = qkv_weight[0], qkv_weight[1], qkv_weight[2]
    pad = jnp.zeros((q.shape[0], 64), BF16)
    wp = jnp.concatenate([q, pad, k, v], axis=1)
    wo = jnp.concatenate(
        [out_weight[64:], jnp.zeros((64, out_weight.shape[1]), BF16), out_weight[:64]], axis=0
    )
    ln = jnp.concatenate([ln_gains, ln_shifts], axis=0).astype(F32)
    ln = jnp.pad(ln, ((0, 4), (0, 0)))
    if exchange:
        return [wp, wo, up_weight, down_weight, ln]
    gather = functools.partial(lax.all_gather, axis_name="dp", tiled=True)
    return [
        gather(wp, axis=0), gather(wo, axis=1)[None], gather(up_weight, axis=0),
        gather(down_weight, axis=1)[None], gather(ln, axis=1)[None],
    ]


def side_by_side(stack):
    return jnp.concatenate([stack[i] for i in range(stack.shape[0])], axis=-1)


def body(
    hidden_in, prefix, block_order, qkv_weight, out_weight, up_weight, down_weight, ln_gains,
    ln_shifts, cotangent,
):
    micro, _, tokens, width = hidden_in.shape
    local_width = qkv_weight.shape[2]
    heads_n = local_width // HEAD_DIM
    n_ctx = lax.axis_size("ctx")
    n_dp = lax.axis_size("dp")
    exchange = n_dp == 2
    seq_len = tokens * n_ctx
    half = tokens // 2
    scale = HEAD_DIM ** (-0.5)
    weights = pack_weights(
        qkv_weight, out_weight, up_weight, down_weight, ln_gains, ln_shifts, exchange
    )
    (attn, heads, lse, o_t, qs, kv, h1, wp, wo, wu, wd, ln) = run_forward(
        n_ctx, exchange, prefix, block_order, hidden_in[:, 0], weights
    )
    out_full = side_by_side(wo)
    down_full = side_by_side(wd)
    ln_full = side_by_side(ln)
    gains, shifts = ln_full[0:2], ln_full[2:4]

    cuts = jnp.arange(seq_len, dtype=jnp.int32)
    key_pos = jnp.repeat(block_order, half, total_repeat_length=seq_len) * half + cuts % half
    query_pos = lax.dynamic_slice_in_dim(key_pos, lax.axis_index("ctx") * tokens, tokens)
    acc = None
    results, grads_in = [], []
    for m in range(micro):
        x = hidden_in[m, 0].astype(F32)
        allowed = (key_pos[None, :] <= query_pos[:, None]) | (key_pos[None, :] < prefix[m, 0])
        xhat1, inv1 = normalize(x)
        mid = x + BRANCH * attn[m].astype(F32)
        n2, xhat2, inv2 = apply_layer_norm(mid, gains[1], shifts[1])
        h2 = n2.astype(BF16)
        up = dot_nn(h2, wu)
        act = gelu_value(up).astype(BF16)
        mlp = lax.psum(dot_nn(act, down_full), "tp")
        results.append((mid + BRANCH * mlp).astype(BF16))
        g = cotangent[m, 0].astype(F32)
        d_mlp = (BRANCH * g).astype(BF16)
        grad_down = dot_tn(act, d_mlp)
        d_up = (dot_nt(d_mlp, down_full) * gelu_slope(up)).astype(BF16)
        grad_up = dot_tn(h2, d_up)
        d_n2 = lax.psum(dot_nt(d_up, wu), "tp")
        d_mid = g + norm_backward(d_n2, xhat2, inv2, gains[1])
        d_attn = (BRANCH * d_mid).astype(BF16)
        grad_out = dot_tn(heads[m], d_attn)
        d_heads = dot_nt(d_attn, out_full).astype(BF16)
        q = qs[m][:, :local_width].reshape(tokens, heads_n, HEAD_DIM)
        flat = kv[m].reshape(seq_len, 2 * local_width)
        keys = flat[:, :local_width].reshape(seq_len, heads_n, HEAD_DIM)
        values = flat[:, local_width:].reshape(seq_len, heads_n, HEAD_DIM)
        dh = jnp.concatenate([d_heads[:, 192:], d_heads[:, :128]], axis=1)
        dh = dh.reshape(tokens, heads_n, HEAD_DIM)
        scores = jnp.einsum("qhd,khd->hqk", q, keys, preferred_element_type=F32)
        scores = jnp.where(allowed[None], scores, NEG)
        prob = jnp.exp(scores - lse[m, :heads_n][:, :, None])
        d_prob = jnp.einsum("qhd,khd->hqk", dh, values, preferred_element_type=F32)
        d_scores = (prob * (d_prob - jnp.sum(prob * d_prob, axis=2, keepdims=True))).astype(BF16)
        d_q = jnp.einsum("hqk,khd->qhd", d_scores, keys, preferred_element_type=F32) * scale
        d_k = jnp.einsum("hqk,qhd->khd", d_scores, q, preferred_element_type=F32)
        d_v = jnp.einsum("hqk,qhd->khd", prob.astype(BF16), dh, preferred_element_type=F32)
        d_kv = jnp.concatenate(
            [d_k.reshape(seq_len, local_width), d_v.reshape(seq_len, local_width)], axis=1
        )
        d_kv = lax.psum_scatter(d_kv, "ctx", scatter_dimension=0, tiled=True)
        d_pack = jnp.concatenate(
            [d_q.reshape(tokens, local_width), jnp.zeros((tokens, 64), F32), d_kv], axis=1
        ).astype(BF16)
        grad_pack = dot_tn(h1[m], d_pack)
        d_n1 = lax.psum(dot_nt(d_pack, wp), "tp")
        grads_in.append(d_mid + norm_backward(d_n1, xhat1, inv1, gains[0]))
        new = (
            grad_pack, grad_out, grad_up, grad_down,
            jnp.stack([jnp.sum(d_n1 * xhat1, axis=0), jnp.sum(d_n2 * xhat2, axis=0)]),
            jnp.stack([jnp.sum(d_n1, axis=0), jnp.sum(d_n2, axis=0)]),
        )
        acc = new if acc is None else jax.tree.map(jnp.add, acc, new)
    pack, g_out, g_up, g_down, g_gains, g_shifts = acc
    g_qkv = jnp.stack([pack[:, 0:192], pack[:, 256:448], pack[:, 448:640]])
    g_out = jnp.concatenate([g_out[192:], g_out[:128]], axis=0)
    whole = lax.psum((g_qkv, g_out, g_up, g_down, g_gains, g_shifts), "ctx")
    dims = (1, 1, 0, 1, 1, 1)
    owned = [
        lax.psum_scatter(v, "dp", scatter_dimension=d, tiled=True) for v, d in zip(whole, dims)
    ]
    return (jnp.stack(results)[:, None], jnp.stack(grads_in)[:, None], *owned)


def solution(mesh):
    in_specs = (
        P(None, "dp", "ctx", None), P(None, "dp"), P(), P(None, "dp", "tp"), P("tp", "dp"),
        P("dp", "tp"), P("tp", "dp"), P(None, "dp"), P(None, "dp"), P(None, "dp", "ctx", None),
    )
    out_specs = (
        P(None, "dp", "ctx", None), P(None, "dp", "ctx", None), P(None, "dp", "tp"),
        P("tp", "dp"), P("dp", "tp"), P("tp", "dp"), P(None, "dp"), P(None, "dp"),
    )
    return jax.shard_map(body, mesh=mesh, in_specs=in_specs, out_specs=out_specs, check_vma=False)
```

```python
import functools

import jax
import jax.numpy as jnp
from jax import lax
from jax.experimental import pallas as pl
from jax.experimental.pallas import tpu as pltpu
from jax.sharding import PartitionSpec as P

HEAD_DIM = 64
DEPTH = 12
EPS = 1e-05
GELU_C = 0.7978845608028654
GELU_A = 0.044715
NEG = -1e30
BRANCH = DEPTH ** (-0.5)
MESH = pl.DeviceIdType.MESH
F32 = jnp.float32
BF16 = jnp.bfloat16
VMEM_LIMIT = 60 * 1024 * 1024


def gelu_value(u):
    return 0.5 * u * (1.0 + jnp.tanh(GELU_C * (u + GELU_A * u * u * u)))


def gelu_slope(u):
    inner = jnp.tanh(GELU_C * (u + GELU_A * u * u * u))
    return 0.5 * (1.0 + inner) + 0.5 * u * (1.0 - inner * inner) * GELU_C * (
        1.0 + 3.0 * GELU_A * u * u
    )


def normalize(x):
    centered = x - jnp.mean(x, axis=1, keepdims=True)
    inv = lax.rsqrt(jnp.mean(centered * centered, axis=1, keepdims=True) + EPS)
    return centered * inv, inv


def dot_nn(a, b):
    return lax.dot_general(a, b, (((1,), (0,)), ((), ())), preferred_element_type=F32)


def dot_nt(a, b):
    return lax.dot_general(a, b, (((1,), (1,)), ((), ())), preferred_element_type=F32)


def dot_tn(a, b):
    return lax.dot_general(a, b, (((0,), (0,)), ((), ())), preferred_element_type=F32)


def remote(src, dst, send, recv, **ids):
    return pltpu.make_async_remote_copy(
        src_ref=src, dst_ref=dst, send_sem=send, recv_sem=recv, device_id=ids, device_id_type=MESH
    )


class Place:
    def __init__(self, n_ctx):
        self.n = n_ctx
        self.c = lax.axis_index("ctx")
        self.d = lax.axis_index("dp")
        tp = lax.axis_index("tp")
        self.core = lax.rem(tp, 2)
        self.mate = tp + 1 - 2 * self.core
        chip = lax.div(tp, 2)
        self.across = (1 - chip) * 2 + self.core

    def barrier(self, dp, tp, ctx):
        sem = pltpu.get_barrier_semaphore()

        def hello(**ids):
            pl.semaphore_signal(sem, inc=1, device_id=ids, device_id_type=MESH)

        count = 0
        if dp:
            hello(dp=1 - self.d)
            count += 1
        if tp:
            hello(tp=self.mate)
            hello(tp=self.across)
            count += 2
        if ctx:
            pl.when(self.c > 0)(lambda: hello(ctx=self.c - 1))
            pl.when(self.c < self.n - 1)(lambda: hello(ctx=self.c + 1))
        if ctx:
            count = count + jnp.minimum(self.c, 1) + jnp.minimum(self.n - 1 - self.c, 1)
        pl.semaphore_wait(sem, count)


class TpSum:
    def __init__(self, place, half, mine, out_half, in_half, out_sum, in_sum, total, send, recv):
        self.p, self.half = place, half
        self.mine, self.out_half, self.in_half = mine, out_half, in_half
        self.out_sum, self.in_sum, self.total = out_sum, in_sum, total
        self.send, self.recv = send, recv

    def rows(self, core):
        return pl.ds(pl.multiple_of(core * self.half, self.half), self.half)

    def c1(self):
        return remote(self.out_half, self.in_half, self.send.at[0], self.recv.at[0], tp=self.p.mate)

    def c2(self):
        return remote(self.out_sum, self.in_sum, self.send.at[1], self.recv.at[1], tp=self.p.across)

    def c3(self, core):
        part = self.total.at[self.rows(core)]
        return remote(part, part, self.send.at[2], self.recv.at[2], tp=self.p.mate)

    def start(self, partial):
        self.out_half[...] = partial(self.rows(1 - self.p.core)).astype(BF16)
        self.c1().start()
        self.mine[...] = partial(self.rows(self.p.core))

    def step2(self):
        self.c1().wait_recv()
        self.out_sum[...] = (self.mine[...] + self.in_half[...].astype(F32)).astype(BF16)
        self.c2().start()

    def step3(self):
        self.c2().wait_recv()
        both = self.out_sum[...].astype(F32) + self.in_sum[...].astype(F32)
        self.total[self.rows(self.p.core), :] = both.astype(BF16)
        self.c3(self.p.core).start()

    def finish(self):
        self.c3(1 - self.p.core).wait_recv()

    def drain(self):
        self.c1().wait_send()
        self.c2().wait_send()
        self.c3(self.p.core).wait_send()


def tp_scratch(sets, half, width):
    return [
        pltpu.VMEM((sets, half, width), F32),
        pltpu.VMEM((sets, half, width), BF16),
        pltpu.VMEM((sets, half, width), BF16),
        pltpu.VMEM((sets, half, width), BF16),
        pltpu.VMEM((sets, half, width), BF16),
        pltpu.SemaphoreType.DMA((sets, 3)),
        pltpu.SemaphoreType.DMA((sets, 3)),
    ]


def tp_set(place, half, scratch, index, total):
    mine, out_half, in_half, out_sum, in_sum, send, recv = scratch
    return TpSum(
        place, half, mine.at[index], out_half.at[index], in_half.at[index], out_sum.at[index],
        in_sum.at[index], total, send.at[index], recv.at[index],
    )


def query_limits(border, prefix, m, c, rows):
    half = rows // 2
    lane = lax.broadcasted_iota(jnp.int32, (1, rows), 1)
    pos = jnp.where(lane < half, border[2 * c] * half + lane, border[2 * c + 1] * half + lane - half)
    return jnp.maximum(pos, prefix[m, 0] - 1)


def key_positions(border, block, half):
    return border[block] * half + lax.broadcasted_iota(jnp.int32, (half, 1), 0)


def forward_kernel(
    n_ctx, exchange, prefix, border, hid, *refs
):
    if exchange:
        (wp_s, wo_s, wu_s, wd_s, ln_s) = refs[:5]
        refs = refs[5:]
        (attn, heads, lse, o_t, qs, kv, h1, wp, wo, wu, wd, ln) = refs[:12]
        refs = refs[12:]
    else:
        (wp, wo, wu, wd, ln) = refs[:5]
        refs = refs[5:]
        (attn, heads, lse, o_t, qs, kv, h1) = refs[:7]
        refs = refs[7:]
    (m_row, l_row, o_acc, heads_t, ks, kr, ws, wr) = refs[:8]
    tp_refs = refs[8:15]
    p = Place(n_ctx)
    c, n = p.c, n_ctx
    micro, rows, width = hid.shape
    half = rows // 2
    p.barrier(exchange, True, True)

    def pairs():
        size = wp_s.shape[0]
        span = pl.ds(pl.multiple_of(p.d * size, size), size)
        usize = wu_s.shape[0]
        uspan = pl.ds(pl.multiple_of(p.d * usize, usize), usize)
        return (
            (ln_s, ln.at[p.d]), (wp_s, wp.at[span]), (wo_s, wo.at[p.d]),
            (wu_s, wu.at[uspan]), (wd_s, wd.at[p.d]),
        )

    def weight_copy(i, src, dst):
        return remote(src, dst, ws.at[i], wr.at[i], dp=1 - p.d)

    if exchange:
        for i, (src, dst) in enumerate(pairs()):
            weight_copy(i, src, dst).start()
        for i, (src, dst) in enumerate(pairs()):
            dst[...] = src[...]
        weight_copy(0, *pairs()[0]).wait_recv()
    gain = jnp.concatenate([ln[i, 0:1, :] for i in range(ln.shape[0])], axis=1)
    shift = jnp.concatenate([ln[i, 2:3, :] for i in range(ln.shape[0])], axis=1)

    for m in range(micro):
        @pl.loop(0, rows // 128)
        def _(i):
            span = pl.ds(pl.multiple_of(i * 128, 128), 128)
            xhat, _ = normalize(hid[m, span, :].astype(F32))
            h1[m, span, :] = (xhat * gain + shift).astype(BF16)

    def kv_copy(m, way, s):
        j, to = (c - s, c + 1) if way == 0 else (c + s, c - 1)
        block = kv.at[m, j]
        return remote(block, block, ks.at[m, way, s], kr.at[m, way, s + 1], ctx=to)

    def kv_arrival(m, way, s):
        j = c - s if way == 0 else c + s
        to = c - 1 if way == 0 else c + 1
        block = kv.at[m, j]
        return remote(block, block, ks.at[m, way, s], kr.at[m, way, s], ctx=to)

    def has(way, s):
        return c - s >= 0 if way == 0 else c + s < n

    def sends(way, s):
        if way == 0:
            return jnp.logical_and(c - s >= 0, c + 1 < n)
        return jnp.logical_and(c + s < n, c - 1 >= 0)

    if exchange:
        weight_copy(1, *pairs()[1]).wait_recv()
    for m in range(micro):
        @pl.loop(0, rows // 128)
        def _(i):
            span = pl.ds(pl.multiple_of(i * 128, 128), 128)
            packed = dot_nn(h1[m, span, :], wp[...])
            qs[m, span, :] = (packed[:, 0:256].astype(BF16).astype(F32) * HEAD_DIM ** (-0.5)).astype(BF16)
            kv[m, c, span, :] = packed[:, 256:640].astype(BF16)

        if m == 0:
            for way in range(2):
                pl.when(sends(way, 0))(lambda way=way: kv_copy(0, way, 0).start())
    pl.when(c == 0)(lambda: kv_copy(1, 0, 0).start())
    pl.when(c == n - 1)(lambda: kv_copy(1, 1, 0).start())

    def attend(m, j, limits):
        lanes = lax.broadcasted_iota(jnp.int32, (rows, 128), 1)
        q01 = qs[m, :, 0:128]
        zero = jnp.zeros_like(q01)
        q_heads = (
            jnp.where(lanes < 64, q01, zero), jnp.where(lanes < 64, zero, q01), qs[m, :, 128:256]
        )
        for b in range(2):
            span = pl.ds(b * half, half)
            k01 = kv[m, j, span, 0:128]
            k2v0 = kv[m, j, span, 128:256]
            v12 = kv[m, j, span, 256:384]
            t0 = k2v0.T
            t12 = v12.T
            allowed = key_positions(border, 2 * j + b, half) <= limits
            for h in range(3):
                scores = dot_nt(k2v0 if h == 2 else k01, q_heads[h])
                scores = jnp.where(allowed, scores, NEG)
                old = m_row[h]
                top = jnp.maximum(old, jnp.max(scores, axis=0, keepdims=True))
                prob = jnp.exp(scores - top)
                fade = jnp.exp(old - top)
                m_row[h] = top
                l_row[h] = l_row[h] * fade + jnp.sum(prob, axis=0, keepdims=True)
                v_t = t0[64:128] if h == 0 else t12[(h - 1) * 64 : h * 64]
                o_acc[h] = o_acc[h] * fade + dot_nn(v_t, prob.astype(BF16))

    tops = [tp_set(p, half, tp_refs, m, attn.at[m]) for m in range(micro)]
    for m in range(micro):
        limits = query_limits(border, prefix, m, c, rows)
        m_row[...] = jnp.full(m_row.shape, NEG, F32)
        l_row[...] = jnp.zeros(l_row.shape, F32)
        o_acc[...] = jnp.zeros(o_acc.shape, F32)

        @pl.loop(0, 2 * n - 1)
        def _(t, m=m, limits=limits):
            s = lax.div(t + 1, 2)
            right = lax.rem(t, 2) == 1
            left = jnp.logical_and(lax.rem(t, 2) == 0, t > 0)

            def arrive(way):
                kv_arrival(m, way, s).wait_recv()
                pl.when(sends(way, s))(lambda: kv_copy(m, way, s).start())
                if m == 0:
                    last = c if way == 0 else n - 1 - c
                    pl.when(jnp.logical_and(s == last, sends(way, 0)))(
                        lambda: kv_copy(1, way, 0).start()
                    )

            pl.when(jnp.logical_and(right, has(0, s)))(lambda: arrive(0))
            pl.when(jnp.logical_and(left, has(1, s)))(lambda: arrive(1))
            j = jnp.where(right, c - s, c + s)

            @pl.when(jnp.logical_and(j >= 0, j < n))
            def _():
                attend(m, j, limits)

            if m == 1:
                pl.when(t == 0)(tops[0].step2)
                pl.when(t == 3)(tops[0].step3)

        for h in range(3):
            norm = o_acc[h] / l_row[h]
            o_t[m, h] = norm
            lse[m, h : h + 1, :] = m_row[h] + jnp.log(l_row[h])
            at = 192 if h == 0 else (h - 1) * 64
            heads_t[at : at + 64, :] = norm
        heads_t[128:192, :] = jnp.zeros((64, rows), F32)
        heads[m] = heads_t[...].T.astype(BF16)
        if exchange and m == 0:
            weight_copy(2, *pairs()[2]).wait_recv()

        def project(span, m=m):
            left = heads[m, span, :]
            return jnp.concatenate([dot_nn(left, wo[i]) for i in range(wo.shape[0])], axis=1)

        tops[m].start(project)
    tops[0].finish()
    tops[1].step2()
    tops[1].step3()
    tops[1].finish()
    if exchange:
        for i in range(3, 5):
            weight_copy(i, *pairs()[i]).wait_recv()
        for i in range(5):
            weight_copy(i, *pairs()[i]).wait_send()
    for m in range(micro):
        for way in range(2):
            for s in range(n - 1):
                pl.when(sends(way, s))(lambda m=m, way=way, s=s: kv_copy(m, way, s).wait_send())
        tops[m].drain()


def vmem_specs(k):
    return [pl.BlockSpec(memory_space=pltpu.VMEM)] * k


def run_forward(n_ctx, exchange, prefix, border, hid, weights):
    micro, rows, width = hid.shape
    half = rows // 2
    sds = jax.ShapeDtypeStruct
    outs = [
        sds((micro, rows, width), BF16),
        sds((micro, rows, 256), BF16),
        sds((micro, 8, rows), F32),
        sds((micro, 3, 64, rows), F32),
        sds((micro, rows, 256), BF16),
        sds((micro, n_ctx, rows, 384), BF16),
        sds((micro, rows, width), BF16),
    ]
    if exchange:
        wp, wo, wu, wd, ln = weights
        outs += [
            sds((2 * wp.shape[0], wp.shape[1]), BF16),
            sds((2,) + wo.shape, BF16),
            sds((2 * wu.shape[0], wu.shape[1]), BF16),
            sds((2,) + wd.shape, BF16),
            sds((2,) + ln.shape, F32),
        ]
    scratch = [
        pltpu.VMEM((3, 1, rows), F32),
        pltpu.VMEM((3, 1, rows), F32),
        pltpu.VMEM((3, 64, rows), F32),
        pltpu.VMEM((256, rows), F32),
        pltpu.SemaphoreType.DMA((micro, 2, n_ctx + 1)),
        pltpu.SemaphoreType.DMA((micro, 2, n_ctx + 1)),
        pltpu.SemaphoreType.DMA((5,)),
        pltpu.SemaphoreType.DMA((5,)),
    ] + tp_scratch(micro, half, width)
    smem = pl.BlockSpec(memory_space=pltpu.SMEM)
    out = pl.pallas_call(
        functools.partial(forward_kernel, n_ctx, exchange),
        out_shape=outs,
        in_specs=[smem, smem] + vmem_specs(1 + len(weights)),
        out_specs=vmem_specs(len(outs)),
        scratch_shapes=scratch,
        compiler_params=pltpu.CompilerParams(
            collective_id=0, has_side_effects=True, vmem_limit_bytes=VMEM_LIMIT
        ),
        name="attention_forward",
    )(prefix, border, hid, *weights)
    return out if exchange else list(out) + list(weights)


def pack_weights(qkv_weight, out_weight, up_weight, down_weight, ln_gains, ln_shifts, exchange):
    q, k, v = qkv_weight[0], qkv_weight[1], qkv_weight[2]
    pad = jnp.zeros((q.shape[0], 64), BF16)
    wp = jnp.concatenate([q, pad, k, v], axis=1)
    wo = jnp.concatenate(
        [out_weight[64:], jnp.zeros((64, out_weight.shape[1]), BF16), out_weight[:64]], axis=0
    )
    ln = jnp.concatenate([ln_gains, ln_shifts], axis=0).astype(F32)
    ln = jnp.pad(ln, ((0, 4), (0, 0)))
    if exchange:
        return [wp, wo, up_weight, down_weight, ln]
    gather = functools.partial(lax.all_gather, axis_name="dp", tiled=True)
    return [
        gather(wp, axis=0), gather(wo, axis=1)[None], gather(up_weight, axis=0),
        gather(down_weight, axis=1)[None], gather(ln, axis=1)[None],
    ]


def wide(ref_stack, fn):
    return jnp.concatenate([fn(ref_stack[i]) for i in range(ref_stack.shape[0])], axis=1)


def narrow(ref_stack, value):
    size = ref_stack.shape[2]
    total = dot_nt(value[:, 0:size], ref_stack[0])
    for i in range(1, ref_stack.shape[0]):
        total += dot_nt(value[:, i * size : (i + 1) * size], ref_stack[i])
    return total


def norm_back(dn, xhat, inv, gain):
    e = dn * gain
    return inv * (
        e - jnp.mean(e, axis=1, keepdims=True) - xhat * jnp.mean(e * xhat, axis=1, keepdims=True)
    )


def ln_row(ln, row):
    return jnp.concatenate([ln[i, row : row + 1, :] for i in range(ln.shape[0])], axis=1)


def column_sums(value):
    return jnp.sum(value, axis=0, keepdims=True)


def mlp_kernel(
    n_ctx, n_dp, hid, attn, cot, heads, wu, wd, ln, d_mid, d_attn, mlp, grads, stats,
    act, d_mlp, d_up, h2, total, *tp_refs
):
    p = Place(n_ctx)
    micro, rows, width = hid.shape
    half = rows // 2
    p.barrier(False, True, False)
    gain, shift = ln_row(ln, 1), ln_row(ln, 3)
    sums = [tp_set(p, half, tp_refs, m, total.at[m]) for m in range(micro)]
    ff = wu.shape[1]
    part = width // n_dp

    def middle(m, span):
        return hid[m, span, :].astype(F32) + BRANCH * attn[m, span, :].astype(F32)

    for m in range(micro):
        @pl.loop(0, rows // 128)
        def _(i, m=m):
            span = pl.ds(pl.multiple_of(i * 128, 128), 128)
            flat = pl.ds(pl.multiple_of(m * rows + i * 128, 128), 128)
            xhat, _ = normalize(middle(m, span))
            normed = (xhat * gain + shift).astype(BF16)
            h2[flat, :] = normed
            up = dot_nn(normed, wu[...])
            active = gelu_value(up).astype(BF16)
            act[flat, :] = active
            down_grad = (BRANCH * cot[m, span, :].astype(F32)).astype(BF16)
            d_mlp[flat, :] = down_grad
            d_up[flat, :] = (narrow(wd, down_grad) * gelu_slope(up)).astype(BF16)
            mlp[m, span, :] = wide(wd, lambda w: dot_nn(active, w)).astype(BF16)
            if m == 1:
                pl.when(i == 1)(sums[0].step2)

        sums[m].start(
            lambda span, m=m: dot_nt(d_up[pl.ds(m * rows + span.start, half), :], wu[...])
        )
    parts = grads.shape[0]
    cols = grads.shape[2]

    @pl.loop(0, ff // 256)
    def _(i):
        left = act[:, pl.ds(pl.multiple_of(i * 256, 256), 256)]
        to = pl.ds(pl.multiple_of(i * 256, 256), 256)
        for k in range(parts):
            grads[k, to, :] = dot_tn(left, d_mlp[:, k * cols : (k + 1) * cols]).astype(BF16)

    sums[1].step2()
    own_rows = width // parts
    for k in range(parts):
        @pl.loop(0, own_rows // 128)
        def _(i, k=k):
            left = h2[:, pl.ds(pl.multiple_of(k * own_rows + i * 128, 128), 128)]
            block = dot_tn(left, d_up[...]).astype(BF16)
            for q in range(ff // cols):
                to = pl.ds(pl.multiple_of(ff + q * own_rows + i * 128, 128), 128)
                grads[k, to, :] = block[:, q * cols : (q + 1) * cols]

    stats[...] = jnp.zeros(stats.shape, F32)
    for m in range(micro):
        if m == 0:
            sums[0].step3()
            sums[0].finish()
            sums[1].step3()
        else:
            sums[1].finish()

        @pl.loop(0, rows // 128)
        def _(i, m=m):
            span = pl.ds(pl.multiple_of(i * 128, 128), 128)
            flat = pl.ds(pl.multiple_of(m * rows + i * 128, 128), 128)
            xhat, inv = normalize(middle(m, span))
            dn = total[m, span, :].astype(F32)
            grad = cot[m, span, :].astype(F32) + norm_back(dn, xhat, inv, gain)
            d_mid[m, span, :] = grad
            d_attn[flat, :] = (BRANCH * grad).astype(BF16)
            stats[0:1, :] += column_sums(dn * xhat)
            stats[1:2, :] += column_sums(dn)

    at = ff + own_rows * (ff // cols)
    for k in range(parts):
        grads[k, at : at + 256, :] = dot_tn(
            heads[...], d_attn[:, k * cols : (k + 1) * cols]
        ).astype(BF16)
    for m in range(micro):
        sums[m].drain()


def run_mlp(n_ctx, exchange, hid, attn, cot, heads, wu, wd, ln):
    micro, rows, width = hid.shape
    ff = wu.shape[1]
    parts = 2 if exchange else 1
    sds = jax.ShapeDtypeStruct
    cols = width // parts
    grad_rows = ff + (width // parts) * (ff // cols) + 256
    outs = [
        sds((micro, rows, width), F32),
        sds((micro * rows, width), BF16),
        sds((micro, rows, width), BF16),
        sds((parts, grad_rows, cols), BF16),
        sds((8, width), F32),
    ]
    scratch = [pltpu.VMEM((micro * rows, w), BF16) for w in (ff, width, ff, width)]
    scratch += [pltpu.VMEM((micro, rows, width), BF16)] + tp_scratch(micro, rows // 2, width)
    return pl.pallas_call(
        functools.partial(mlp_kernel, n_ctx, parts),
        out_shape=outs,
        in_specs=vmem_specs(7),
        out_specs=vmem_specs(len(outs)),
        scratch_shapes=scratch,
        compiler_params=pltpu.CompilerParams(
            collective_id=1, has_side_effects=True, vmem_limit_bytes=VMEM_LIMIT
        ),
        name="mlp_both_ways",
    )(hid, attn, cot, heads.reshape(micro * rows, 256), wu, wd, ln)


class GradSum:
    def __init__(self, place, peer, own, from_dp, up, from_up, from_mid, out, send, recv):
        self.p = place
        self.peer, self.own, self.from_dp, self.up = peer, own, from_dp, up
        self.from_up, self.from_mid, self.out = from_up, from_mid, out
        self.send, self.recv = send, recv
        c, n = place.c, place.n
        low = c < n // 2
        self.toward = jnp.where(low, c + 1, c - 1)
        self.away = jnp.where(low, c - 1, c + 1)
        self.end = jnp.logical_or(c == 0, c == n - 1)
        self.inner = jnp.logical_or(c == n // 2 - 1, c == n // 2)

    def dp_copy(self):
        return remote(self.peer, self.from_dp, self.send.at[0], self.recv.at[0], dp=1 - self.p.d)

    def up_copy(self):
        return remote(self.up, self.from_up, self.send.at[1], self.recv.at[1], ctx=self.toward)

    def mid_copy(self):
        return remote(self.up, self.from_mid, self.send.at[2], self.recv.at[2], ctx=self.toward)

    def down_copy(self):
        return remote(self.out, self.out, self.send.at[3], self.recv.at[3], ctx=self.away)

    def s0(self):
        self.dp_copy().start()

    def s1(self):
        self.dp_copy().wait_recv()

        @pl.when(self.end)
        def _():
            self.up[...] = (self.own[...].astype(F32) + self.from_dp[...].astype(F32)).astype(BF16)

        @pl.when(jnp.logical_not(self.end))
        def _():
            self.up_copy().wait_recv()
            self.up[...] = (
                self.own[...].astype(F32) + self.from_dp[...].astype(F32)
                + self.from_up[...].astype(F32)
            ).astype(BF16)

        pl.when(self.inner)(lambda: self.mid_copy().start())
        pl.when(jnp.logical_not(self.inner))(lambda: self.up_copy().start())

    def s2(self):
        @pl.when(self.inner)
        def _():
            self.mid_copy().wait_recv()
            self.out[...] = (self.up[...].astype(F32) + self.from_mid[...].astype(F32)).astype(BF16)
            pl.when(jnp.logical_not(self.end))(lambda: self.down_copy().start())

    def s3(self):
        @pl.when(jnp.logical_not(self.inner))
        def _():
            self.down_copy().wait_recv()
            pl.when(jnp.logical_not(self.end))(lambda: self.down_copy().start())

    def drain(self):
        self.dp_copy().wait_send()
        pl.when(self.inner)(lambda: self.mid_copy().wait_send())
        pl.when(jnp.logical_not(self.inner))(lambda: self.up_copy().wait_send())
        pl.when(jnp.logical_not(self.end))(lambda: self.down_copy().wait_send())


PIECES = 4


def backward_kernel(n_ctx, exchange, *refs):
    (prefix, border, hid, attn, d_mid, d_attn, mlp, h1, qs, kv, o_t, lse, wo, wp, ln, grads, stats1) = refs[:17]
    refs = refs[17:]
    if exchange:
        (block, grad_in, ga, gb, gs) = refs[:5]
        refs = refs[5:]
    else:
        (block, grad_in, gb, gs) = refs[:4]
        refs = refs[4:]
    (sbuf, rbuf, acc, qh, doh, dq_t, delta, d_pack, total, stats0, kvs, kvr) = refs[:12]
    tp_refs = refs[12:19]
    refs = refs[19:]
    p = Place(n_ctx)
    c, n = p.c, n_ctx
    micro, rows, width = hid.shape
    half = rows // 2
    p.barrier(exchange, True, True)
    pieces, pack_sum, stat_sum = [], None, None
    if exchange:
        (g_dp, g_up, g_fu, g_fm, b_buf, b_dp, b_up, b_fu, b_fm, s_buf, s_dp, s_up, s_fu, s_fm, gsend, grecv) = refs
        count = ga.shape[0] // PIECES
        for i in range(PIECES):
            cut = pl.ds(i * count, count)
            pieces.append(GradSum(
                p, grads.at[1 - p.d, cut], grads.at[p.d, cut], g_dp.at[cut], g_up.at[cut],
                g_fu.at[cut], g_fm.at[cut], ga.at[cut], gsend.at[i], grecv.at[i],
            ))
        pack_sum = GradSum(
            p, b_buf.at[1 - p.d], b_buf.at[p.d], b_dp, b_up, b_fu, b_fm, gb,
            gsend.at[PIECES], grecv.at[PIECES],
        )
        stat_sum = GradSum(
            p, s_buf.at[1 - p.d], s_buf.at[p.d], s_dp, s_up, s_fu, s_fm, gs,
            gsend.at[PIECES + 1], grecv.at[PIECES + 1],
        )
        for piece in pieces:
            piece.s0()
    mlp_sums = [tp_set(p, half, tp_refs, m, block.at[m]) for m in range(micro)]
    n1_sums = [tp_set(p, half, tp_refs, micro + m, total.at[m]) for m in range(micro)]
    for m in range(micro):
        mlp_sums[m].start(lambda span, m=m: mlp[m, span, :].astype(F32))

    def kv_copy(m, way, j):
        slot = j + 1 - way
        to = c + 1 if way == 0 else c - 1
        return remote(sbuf.at[m, j], rbuf.at[m, slot], kvs.at[m, way, j], kvr.at[m, way, j], ctx=to)

    def kv_landed(m, way, j):
        slot = j + 1 - way
        to = c - 1 if way == 0 else c + 1
        return remote(sbuf.at[m, j], rbuf.at[m, slot], kvs.at[m, way, j], kvr.at[m, way, j], ctx=to)

    def upstream(way):
        return c > 0 if way == 0 else c < n - 1

    def attend_back(m, j, limits):
        for b in range(2):
            span = pl.ds(b * half, half)
            k01 = kv[m, j, span, 0:128]
            k2v0 = kv[m, j, span, 128:256]
            v12 = kv[m, j, span, 256:384]
            t01 = k01.T
            t2 = k2v0.T
            allowed = key_positions(border, 2 * j + b, half) <= limits
            sums = {}
            for h in range(3):
                scores = dot_nt(k2v0 if h == 2 else k01, qh[h])
                prob = jnp.exp(jnp.where(allowed, scores, NEG) - lse[m, h : h + 1, :])
                d_prob = dot_nt(k2v0 if h == 0 else v12, doh[h])
                d_scores = (prob * (d_prob - delta[h])).astype(BF16)
                dk = dot_nn(d_scores, qh[h])
                dv = dot_nn(prob.astype(BF16), doh[h])
                k_at, v_at = (1 if h == 2 else 0), (1 if h == 0 else 2)
                sums[k_at] = dk if k_at not in sums else sums[k_at] + dk
                sums[v_at] = dv if v_at not in sums else sums[v_at] + dv
                k_t = t2[0:64] if h == 2 else t01[h * 64 : (h + 1) * 64]
                dq_t[h * 64 : (h + 1) * 64, :] += dot_nn(k_t, d_scores)
            for k in range(3):
                acc[span, k * 128 : (k + 1) * 128] = sums[k]

    lanes = lax.broadcasted_iota(jnp.int32, (rows, 128), 1)

    def halves(value):
        zero = jnp.zeros_like(value)
        return jnp.where(lanes < 64, value, zero), jnp.where(lanes < 64, zero, value)

    def write_block(m):
        @pl.loop(0, rows // 128)
        def _(i):
            span = pl.ds(pl.multiple_of(i * 128, 128), 128)
            mid = hid[m, span, :].astype(F32) + BRANCH * attn[m, span, :].astype(F32)
            block[m, span, :] = (mid + BRANCH * block[m, span, :].astype(F32)).astype(BF16)

    def side_work(m, t):
        jobs = {}
        if m == 0:
            jobs[0] = [s.step2 for s in mlp_sums]
            jobs[4] = [s.step3 for s in mlp_sums]
            if exchange:
                jobs[2] = [pieces[0].s1, pieces[1].s1]
                jobs[5] = [pieces[2].s1, pieces[3].s1]
                jobs[6] = [pieces[0].s2, pieces[1].s2]
        else:
            jobs[0] = [n1_sums[0].step2]
            jobs[4] = [n1_sums[0].step3]
            if exchange:
                jobs[1] = [pieces[2].s2, pieces[3].s2]
                jobs[5] = [piece.s3 for piece in pieces]
        for at, work in jobs.items():
            @pl.when(t == min(at, 2 * n - 2))
            def _(work=work):
                for job in work:
                    job()

    for m in range(micro):
        flat = pl.ds(m * rows, rows)
        limits = query_limits(border, prefix, m, c, rows)
        upper = d_attn[flat, :]
        d_heads = narrow(wo, upper).astype(BF16)
        doh[0] = d_heads[:, 128:256]
        doh[1], doh[2] = halves(d_heads[:, 0:128])
        size = wo.shape[2]
        d_heads_t = dot_nt(wo[0], upper[:, 0:size])
        for i in range(1, wo.shape[0]):
            d_heads_t += dot_nt(wo[i], upper[:, i * size : (i + 1) * size])
        for h in range(3):
            at = 192 if h == 0 else (h - 1) * 64
            delta[h] = jnp.sum(d_heads_t[at : at + 64] * o_t[m, h], axis=0, keepdims=True)
        qh[0], qh[1] = halves(qs[m, :, 0:128])
        qh[2] = qs[m, :, 128:256]
        dq_t[...] = jnp.zeros(dq_t.shape, F32)

        @pl.loop(0, 2 * n - 1)
        def _(t, m=m, limits=limits):
            s = n - 1 - lax.div(t, 2)
            own = t == 2 * n - 2
            right = jnp.logical_and(lax.rem(t, 2) == 0, jnp.logical_not(own))
            j = jnp.where(right, c + s, c - s)

            @pl.when(jnp.logical_and(j >= 0, j < n))
            def _():
                attend_back(m, j, limits)

                def pass_on(way):
                    @pl.when(upstream(way))
                    def _():
                        kv_landed(m, way, j).wait_recv()
                        sbuf[m, j] = (acc[...] + rbuf[m, j + 1 - way].astype(F32)).astype(BF16)

                    @pl.when(jnp.logical_not(upstream(way)))
                    def _():
                        sbuf[m, j] = acc[...].astype(BF16)

                    kv_copy(m, way, j).start()

                pl.when(right)(lambda: pass_on(0))
                pl.when(jnp.logical_and(jnp.logical_not(right), jnp.logical_not(own)))(
                    lambda: pass_on(1)
                )

            side_work(m, t)

        @pl.when(upstream(0))
        def _():
            kv_landed(m, 0, c).wait_recv()
            acc[...] += rbuf[m, c + 1].astype(F32)

        @pl.when(upstream(1))
        def _():
            kv_landed(m, 1, c).wait_recv()
            acc[...] += rbuf[m, c].astype(F32)

        d_pack[flat, 256:640] = acc[...].astype(BF16)
        d_pack[flat, 0:256] = (dq_t[...].T * HEAD_DIM ** (-0.5)).astype(BF16)
        n1_sums[m].start(
            lambda span, m=m: dot_nt(d_pack[pl.ds(m * rows + span.start, half), :], wp[...])
        )
        if m == 0:
            for k in range(micro):
                mlp_sums[k].finish()
                mlp_sums[k].drain()
                write_block(k)

    parts = 2 if exchange else 1
    own_rows = width // parts

    def pack_part(k, to):
        @pl.loop(0, own_rows // 128)
        def _(i):
            left = h1[:, pl.ds(pl.multiple_of(k * own_rows + i * 128, 128), 128)]
            span = pl.ds(pl.multiple_of(i * 128, 128), 128)
            to[span, :] = dot_tn(left, d_pack[...]).astype(to.dtype)

    def finish_rows(m):
        gain = ln_row(ln, 0)

        @pl.loop(0, rows // 128)
        def _(i):
            span = pl.ds(pl.multiple_of(i * 128, 128), 128)
            xhat, inv = normalize(hid[m, span, :].astype(F32))
            dn = total[m, span, :].astype(F32)
            grad_in[m, span, :] = d_mid[m, span, :] + norm_back(dn, xhat, inv, gain)
            stats0[0:1, :] += column_sums(dn * xhat)
            stats0[1:2, :] += column_sums(dn)

    stats0[...] = jnp.zeros(stats0.shape, F32)
    if exchange:
        pack_part(1 - p.d, b_buf.at[1 - p.d])
        pack_sum.s0()
        n1_sums[1].step2()
        pack_part(p.d, b_buf.at[p.d])
        n1_sums[0].finish()
        finish_rows(0)
        pack_sum.s1()
        n1_sums[1].step3()
        pack_sum.s2()
        n1_sums[1].finish()
        finish_rows(1)
        for k in range(2):
            cut = slice(k * own_rows, (k + 1) * own_rows)
            s_buf[k] = jnp.concatenate(
                [stats0[0:1, cut], stats1[0:1, cut], stats0[1:2, cut], stats1[1:2, cut],
                 jnp.zeros((12, own_rows), F32)], axis=0,
            ).astype(BF16)
        stat_sum.s0()
        stat_sum.s1()
        pack_sum.s3()
        stat_sum.s2()
        stat_sum.s3()
        for piece in pieces + [pack_sum, stat_sum]:
            piece.drain()
    else:
        pack_part(0, gb)
        n1_sums[1].step2()
        n1_sums[0].finish()
        finish_rows(0)
        n1_sums[1].step3()
        n1_sums[1].finish()
        finish_rows(1)
        gs[...] = jnp.concatenate(
            [stats0[0:1, :], stats1[0:1, :], stats0[1:2, :], stats1[1:2, :],
             jnp.zeros((4, width), F32)], axis=0,
        )
    for m in range(micro):
        for j in range(n):
            pl.when(c < j)(lambda m=m, j=j: kv_copy(m, 0, j).wait_send())
            pl.when(c > j)(lambda m=m, j=j: kv_copy(m, 1, j).wait_send())
        n1_sums[m].drain()


def run_backward(n_ctx, exchange, prefix, border, tensors):
    (hid, attn, d_mid, d_attn, mlp, h1, qs, kv, o_t, lse, wo, wp, ln, grads, stats) = tensors
    micro, rows, width = hid.shape
    own_rows = width // 2
    sds = jax.ShapeDtypeStruct
    outs = [sds((micro, rows, width), BF16), sds((micro, rows, width), F32)]
    if exchange:
        outs += [
            sds(grads.shape[1:], BF16), sds((own_rows, 640), BF16), sds((16, own_rows), BF16)
        ]
    else:
        outs += [sds((width, 640), F32), sds((8, width), F32)]
    scratch = [
        pltpu.VMEM((micro, n_ctx, rows, 384), BF16),
        pltpu.VMEM((micro, n_ctx + 1, rows, 384), BF16),
        pltpu.VMEM((rows, 384), F32),
        pltpu.VMEM((3, rows, 128), BF16),
        pltpu.VMEM((3, rows, 128), BF16),
        pltpu.VMEM((256, rows), F32),
        pltpu.VMEM((3, 1, rows), F32),
        pltpu.VMEM((micro * rows, 640), BF16),
        pltpu.VMEM((micro, rows, width), BF16),
        pltpu.VMEM((8, width), F32),
        pltpu.SemaphoreType.DMA((micro, 2, n_ctx)),
        pltpu.SemaphoreType.DMA((micro, 2, n_ctx)),
    ] + tp_scratch(2 * micro, rows // 2, width)
    if exchange:
        scratch += [pltpu.VMEM(grads.shape[1:], BF16)] * 4
        scratch += [pltpu.VMEM((2, own_rows, 640), BF16)] + [pltpu.VMEM((own_rows, 640), BF16)] * 4
        scratch += [pltpu.VMEM((2, 16, own_rows), BF16)] + [pltpu.VMEM((16, own_rows), BF16)] * 4
        scratch += [pltpu.SemaphoreType.DMA((PIECES + 2, 4))] * 2
    smem = pl.BlockSpec(memory_space=pltpu.SMEM)
    return pl.pallas_call(
        functools.partial(backward_kernel, n_ctx, exchange),
        out_shape=outs,
        in_specs=[smem, smem] + vmem_specs(len(tensors)),
        out_specs=vmem_specs(len(outs)),
        scratch_shapes=scratch,
        compiler_params=pltpu.CompilerParams(
            collective_id=2, has_side_effects=True, vmem_limit_bytes=67043328
        ),
        name="attention_backward",
    )(prefix, border, *tensors)


def body(
    hidden_in, prefix, block_order, qkv_weight, out_weight, up_weight, down_weight, ln_gains,
    ln_shifts, cotangent,
):
    micro, _, tokens, width = hidden_in.shape
    n_ctx = lax.axis_size("ctx")
    exchange = lax.axis_size("dp") == 2 and n_ctx % 2 == 0
    weights = pack_weights(
        qkv_weight, out_weight, up_weight, down_weight, ln_gains, ln_shifts, exchange
    )
    hid, cot = hidden_in[:, 0], cotangent[:, 0]
    (attn, heads, lse, o_t, qs, kv, h1, wp, wo, wu, wd, ln) = run_forward(
        n_ctx, exchange, prefix, block_order, hid, weights
    )
    d_mid, d_attn, mlp, grads, stats = run_mlp(n_ctx, exchange, hid, attn, cot, heads, wu, wd, ln)
    tensors = (
        hid, attn, d_mid, d_attn, mlp, h1.reshape(micro * tokens, width), qs, kv, o_t, lse, wo, wp,
        ln, grads, stats,
    )
    out = run_backward(n_ctx, exchange, prefix, block_order, tensors)
    block, grad_in = out[:2]
    ff = up_weight.shape[1]
    if exchange:
        ga, gb, gs = (v.astype(F32) for v in out[2:])
        cols = ga.shape[1]
        g_down = ga[:ff]
        rest = ga[ff:]
        own_rows = width // 2
        g_up = jnp.concatenate(
            [rest[k * own_rows : (k + 1) * own_rows] for k in range(ff // cols)], axis=1
        )
        g_out = rest[own_rows * (ff // cols) :]
        owned = [
            jnp.stack([gb[:, 0:192], gb[:, 256:448], gb[:, 448:640]]),
            jnp.concatenate([g_out[192:], g_out[:128]], axis=0), g_up, g_down, gs[0:2], gs[2:4],
        ]
    else:
        gb, gs = out[2:]
        ga = grads[0].astype(F32)
        g_out = ga[ff + width :]
        g_up = ga[ff : ff + width]
        whole = lax.psum(
            (
                jnp.stack([gb[:, 0:192], gb[:, 256:448], gb[:, 448:640]]),
                jnp.concatenate([g_out[192:], g_out[:128]], axis=0), g_up, ga[:ff], gs[0:2], gs[2:4],
            ),
            "ctx",
        )
        owned = [
            lax.psum_scatter(v, "dp", scatter_dimension=d, tiled=True)
            for v, d in zip(whole, (1, 1, 0, 1, 1, 1))
        ]
    return (block[:, None], grad_in[:, None], *owned)


def solution(mesh):
    in_specs = (
        P(None, "dp", "ctx", None), P(None, "dp"), P(), P(None, "dp", "tp"), P("tp", "dp"),
        P("dp", "tp"), P("tp", "dp"), P(None, "dp"), P(None, "dp"), P(None, "dp", "ctx", None),
    )
    out_specs = (
        P(None, "dp", "ctx", None), P(None, "dp", "ctx", None), P(None, "dp", "tp"),
        P("tp", "dp"), P("dp", "tp"), P("tp", "dp"), P(None, "dp"), P(None, "dp"),
    )
    return jax.shard_map(body, mesh=mesh, in_specs=in_specs, out_specs=out_specs, check_vma=False)
```

```python
import functools

import jax
import jax.numpy as jnp
from jax import lax
from jax.experimental import pallas as pl
from jax.experimental.pallas import tpu as pltpu
from jax.sharding import PartitionSpec as P

HEAD_DIM = 64
DEPTH = 12
EPS = 1e-05
GELU_C = 0.7978845608028654
GELU_A = 0.044715
NEG = -1e30
BRANCH = DEPTH ** (-0.5)
MESH = pl.DeviceIdType.MESH
F32 = jnp.float32
BF16 = jnp.bfloat16


def gelu_value(u):
    return 0.5 * u * (1.0 + jnp.tanh(GELU_C * (u + GELU_A * u * u * u)))


def gelu_slope(u):
    inner = jnp.tanh(GELU_C * (u + GELU_A * u * u * u))
    return 0.5 * (1.0 + inner) + 0.5 * u * (1.0 - inner * inner) * GELU_C * (
        1.0 + 3.0 * GELU_A * u * u
    )


def normalize(x):
    centered = x - jnp.mean(x, axis=1, keepdims=True)
    inv = lax.rsqrt(jnp.mean(centered * centered, axis=1, keepdims=True) + EPS)
    return centered * inv, inv


def dot_nn(a, b):
    return lax.dot_general(a, b, (((1,), (0,)), ((), ())), preferred_element_type=F32)


def dot_nt(a, b):
    return lax.dot_general(a, b, (((1,), (1,)), ((), ())), preferred_element_type=F32)


def dot_tn(a, b):
    return lax.dot_general(a, b, (((0,), (0,)), ((), ())), preferred_element_type=F32)


def remote(src, dst, send, recv, **ids):
    return pltpu.make_async_remote_copy(
        src_ref=src, dst_ref=dst, send_sem=send, recv_sem=recv, device_id=ids, device_id_type=MESH
    )


class Place:
    def __init__(self, n_ctx):
        self.n = n_ctx
        self.c = lax.axis_index("ctx")
        self.d = lax.axis_index("dp")
        tp = lax.axis_index("tp")
        self.core = lax.rem(tp, 2)
        self.mate = tp + 1 - 2 * self.core
        chip = lax.div(tp, 2)
        self.across = (1 - chip) * 2 + self.core

    def barrier(self, dp, tp, ctx):
        sem = pltpu.get_barrier_semaphore()

        def hello(**ids):
            pl.semaphore_signal(sem, inc=1, device_id=ids, device_id_type=MESH)

        count = 0
        if dp:
            hello(dp=1 - self.d)
            count += 1
        if tp:
            hello(tp=self.mate)
            hello(tp=self.across)
            count += 2
        if ctx:
            pl.when(self.c > 0)(lambda: hello(ctx=self.c - 1))
            pl.when(self.c < self.n - 1)(lambda: hello(ctx=self.c + 1))
        if ctx:
            count = count + jnp.minimum(self.c, 1) + jnp.minimum(self.n - 1 - self.c, 1)
        pl.semaphore_wait(sem, count)


class TpSum:
    def __init__(self, place, half, mine, out_half, in_half, in_sum, total, send, recv):
        self.p, self.half = place, half
        self.mine, self.out_half, self.in_half = mine, out_half, in_half
        self.in_sum, self.total = in_sum, total
        self.send, self.recv = send, recv

    def rows(self, core):
        return pl.ds(pl.multiple_of(core * self.half, self.half), self.half)

    def c1(self):
        return remote(self.out_half, self.in_half, self.send.at[0], self.recv.at[0], tp=self.p.mate)

    def c2(self):
        return remote(self.mine, self.in_sum, self.send.at[1], self.recv.at[1], tp=self.p.across)

    def c3(self, core):
        part = self.total.at[self.rows(core)]
        return remote(part, part, self.send.at[2], self.recv.at[2], tp=self.p.mate)

    def start(self, partial):
        self.out_half[...] = partial(self.rows(1 - self.p.core)).astype(BF16)
        self.c1().start()
        self.mine[...] = partial(self.rows(self.p.core)).astype(BF16)

    def step2(self):
        self.c1().wait_recv()
        self.mine[...] = (self.mine[...].astype(F32) + self.in_half[...].astype(F32)).astype(BF16)
        self.c2().start()

    def step3(self):
        self.c2().wait_recv()
        both = self.mine[...].astype(F32) + self.in_sum[...].astype(F32)
        self.total[self.rows(self.p.core), :] = both.astype(BF16)
        self.c3(self.p.core).start()

    def finish(self):
        self.c3(1 - self.p.core).wait_recv()

    def drain(self):
        self.c1().wait_send()
        self.c2().wait_send()
        self.c3(self.p.core).wait_send()


def query_limits(border, prefix, m, c, rows):
    half = rows // 2
    lane = lax.broadcasted_iota(jnp.int32, (1, rows), 1)
    pos = jnp.where(lane < half, border[2 * c] * half + lane, border[2 * c + 1] * half + lane - half)
    return jnp.maximum(pos, prefix[m, 0] - 1)


def key_positions(border, block, half):
    return border[block] * half + lax.broadcasted_iota(jnp.int32, (half, 1), 0)


def vmem_specs(k):
    return [pl.BlockSpec(memory_space=pltpu.VMEM)] * k


def pack_weights(qkv_weight, out_weight, up_weight, down_weight, ln_gains, ln_shifts):
    q, k, v = qkv_weight[0], qkv_weight[1], qkv_weight[2]
    pad = jnp.zeros((q.shape[0], 64), BF16)
    wp = jnp.concatenate([q, pad, k, v], axis=1)
    wo = jnp.concatenate(
        [out_weight[64:], jnp.zeros((64, out_weight.shape[1]), BF16), out_weight[:64]], axis=0
    )
    ln = jnp.concatenate([ln_gains, ln_shifts], axis=0).astype(F32)
    ln = jnp.pad(ln, ((0, 4), (0, 0)))
    gather = functools.partial(lax.all_gather, axis_name="dp", tiled=True)
    return [
        gather(wp, axis=0), gather(wo, axis=1)[None], gather(up_weight, axis=0),
        gather(down_weight, axis=1)[None], gather(ln, axis=1)[None],
    ]


def wide(ref_stack, fn):
    return jnp.concatenate([fn(ref_stack[i]) for i in range(ref_stack.shape[0])], axis=1)


def narrow(ref_stack, value):
    size = ref_stack.shape[2]
    total = dot_nt(value[:, 0:size], ref_stack[0])
    for i in range(1, ref_stack.shape[0]):
        total += dot_nt(value[:, i * size : (i + 1) * size], ref_stack[i])
    return total


def norm_back(dn, xhat, inv, gain):
    e = dn * gain
    return inv * (
        e - jnp.mean(e, axis=1, keepdims=True) - xhat * jnp.mean(e * xhat, axis=1, keepdims=True)
    )


def ln_row(ln, row):
    return jnp.concatenate([ln[i, row : row + 1, :] for i in range(ln.shape[0])], axis=1)


def column_sums(value):
    return jnp.sum(value, axis=0, keepdims=True)


class GradSum:
    def __init__(self, place, peer, own, out, from_up, from_mid, send, recv):
        self.p = place
        self.peer, self.own, self.from_dp, self.up = peer, own, out, own
        self.from_up, self.from_mid, self.out = from_up, from_mid, out
        self.send, self.recv = send, recv
        c, n = place.c, place.n
        low = c < n // 2
        self.toward = jnp.where(low, c + 1, c - 1)
        self.away = jnp.where(low, c - 1, c + 1)
        self.end = jnp.logical_or(c == 0, c == n - 1)
        self.inner = jnp.logical_or(c == n // 2 - 1, c == n // 2)

    def dp_copy(self):
        return remote(self.peer, self.from_dp, self.send.at[0], self.recv.at[0], dp=1 - self.p.d)

    def up_copy(self):
        return remote(self.up, self.from_up, self.send.at[1], self.recv.at[1], ctx=self.toward)

    def mid_copy(self):
        return remote(self.up, self.from_mid, self.send.at[2], self.recv.at[2], ctx=self.toward)

    def down_copy(self):
        return remote(self.out, self.out, self.send.at[3], self.recv.at[3], ctx=self.away)

    def s0(self):
        self.dp_copy().start()

    def s1(self):
        self.dp_copy().wait_recv()

        @pl.when(self.end)
        def _():
            self.up[...] = (self.own[...].astype(F32) + self.from_dp[...].astype(F32)).astype(BF16)

        @pl.when(jnp.logical_not(self.end))
        def _():
            self.up_copy().wait_recv()
            self.up[...] = (
                self.own[...].astype(F32) + self.from_dp[...].astype(F32)
                + self.from_up[...].astype(F32)
            ).astype(BF16)

        pl.when(self.inner)(lambda: self.mid_copy().start())
        pl.when(jnp.logical_not(self.inner))(lambda: self.up_copy().start())

    def s2(self):
        @pl.when(self.inner)
        def _():
            self.mid_copy().wait_recv()
            self.out[...] = (self.up[...].astype(F32) + self.from_mid[...].astype(F32)).astype(BF16)
            pl.when(jnp.logical_not(self.end))(lambda: self.down_copy().start())

    def s3(self):
        @pl.when(jnp.logical_not(self.inner))
        def _():
            self.down_copy().wait_recv()
            pl.when(jnp.logical_not(self.end))(lambda: self.down_copy().start())

    def drain(self):
        self.dp_copy().wait_send()
        pl.when(self.inner)(lambda: self.mid_copy().wait_send())
        pl.when(jnp.logical_not(self.inner))(lambda: self.up_copy().wait_send())
        pl.when(jnp.logical_not(self.end))(lambda: self.down_copy().wait_send())


A_SUM, N2_SUM, MLP_SUM, N1_SUM = 0, 2, 4, 6
B_CUT = 128


def cuts_of(rows):
    at, cuts = 0, []
    while at < rows:
        size = min(512, rows - at)
        cuts.append((at, size))
        at += size
    return cuts


def block_kernel(n_ctx, exchange, prefix, border, hid, cot, *refs):
    if exchange:
        (qkv_s, out_s, up_s, down_s, gain_s, shift_s) = refs[:6]
        (block, grad_in, ga, gb, gs) = refs[6:11]
        (wp, wo, wu, wd, ln, grads, gb_buf, gs_buf, b_fu, b_fm, a_fu, a_fm, s_fu, s_fm,
         wsend, wrecv, gsend, grecv) = refs[11:29]
        refs = refs[29:]
    else:
        (wp, wo, wu, wd, ln) = refs[:5]
        (block, grad_in, grads, gb, gs) = refs[5:10]
        refs = refs[10:]
    (attn, heads, lse, o_t, qs, kv, h1, m_row, l_row, o_acc, act, d_mlp, d_up, h2, n2_tot, d_attn,
     sbuf, rbuf, acc, qh, doh, dq_t, delta, d_pack, stats, ks, kr, kvs, kvr,
     t_mine, t_out, t_in, t_sum, tsend, trecv) = refs
    p = Place(n_ctx)
    c, n = p.c, n_ctx
    micro, rows, width = hid.shape
    half = rows // 2
    ff = wu.shape[1]
    parts = 2 if exchange else 1
    cols = width // parts
    own_rows = width // parts
    tiles = rows // 128
    p.barrier(exchange, True, True)

    def tp_sum(kind, m, total):
        i = kind + m
        return TpSum(
            p, half, t_mine.at[i], t_out.at[i], t_in.at[i], t_sum.at[i], total, tsend.at[i],
            trecv.at[i],
        )

    a_sums = [tp_sum(A_SUM, m, attn.at[m]) for m in range(micro)]
    n2_sums = [tp_sum(N2_SUM, m, n2_tot.at[m]) for m in range(micro)]
    mlp_sums = [tp_sum(MLP_SUM, m, block.at[m]) for m in range(micro)]
    n1_sums = [tp_sum(N1_SUM, m, n2_tot.at[m]) for m in range(micro)]

    def tile(i, base=0):
        return pl.ds(pl.multiple_of(base + i * 128, 128), 128)

    if exchange:
        mine = pl.ds(pl.multiple_of(p.d * own_rows, own_rows), own_rows)
        places = (ln.at[p.d], wp.at[mine], wo.at[p.d], wu.at[mine], wd.at[p.d])
        sources = (ln.at[p.d], wp.at[mine], wo.at[p.d], up_s, down_s)

        def weight_copy(i):
            return remote(sources[i], places[i], wsend.at[i], wrecv.at[i], dp=1 - p.d)

        ln[p.d] = jnp.concatenate(
            [gain_s[...].astype(F32), shift_s[...].astype(F32), jnp.zeros((4, cols), F32)], axis=0
        )
        weight_copy(0).start()
        wp[mine, 0:256] = jnp.concatenate(
            [qkv_s[0], jnp.zeros((own_rows, 64), BF16)], axis=1
        )
        wp[mine, 256:640] = jnp.concatenate([qkv_s[1], qkv_s[2]], axis=1)
        weight_copy(1).start()
        wo[p.d, 0:128, :] = out_s[64:192, :]
        wo[p.d, 128:192, :] = jnp.zeros((64, cols), BF16)
        wo[p.d, 192:256, :] = out_s[0:64, :]
        for i in range(2, 5):
            weight_copy(i).start()
        wu[mine, :] = up_s[...]
        wd[p.d] = down_s[...]

    def weight_wait(*which):
        if exchange:
            for i in which:
                weight_copy(i).wait_recv()

    weight_wait(0)
    gain0, gain1, shift0, shift1 = (ln_row(ln, i) for i in range(4))
    for m in range(micro):
        @pl.loop(0, tiles)
        def _(i, m=m):
            xhat, _ = normalize(hid[m, tile(i), :].astype(F32))
            h1[tile(i, m * rows), :] = (xhat * gain0 + shift0).astype(BF16)

    def kv_copy(m, way, s):
        j, to = (c - s, c + 1) if way == 0 else (c + s, c - 1)
        piece = kv.at[m, j]
        return remote(piece, piece, ks.at[m, way, s], kr.at[m, way, s + 1], ctx=to)

    def kv_arrival(m, way, s):
        j, to = (c - s, c - 1) if way == 0 else (c + s, c + 1)
        piece = kv.at[m, j]
        return remote(piece, piece, ks.at[m, way, s], kr.at[m, way, s], ctx=to)

    def has(way, s):
        return c - s >= 0 if way == 0 else c + s < n

    def sends(way, s):
        if way == 0:
            return jnp.logical_and(c - s >= 0, c + 1 < n)
        return jnp.logical_and(c + s < n, c - 1 >= 0)

    weight_wait(1)
    for m in range(micro):
        @pl.loop(0, tiles)
        def _(i, m=m):
            packed = dot_nn(h1[tile(i, m * rows), :], wp[...])
            q = packed[:, 0:256].astype(BF16).astype(F32) * HEAD_DIM ** (-0.5)
            qs[m, tile(i), :] = q.astype(BF16)
            kv[m, c, tile(i), :] = packed[:, 256:640].astype(BF16)

        if m == 0:
            for way in range(2):
                pl.when(sends(way, 0))(lambda way=way: kv_copy(0, way, 0).start())
    pl.when(c == 0)(lambda: kv_copy(1, 0, 0).start())
    pl.when(c == n - 1)(lambda: kv_copy(1, 1, 0).start())

    lanes = lax.broadcasted_iota(jnp.int32, (rows, 128), 1)

    def halves(value):
        zero = jnp.zeros_like(value)
        return jnp.where(lanes < 64, value, zero), jnp.where(lanes < 64, zero, value)

    def split_queries(m):
        qh[0], qh[1] = halves(qs[m, :, 0:128])
        qh[2] = qs[m, :, 128:256]

    def attend(m, j, limits):
        for b in range(2):
            span = pl.ds(b * half, half)
            k01 = kv[m, j, span, 0:128]
            k2v0 = kv[m, j, span, 128:256]
            t0 = k2v0.T
            t12 = kv[m, j, span, 256:384].T
            allowed = key_positions(border, 2 * j + b, half) <= limits
            for h in range(3):
                scores = dot_nt(k2v0 if h == 2 else k01, qh[h])
                scores = jnp.where(allowed, scores, NEG)
                old = m_row[h]
                top = jnp.maximum(old, jnp.max(scores, axis=0, keepdims=True))
                prob = jnp.exp(scores - top)
                fade = jnp.exp(old - top)
                m_row[h] = top
                l_row[h] = l_row[h] * fade + jnp.sum(prob, axis=0, keepdims=True)
                v_t = t0[64:128] if h == 0 else t12[(h - 1) * 64 : h * 64]
                o_acc[h] = o_acc[h] * fade + dot_nn(v_t, prob.astype(BF16))

    def at_step(t, at, jobs):
        @pl.when(t == min(at, 2 * n - 2))
        def _():
            for job in jobs:
                job()

    def forward(m, side):
        limits = query_limits(border, prefix, m, c, rows)
        split_queries(m)
        m_row[...] = jnp.full(m_row.shape, NEG, F32)
        l_row[...] = jnp.zeros(l_row.shape, F32)
        o_acc[...] = jnp.zeros(o_acc.shape, F32)

        @pl.loop(0, 2 * n - 1)
        def _(t):
            s = lax.div(t + 1, 2)
            right = lax.rem(t, 2) == 1
            left = jnp.logical_and(lax.rem(t, 2) == 0, t > 0)

            def arrive(way):
                kv_arrival(m, way, s).wait_recv()
                pl.when(sends(way, s))(lambda: kv_copy(m, way, s).start())
                if m == 0:
                    last = c if way == 0 else n - 1 - c
                    pl.when(jnp.logical_and(s == last, sends(way, 0)))(
                        lambda: kv_copy(1, way, 0).start()
                    )

            pl.when(jnp.logical_and(right, has(0, s)))(lambda: arrive(0))
            pl.when(jnp.logical_and(left, has(1, s)))(lambda: arrive(1))
            j = jnp.where(right, c - s, c + s)

            @pl.when(jnp.logical_and(j >= 0, j < n))
            def _():
                attend(m, j, limits)

            for at, jobs in side.items():
                at_step(t, at, jobs)

        flat = pl.ds(m * rows, rows)
        dq_t[128:192, :] = jnp.zeros((64, rows), F32)
        for h in range(3):
            norm = o_acc[h] / l_row[h]
            o_t[m, h] = norm
            lse[m, h : h + 1, :] = m_row[h] + jnp.log(l_row[h])
            at = 192 if h == 0 else (h - 1) * 64
            dq_t[at : at + 64, :] = norm
        heads[flat, :] = dq_t[...].T.astype(BF16)
        if m == 0:
            weight_wait(2)
        a_sums[m].start(
            lambda span: wide(wo, lambda w: dot_nn(heads[pl.ds(m * rows + span.start, half), :], w))
        )

    def middle(m, i):
        return hid[m, tile(i), :].astype(F32) + BRANCH * attn[m, tile(i), :].astype(F32)

    def mlp_tiles(m, first, last):
        @pl.loop(first, last)
        def _(i):
            flat = tile(i, m * rows)
            xhat, _ = normalize(middle(m, i))
            normed = (xhat * gain1 + shift1).astype(BF16)
            h2[flat, :] = normed
            up = dot_nn(normed, wu[...])
            active = gelu_value(up).astype(BF16)
            act[flat, :] = active
            down_grad = (BRANCH * cot[m, tile(i), :].astype(F32)).astype(BF16)
            d_mlp[flat, :] = down_grad
            d_up[flat, :] = (narrow(wd, down_grad) * gelu_slope(up)).astype(BF16)
            block[m, tile(i), :] = wide(wd, lambda w: dot_nn(active, w)).astype(BF16)

    def n2_start(m):
        n2_sums[m].start(
            lambda span: dot_nt(d_up[pl.ds(m * rows + span.start, half), :], wu[...])
        )

    def mlp_start(m):
        mlp_sums[m].start(lambda span: block[m, span, :])

    def middle_gradient(m):
        @pl.loop(0, tiles)
        def _(i):
            xhat, inv = normalize(middle(m, i))
            dn = n2_tot[m, tile(i), :].astype(F32)
            grad = cot[m, tile(i), :].astype(F32) + norm_back(dn, xhat, inv, gain1)
            grad_in[m, tile(i), :] = grad
            d_attn[tile(i, m * rows), :] = (BRANCH * grad).astype(BF16)
            stats[1:2, :] += column_sums(dn * xhat)
            stats[3:4, :] += column_sums(dn)

    def write_block(m):
        mlp_sums[m].finish()
        mlp_sums[m].drain()

        @pl.loop(0, tiles)
        def _(i):
            out = middle(m, i) + BRANCH * block[m, tile(i), :].astype(F32)
            block[m, tile(i), :] = out.astype(BF16)

    def down_gradient():
        @pl.loop(0, ff // 256)
        def _(i):
            to = pl.ds(pl.multiple_of(i * 256, 256), 256)
            left = act[:, to]
            for k in range(parts):
                grads[k, to, :] = dot_tn(left, d_mlp[:, k * cols : (k + 1) * cols]).astype(BF16)

    def up_gradient():
        for k in range(parts):
            @pl.loop(0, own_rows // 128)
            def _(i, k=k):
                value = dot_tn(h2[:, tile(i, k * own_rows)], d_up[...]).astype(BF16)
                for q in range(ff // cols):
                    grads[k, tile(i, ff + q * own_rows), :] = value[:, q * cols : (q + 1) * cols]

    def out_gradient():
        at = ff + own_rows * (ff // cols)
        for k in range(parts):
            grads[k, at : at + 256, :] = dot_tn(
                heads[...], d_attn[:, k * cols : (k + 1) * cols]
            ).astype(BF16)

    early, late, last = [], [], []
    if exchange:
        for i, (at, size) in enumerate(cuts_of(grads.shape[1])):
            cut = pl.ds(at, size)
            early.append(GradSum(
                p, grads.at[1 - p.d, cut], grads.at[p.d, cut], ga.at[cut], a_fu.at[cut],
                a_fm.at[cut], gsend.at[i], grecv.at[i],
            ))
        for i in range(own_rows // B_CUT):
            cut, k = pl.ds(i * B_CUT, B_CUT), len(early) + i
            late.append(GradSum(
                p, gb_buf.at[1 - p.d, cut], gb_buf.at[p.d, cut], gb.at[cut], b_fu.at[cut],
                b_fm.at[cut], gsend.at[k], grecv.at[k],
            ))
        k = len(early) + len(late)
        last = [GradSum(
            p, gs_buf.at[1 - p.d], gs_buf.at[p.d], gs, s_fu, s_fm, gsend.at[k], grecv.at[k]
        )]

    def stage(group, name):
        return [getattr(piece, name) for piece in group]

    def dkv_copy(m, way, j):
        to = c + 1 if way == 0 else c - 1
        return remote(
            sbuf.at[j], rbuf.at[m, j + 1 - way], kvs.at[m, way, j], kvr.at[m, way, j], ctx=to
        )

    def dkv_landed(m, way, j):
        to = c - 1 if way == 0 else c + 1
        return remote(
            sbuf.at[j], rbuf.at[m, j + 1 - way], kvs.at[m, way, j], kvr.at[m, way, j], ctx=to
        )

    def upstream(way):
        return c > 0 if way == 0 else c < n - 1

    def attend_back(m, j, limits):
        for b in range(2):
            span = pl.ds(b * half, half)
            k01 = kv[m, j, span, 0:128]
            k2v0 = kv[m, j, span, 128:256]
            v12 = kv[m, j, span, 256:384]
            t01 = k01.T
            t2 = k2v0.T
            allowed = key_positions(border, 2 * j + b, half) <= limits
            sums = {}
            for h in range(3):
                scores = dot_nt(k2v0 if h == 2 else k01, qh[h])
                prob = jnp.exp(jnp.where(allowed, scores, NEG) - lse[m, h : h + 1, :])
                d_prob = dot_nt(k2v0 if h == 0 else v12, doh[h])
                d_scores = (prob * (d_prob - delta[h])).astype(BF16)
                dk = dot_nn(d_scores, qh[h])
                dv = dot_nn(prob.astype(BF16), doh[h])
                k_at, v_at = (1 if h == 2 else 0), (1 if h == 0 else 2)
                sums[k_at] = dk if k_at not in sums else sums[k_at] + dk
                sums[v_at] = dv if v_at not in sums else sums[v_at] + dv
                k_t = t2[0:64] if h == 2 else t01[h * 64 : (h + 1) * 64]
                dq_t[h * 64 : (h + 1) * 64, :] += dot_nn(k_t, d_scores)
            for k in range(3):
                acc[span, k * 128 : (k + 1) * 128] = sums[k]

    def backward(m, side):
        flat = pl.ds(m * rows, rows)
        limits = query_limits(border, prefix, m, c, rows)
        upper = d_attn[flat, :]
        d_heads = narrow(wo, upper).astype(BF16)
        doh[0] = d_heads[:, 128:256]
        doh[1], doh[2] = halves(d_heads[:, 0:128])
        size = wo.shape[2]
        d_heads_t = dot_nt(wo[0], upper[:, 0:size])
        for i in range(1, wo.shape[0]):
            d_heads_t += dot_nt(wo[i], upper[:, i * size : (i + 1) * size])
        for h in range(3):
            at = 192 if h == 0 else (h - 1) * 64
            delta[h] = jnp.sum(d_heads_t[at : at + 64] * o_t[m, h], axis=0, keepdims=True)
        split_queries(m)
        dq_t[...] = jnp.zeros(dq_t.shape, F32)

        @pl.loop(0, 2 * n - 1)
        def _(t):
            s = n - 1 - lax.div(t, 2)
            own = t == 2 * n - 2
            right = jnp.logical_and(lax.rem(t, 2) == 0, jnp.logical_not(own))
            j = jnp.where(right, c + s, c - s)

            @pl.when(jnp.logical_and(j >= 0, j < n))
            def _():
                attend_back(m, j, limits)

                def pass_on(way):
                    if m > 0:
                        dkv_copy(m - 1, way, j).wait_send()

                    @pl.when(upstream(way))
                    def _():
                        dkv_landed(m, way, j).wait_recv()
                        sbuf[j] = (acc[...] + rbuf[m, j + 1 - way].astype(F32)).astype(BF16)

                    @pl.when(jnp.logical_not(upstream(way)))
                    def _():
                        sbuf[j] = acc[...].astype(BF16)

                    dkv_copy(m, way, j).start()

                pl.when(right)(lambda: pass_on(0))
                pl.when(jnp.logical_and(jnp.logical_not(right), jnp.logical_not(own)))(
                    lambda: pass_on(1)
                )

            for at, jobs in side.items():
                at_step(t, at, jobs)

        @pl.when(upstream(0))
        def _():
            dkv_landed(m, 0, c).wait_recv()
            acc[...] += rbuf[m, c + 1].astype(F32)

        @pl.when(upstream(1))
        def _():
            dkv_landed(m, 1, c).wait_recv()
            acc[...] += rbuf[m, c].astype(F32)

        d_pack[flat, 256:640] = acc[...].astype(BF16)
        d_pack[flat, 0:256] = (dq_t[...].T * HEAD_DIM ** (-0.5)).astype(BF16)
        n1_sums[m].start(
            lambda span: dot_nt(d_pack[pl.ds(m * rows + span.start, half), :], wp[...])
        )

    def finish_rows(m):
        @pl.loop(0, tiles)
        def _(i):
            xhat, inv = normalize(hid[m, tile(i), :].astype(F32))
            dn = n2_tot[m, tile(i), :].astype(F32)
            grad_in[m, tile(i), :] += norm_back(dn, xhat, inv, gain0)
            stats[0:1, :] += column_sums(dn * xhat)
            stats[2:3, :] += column_sums(dn)

    def pack_tile(k, i):
        return dot_tn(h1[:, tile(i, k * own_rows)], d_pack[...])

    def do(jobs):
        for job in jobs:
            job()

    stats[...] = jnp.zeros(stats.shape, F32)
    a0, a1 = a_sums
    x0, x1 = n2_sums
    u0, u1 = mlp_sums
    y0, y1 = n1_sums
    forward(0, {})
    forward(1, {
        0: [a0.step2],
        2: [a0.step3, a0.finish, lambda: weight_wait(3, 4), lambda: mlp_tiles(0, 0, tiles // 2)],
        4: [lambda: mlp_tiles(0, tiles // 2, tiles), lambda: n2_start(0)],
        6: [x0.step2],
    })
    a1.step2()
    x0.step3()
    x0.finish()
    middle_gradient(0)
    x0.drain()
    backward(0, {
        0: [lambda: mlp_start(0)],
        1: [a1.step3],
        2: [a1.finish, lambda: mlp_tiles(1, 0, tiles // 2)],
        3: [u0.step2, lambda: mlp_tiles(1, tiles // 2, tiles), lambda: n2_start(1)],
        4: [x1.step2, down_gradient] + stage(early[0:1], "s0"),
        5: [up_gradient] + stage(early[1:3], "s0"),
        6: [u0.step3, lambda: mlp_start(1), x1.step3],
    })
    x1.finish()
    middle_gradient(1)
    x1.drain()
    out_gradient()
    do(stage(early[3:], "s0"))
    backward(1, {
        0: [y0.step2, u1.step2],
        2: stage(early[0:1], "s1"),
        3: [y0.step3] + stage(early[1:2], "s1"),
        4: stage(early[2:3], "s1") + stage(early[0:1], "s2"),
        5: [u1.step3] + stage(early[3:], "s1") + stage(early[1:2], "s2"),
        6: stage(early[2:], "s2") + stage(early[0:2], "s3"),
    })
    if exchange:
        for i in range(len(late)):
            gb_buf[1 - p.d, i * B_CUT : (i + 1) * B_CUT, :] = pack_tile(1 - p.d, i).astype(BF16)
            late[i].s0()
        for i in range(len(late)):
            gb_buf[p.d, i * B_CUT : (i + 1) * B_CUT, :] = pack_tile(p.d, i).astype(BF16)
    else:
        @pl.loop(0, width // 128)
        def _(i):
            gb[tile(i), :] = pack_tile(0, i)
    y1.step2()
    y0.finish()
    finish_rows(0)
    do(stage(late[0:2], "s1"))
    write_block(0)
    do(stage(late[2:], "s1"))
    y1.step3()
    do(stage(late[0:2], "s2"))
    write_block(1)
    do(stage(late[2:], "s2"))
    y1.finish()
    finish_rows(1)
    if exchange:
        for k in range(2):
            cut = slice(k * cols, (k + 1) * cols)
            gs_buf[k] = jnp.concatenate([stats[:, cut], jnp.zeros((8, cols), F32)], axis=0).astype(BF16)
        do(stage(last, "s0"))
        do(stage(early[2:], "s3"))
        do(stage(last, "s1"))
        do(stage(late, "s3"))
        do(stage(last, "s2"))
        do(stage(last, "s3"))
        for piece in early + late + last:
            piece.drain()
        for i in range(5):
            weight_copy(i).wait_send()
    else:
        gs[...] = stats[...]
    for m in range(micro):
        for way in range(2):
            for s in range(n - 1):
                pl.when(sends(way, s))(lambda m=m, way=way, s=s: kv_copy(m, way, s).wait_send())
        a_sums[m].drain()
        n1_sums[m].drain()
    for j in range(n):
        pl.when(c < j)(lambda j=j: dkv_copy(micro - 1, 0, j).wait_send())
        pl.when(c > j)(lambda j=j: dkv_copy(micro - 1, 1, j).wait_send())


def run_block(n_ctx, exchange, prefix, border, hid, cot, weights, ff):
    micro, rows, width = hid.shape
    half = rows // 2
    total = micro * rows
    parts = 2 if exchange else 1
    cols = width // parts
    sds = jax.ShapeDtypeStruct
    vmem = pltpu.VMEM
    sems = pltpu.SemaphoreType.DMA
    grad_rows = ff + cols * (ff // cols) + 256
    outs = [sds((micro, rows, width), BF16), sds((micro, rows, width), F32)]
    scratch = []
    if exchange:
        outs += [sds((grad_rows, cols), BF16), sds((cols, 640), BF16), sds((16, cols), BF16)]
        pieces = len(cuts_of(grad_rows)) + cols // B_CUT + 1
        scratch += [
            vmem((width, 640), BF16), vmem((2, 256, cols), BF16), vmem((width, ff), BF16),
            vmem((2, ff, cols), BF16), vmem((2, 8, cols), F32),
            vmem((2, grad_rows, cols), BF16), vmem((2, cols, 640), BF16), vmem((2, 16, cols), BF16),
            vmem((cols, 640), BF16), vmem((cols, 640), BF16),
            vmem((grad_rows, cols), BF16), vmem((grad_rows, cols), BF16),
            vmem((16, cols), BF16), vmem((16, cols), BF16),
            sems((5,)), sems((5,)), sems((pieces, 4)), sems((pieces, 4)),
        ]
    else:
        outs += [
            sds((1, grad_rows, cols), BF16), sds((width, 640), F32), sds((8, width), F32)
        ]
    scratch += [
        vmem((micro, rows, width), BF16), vmem((total, 256), BF16), vmem((micro, 8, rows), F32),
        vmem((micro, 3, 64, rows), F32), vmem((micro, rows, 256), BF16),
        vmem((micro, n_ctx, rows, 384), BF16), vmem((total, width), BF16),
        vmem((3, 1, rows), F32), vmem((3, 1, rows), F32), vmem((3, 64, rows), F32),
        vmem((total, ff), BF16), vmem((total, width), BF16), vmem((total, ff), BF16),
        vmem((total, width), BF16), vmem((micro, rows, width), BF16), vmem((total, width), BF16),
        vmem((n_ctx, rows, 384), BF16), vmem((micro, n_ctx + 1, rows, 384), BF16),
        vmem((rows, 384), F32), vmem((3, rows, 128), BF16), vmem((3, rows, 128), BF16),
        vmem((256, rows), F32), vmem((3, 1, rows), F32), vmem((total, 640), BF16),
        vmem((8, width), F32),
        sems((micro, 2, n_ctx + 1)), sems((micro, 2, n_ctx + 1)),
        sems((micro, 2, n_ctx)), sems((micro, 2, n_ctx)),
    ]
    scratch += [vmem((8, half, width), BF16)] * 4 + [sems((8, 3))] * 2
    smem = pl.BlockSpec(memory_space=pltpu.SMEM)
    return pl.pallas_call(
        functools.partial(block_kernel, n_ctx, exchange),
        out_shape=outs,
        in_specs=[smem, smem] + vmem_specs(2 + len(weights)),
        out_specs=vmem_specs(len(outs)),
        scratch_shapes=scratch,
        compiler_params=pltpu.CompilerParams(
            collective_id=0, has_side_effects=True, vmem_limit_bytes=67043328
        ),
        name="block_both_ways",
    )(prefix, border, hid, cot, *weights)


def unpack_kernel(ff, ga, gb, gs, qkv, out, up, down, gains, shifts):
    rows, cols = qkv.shape[1], ga.shape[1]
    down[...] = ga[0:ff, :].astype(F32)
    for k in range(ff // cols):
        up[:, k * cols : (k + 1) * cols] = ga[ff + k * rows : ff + (k + 1) * rows, :].astype(F32)
    at = ff + rows * (ff // cols)
    out[0:64, :] = ga[at + 192 : at + 256, :].astype(F32)
    out[64:192, :] = ga[at : at + 128, :].astype(F32)
    qkv[0] = gb[:, 0:192].astype(F32)
    qkv[1] = gb[:, 256:448].astype(F32)
    qkv[2] = gb[:, 384:640].astype(F32)[:, 64:256]
    gains[...] = gs[...].astype(F32)[0:2]
    shifts[...] = gs[...].astype(F32)[2:4]


def body(
    hidden_in, prefix, block_order, qkv_weight, out_weight, up_weight, down_weight, ln_gains,
    ln_shifts, cotangent,
):
    micro, _, tokens, width = hidden_in.shape
    n_ctx = lax.axis_size("ctx")
    exchange = lax.axis_size("dp") == 2 and n_ctx % 2 == 0
    ff = up_weight.shape[1]
    params = (qkv_weight, out_weight, up_weight, down_weight, ln_gains, ln_shifts)
    weights = params if exchange else pack_weights(*params)
    hid, cot = hidden_in[:, 0], cotangent[:, 0]
    block, grad_in, ga, gb, gs = run_block(
        n_ctx, exchange, prefix, block_order, hid, cot, weights, ff
    )
    if exchange:
        owned = pl.pallas_call(
            functools.partial(unpack_kernel, ff),
            out_shape=[jax.ShapeDtypeStruct(w.shape, F32) for w in params],
            in_specs=vmem_specs(3),
            out_specs=vmem_specs(6),
            name="unpack_gradients",
        )(ga, gb, gs)
    else:
        ga = ga[0].astype(F32)
        g_out = ga[ff + width :]
        whole = lax.psum(
            (
                jnp.stack([gb[:, 0:192], gb[:, 256:448], gb[:, 448:640]]),
                jnp.concatenate([g_out[192:], g_out[:128]], axis=0), ga[ff : ff + width], ga[:ff],
                gs[0:2], gs[2:4],
            ),
            "ctx",
        )
        owned = [
            lax.psum_scatter(v, "dp", scatter_dimension=d, tiled=True)
            for v, d in zip(whole, (1, 1, 0, 1, 1, 1))
        ]
    return (block[:, None], grad_in[:, None], *owned)


def solution(mesh):
    in_specs = (
        P(None, "dp", "ctx", None), P(None, "dp"), P(), P(None, "dp", "tp"), P("tp", "dp"),
        P("dp", "tp"), P("tp", "dp"), P(None, "dp"), P(None, "dp"), P(None, "dp", "ctx", None),
    )
    out_specs = (
        P(None, "dp", "ctx", None), P(None, "dp", "ctx", None), P(None, "dp", "tp"),
        P("tp", "dp"), P("dp", "tp"), P("tp", "dp"), P(None, "dp"), P(None, "dp"),
    )
    return jax.shard_map(body, mesh=mesh, in_specs=in_specs, out_specs=out_specs, check_vma=False)
```

```python
import functools

import jax
import jax.numpy as jnp
from jax import lax
from jax.experimental import pallas as pl
from jax.experimental.pallas import tpu as pltpu
from jax.sharding import PartitionSpec as P

HEAD_DIM = 64
DEPTH = 12
EPS = 1e-05
GELU_C = 0.7978845608028654
GELU_A = 0.044715
NEG = -1e30
BRANCH = DEPTH ** (-0.5)
MESH = pl.DeviceIdType.MESH
F32 = jnp.float32
BF16 = jnp.bfloat16


def gelu_value(u):
    return 0.5 * u * (1.0 + jnp.tanh(GELU_C * (u + GELU_A * u * u * u)))


def gelu_slope(u):
    inner = jnp.tanh(GELU_C * (u + GELU_A * u * u * u))
    return 0.5 * (1.0 + inner) + 0.5 * u * (1.0 - inner * inner) * GELU_C * (
        1.0 + 3.0 * GELU_A * u * u
    )


def normalize(x):
    centered = x - jnp.mean(x, axis=1, keepdims=True)
    inv = lax.rsqrt(jnp.mean(centered * centered, axis=1, keepdims=True) + EPS)
    return centered * inv, inv


def dot_nn(a, b):
    return lax.dot_general(a, b, (((1,), (0,)), ((), ())), preferred_element_type=F32)


def dot_nt(a, b):
    return lax.dot_general(a, b, (((1,), (1,)), ((), ())), preferred_element_type=F32)


def dot_tn(a, b):
    return lax.dot_general(a, b, (((0,), (0,)), ((), ())), preferred_element_type=F32)


def remote(src, dst, send, recv, **ids):
    return pltpu.make_async_remote_copy(
        src_ref=src, dst_ref=dst, send_sem=send, recv_sem=recv, device_id=ids, device_id_type=MESH
    )


class Place:
    def __init__(self, n_ctx):
        self.n = n_ctx
        self.c = lax.axis_index("ctx")
        self.d = lax.axis_index("dp")
        tp = lax.axis_index("tp")
        self.core = lax.rem(tp, 2)
        self.mate = tp + 1 - 2 * self.core
        chip = lax.div(tp, 2)
        self.across = (1 - chip) * 2 + self.core

    def barrier(self, dp, tp, ctx):
        sem = pltpu.get_barrier_semaphore()

        def hello(**ids):
            pl.semaphore_signal(sem, inc=1, device_id=ids, device_id_type=MESH)

        count = 0
        if dp:
            hello(dp=1 - self.d)
            count += 1
        if tp:
            hello(tp=self.mate)
            hello(tp=self.across)
            count += 2
        if ctx:
            pl.when(self.c > 0)(lambda: hello(ctx=self.c - 1))
            pl.when(self.c < self.n - 1)(lambda: hello(ctx=self.c + 1))
        if ctx:
            count = count + jnp.minimum(self.c, 1) + jnp.minimum(self.n - 1 - self.c, 1)
        pl.semaphore_wait(sem, count)


class TpSum:
    def __init__(self, place, half, first, size, mine, out_half, in_half, in_sum, total, send, recv):
        self.p, self.half, self.first, self.size = place, half, first, size
        self.mine, self.out_half, self.in_half = mine, out_half, in_half
        self.in_sum, self.total = in_sum, total
        self.send, self.recv = send, recv

    def rows(self, core):
        return pl.ds(pl.multiple_of(core * self.half + self.first, self.size), self.size)

    def c1(self):
        return remote(self.out_half, self.in_half, self.send.at[0], self.recv.at[0], tp=self.p.mate)

    def c2(self):
        return remote(self.mine, self.in_sum, self.send.at[1], self.recv.at[1], tp=self.p.across)

    def c3(self, core):
        part = self.total.at[self.rows(core)]
        return remote(part, part, self.send.at[2], self.recv.at[2], tp=self.p.mate)

    def start_other(self, partial):
        self.out_half[...] = partial(self.rows(1 - self.p.core)).astype(BF16)
        self.c1().start()

    def start_own(self, partial):
        self.mine[...] = partial(self.rows(self.p.core)).astype(BF16)

    def start(self, partial):
        self.start_other(partial)
        self.start_own(partial)

    def step2(self):
        self.c1().wait_recv()
        self.mine[...] = (self.mine[...].astype(F32) + self.in_half[...].astype(F32)).astype(BF16)
        self.c2().start()

    def step3(self):
        self.c2().wait_recv()
        both = self.mine[...].astype(F32) + self.in_sum[...].astype(F32)
        self.total[self.rows(self.p.core), :] = both.astype(BF16)
        self.c3(self.p.core).start()

    def finish(self):
        self.c3(1 - self.p.core).wait_recv()

    def drain(self):
        self.c1().wait_send()
        self.c2().wait_send()
        self.c3(self.p.core).wait_send()


def query_limits(border, prefix, m, c, rows):
    half = rows // 2
    lane = lax.broadcasted_iota(jnp.int32, (1, rows), 1)
    pos = jnp.where(lane < half, border[2 * c] * half + lane, border[2 * c + 1] * half + lane - half)
    return jnp.maximum(pos, prefix[m] - 1)


def key_positions(border, block, half):
    return border[block] * half + lax.broadcasted_iota(jnp.int32, (half, 1), 0)


def vmem_specs(k):
    return [pl.BlockSpec(memory_space=pltpu.VMEM)] * k


def pack_weights(qkv_weight, out_weight, up_weight, down_weight, ln_gains, ln_shifts):
    turned = jnp.swapaxes(qkv_weight, 1, 2)
    pad = jnp.zeros((64, turned.shape[2]), BF16)
    wp = jnp.concatenate([turned[0], pad, turned[1], turned[2]], axis=0)
    pad = jnp.zeros((64, out_weight.shape[1]), BF16)
    wo = jnp.concatenate([out_weight[64:], pad, out_weight[:64]], axis=0)
    ln = jnp.concatenate([ln_gains, ln_shifts], axis=0).astype(F32)
    ln = jnp.pad(ln, ((0, 4), (0, 0)))
    gather = functools.partial(lax.all_gather, axis_name="dp", tiled=True)
    return [
        gather(wp, axis=1)[None], gather(wo, axis=1)[None], gather(up_weight, axis=0),
        gather(down_weight, axis=1)[None], gather(ln, axis=1)[None],
    ]


def wide(ref_stack, fn):
    return jnp.concatenate([fn(ref_stack[i]) for i in range(ref_stack.shape[0])], axis=1)


def narrow(ref_stack, value):
    size = ref_stack.shape[2]
    total = dot_nt(value[:, 0:size], ref_stack[0])
    for i in range(1, ref_stack.shape[0]):
        total += dot_nt(value[:, i * size : (i + 1) * size], ref_stack[i])
    return total


def norm_back(dn, xhat, inv, gain):
    e = dn * gain
    return inv * (
        e - jnp.mean(e, axis=1, keepdims=True) - xhat * jnp.mean(e * xhat, axis=1, keepdims=True)
    )


def ln_row(ln, row):
    return jnp.concatenate([ln[i, row : row + 1, :] for i in range(ln.shape[0])], axis=1)


def column_sums(value):
    return jnp.sum(value, axis=0, keepdims=True)


class GradSum:
    def __init__(self, place, peer, own, out, from_up, from_mid, send, recv):
        self.p = place
        self.peer, self.own, self.from_dp, self.up = peer, own, out, own
        self.from_up, self.from_mid, self.out = from_up, from_mid, out
        self.send, self.recv = send, recv
        c, n = place.c, place.n
        low = c < n // 2
        self.toward = jnp.where(low, c + 1, c - 1)
        self.away = jnp.where(low, c - 1, c + 1)
        self.end = jnp.logical_or(c == 0, c == n - 1)
        self.inner = jnp.logical_or(c == n // 2 - 1, c == n // 2)

    def dp_copy(self):
        return remote(self.peer, self.from_dp, self.send.at[0], self.recv.at[0], dp=1 - self.p.d)

    def up_copy(self):
        return remote(self.up, self.from_up, self.send.at[1], self.recv.at[1], ctx=self.toward)

    def mid_copy(self):
        return remote(self.up, self.from_mid, self.send.at[2], self.recv.at[2], ctx=self.toward)

    def down_copy(self):
        return remote(self.out, self.out, self.send.at[3], self.recv.at[3], ctx=self.away)

    def s0(self):
        self.dp_copy().start()

    def s1(self):
        self.dp_copy().wait_recv()

        @pl.when(self.end)
        def _():
            self.up[...] = (self.own[...].astype(F32) + self.from_dp[...].astype(F32)).astype(BF16)

        @pl.when(jnp.logical_not(self.end))
        def _():
            self.up_copy().wait_recv()
            self.up[...] = (
                self.own[...].astype(F32) + self.from_dp[...].astype(F32)
                + self.from_up[...].astype(F32)
            ).astype(BF16)

        pl.when(self.inner)(lambda: self.mid_copy().start())
        pl.when(jnp.logical_not(self.inner))(lambda: self.up_copy().start())

    def s2(self):
        @pl.when(self.inner)
        def _():
            self.mid_copy().wait_recv()
            self.out[...] = (self.up[...].astype(F32) + self.from_mid[...].astype(F32)).astype(BF16)
            pl.when(jnp.logical_not(self.end))(lambda: self.down_copy().start())

    def s3(self):
        @pl.when(jnp.logical_not(self.inner))
        def _():
            self.down_copy().wait_recv()
            pl.when(jnp.logical_not(self.end))(lambda: self.down_copy().start())

    def drain(self):
        self.dp_copy().wait_send()
        pl.when(self.inner)(lambda: self.mid_copy().wait_send())
        pl.when(jnp.logical_not(self.inner))(lambda: self.up_copy().wait_send())
        pl.when(jnp.logical_not(self.end))(lambda: self.down_copy().wait_send())


A_SUM, N2_SUM, MLP_SUM, N1_SUM = 0, 2, 4, 6


def cuts_of(rows, most):
    at, cuts = 0, []
    while at < rows:
        size = min(most, rows - at)
        cuts.append((at, size))
        at += size
    return cuts


def block_kernel(n_ctx, exchange, prefix, border, hid, cot, *refs):
    if exchange:
        (qkv_s, out_s, up_s, down_s, gain_s, shift_s) = refs[:6]
        (block, grad_in, ga, gb, gs) = refs[6:11]
        (wp, wo, wu, wd, ln, grads, gb_buf, gs_buf, b_fu, b_fm, a_fu, a_fm, s_fu, s_fm,
         wsend, wrecv, gsend, grecv) = refs[11:29]
        refs = refs[29:]
    else:
        (wp, wo, wu, wd, ln) = refs[:5]
        (block, grad_in, grads, gb, gs) = refs[5:10]
        refs = refs[10:]
    (attn, heads, lse, o_t, qs, kv, h1, m_row, l_row, o_acc, act, d_mlp, d_up, h2, n2_tot, d_attn,
     sbuf, rbuf, acc, qh, doh, dq_t, delta, d_pack, stats, ks, kr, kvs, kvr,
     t_mine, t_out, t_in, t_sum, tsend, trecv) = refs
    p = Place(n_ctx)
    c, n = p.c, n_ctx
    micro, rows, width = hid.shape
    half = rows // 2
    ff = wu.shape[1]
    parts = 2 if exchange else 1
    cols = width // parts
    own_rows = width // parts
    tiles = rows // 128
    p.barrier(exchange, True, True)

    size = half // 2

    def tp_sums(kind, m, total):
        pieces = []
        for q in range(2):
            i = 2 * (kind + m) + q
            pieces.append(TpSum(
                p, half, q * size, size, t_mine.at[i], t_out.at[i], t_in.at[i], t_sum.at[i], total,
                tsend.at[i], trecv.at[i],
            ))
        return pieces

    a_sums = [tp_sums(A_SUM, m, attn.at[m]) for m in range(micro)]
    n2_sums = [tp_sums(N2_SUM, m, n2_tot.at[m]) for m in range(micro)]
    mlp_sums = [tp_sums(MLP_SUM, m, block.at[m]) for m in range(micro)]
    n1_sums = [tp_sums(N1_SUM, m, n2_tot.at[m]) for m in range(micro)]

    def start_both(group, partial):
        for piece in group:
            piece.start_other(partial)
        for piece in group:
            piece.start_own(partial)

    def tile(i, base=0):
        return pl.ds(pl.multiple_of(base + i * 128, 128), 128)

    if exchange:
        mine = pl.ds(pl.multiple_of(p.d * own_rows, own_rows), own_rows)
        places = (ln.at[p.d], wp.at[p.d], wo.at[p.d], wu.at[mine], wd.at[p.d])
        sources = (ln.at[p.d], wp.at[p.d], wo.at[p.d], up_s, down_s)

        def weight_copy(i):
            return remote(sources[i], places[i], wsend.at[i], wrecv.at[i], dp=1 - p.d)

        ln[p.d] = jnp.concatenate(
            [gain_s[...].astype(F32), shift_s[...].astype(F32), jnp.zeros((4, cols), F32)], axis=0
        )
        weight_copy(0).start()
        for i, at in enumerate((0, 256, 448)):
            wp[p.d, at : at + 192, :] = qkv_s[i]
        wp[p.d, 192:256, :] = jnp.zeros((64, cols), BF16)
        weight_copy(1).start()
        wo[p.d, 0:128, :] = out_s[64:192, :]
        wo[p.d, 128:192, :] = jnp.zeros((64, cols), BF16)
        wo[p.d, 192:256, :] = out_s[0:64, :]
        wu[mine, :] = up_s[...]
        wd[p.d] = down_s[...]

    def weight_wait(*which):
        if exchange:
            for i in which:
                weight_copy(i).wait_recv()

    weight_wait(0)
    gain0, gain1, shift0, shift1 = (ln_row(ln, i) for i in range(4))
    for m in range(micro):
        @pl.loop(0, tiles)
        def _(i, m=m):
            xhat, _ = normalize(hid[m, tile(i), :].astype(F32))
            h1[tile(i, m * rows), :] = (xhat * gain0 + shift0).astype(BF16)

    def block_rows(b):
        return pl.ds(pl.multiple_of(b * half, half), half)

    def kv_copy(m, way, s, b):
        j, to = (c - s, c + 1) if way == 0 else (c + s, c - 1)
        piece = kv.at[m, j, block_rows(b)]
        return remote(piece, piece, ks.at[m, way, s, b], kr.at[m, way, s + 1, b], ctx=to)

    def kv_arrival(m, way, s, b):
        j, to = (c - s, c - 1) if way == 0 else (c + s, c + 1)
        piece = kv.at[m, j, block_rows(b)]
        return remote(piece, piece, ks.at[m, way, s, b], kr.at[m, way, s, b], ctx=to)

    def send_own(m, way):
        for b in range(2):
            kv_copy(m, way, 0, b).start()

    def has(way, s):
        return c - s >= 0 if way == 0 else c + s < n

    def sends(way, s):
        if way == 0:
            return jnp.logical_and(c - s >= 0, c + 1 < n)
        return jnp.logical_and(c + s < n, c - 1 >= 0)

    weight_wait(1)
    if exchange:
        for i in range(2, 5):
            weight_copy(i).start()
    for m in range(micro):
        @pl.loop(0, tiles)
        def _(i, m=m):
            packed = narrow(wp, h1[tile(i, m * rows), :])
            q = packed[:, 0:256].astype(BF16).astype(F32) * HEAD_DIM ** (-0.5)
            qs[m, tile(i), :] = q.astype(BF16)
            kv[m, c, tile(i), :] = packed[:, 256:640].astype(BF16)

        if m == 0:
            for way in range(2):
                pl.when(sends(way, 0))(lambda way=way: send_own(0, way))
    pl.when(c == 0)(lambda: send_own(1, 0))
    pl.when(c == n - 1)(lambda: send_own(1, 1))

    lanes = lax.broadcasted_iota(jnp.int32, (rows, 128), 1)

    def halves(value):
        zero = jnp.zeros_like(value)
        return jnp.where(lanes < 64, value, zero), jnp.where(lanes < 64, zero, value)

    def split_queries(m):
        qh[0], qh[1] = halves(qs[m, :, 0:128])
        qh[2] = qs[m, :, 128:256]

    def attend(m, j, b, limits):
        span = block_rows(b)
        k01 = kv[m, j, span, 0:128]
        k2v0 = kv[m, j, span, 128:256]
        t0 = k2v0.T
        t12 = kv[m, j, span, 256:384].T
        allowed = key_positions(border, 2 * j + b, half) <= limits
        for h in range(3):
            scores = dot_nt(k2v0 if h == 2 else k01, qh[h])
            scores = jnp.where(allowed, scores, NEG)
            old = m_row[h]
            top = jnp.maximum(old, jnp.max(scores, axis=0, keepdims=True))
            prob = jnp.exp(scores - top)
            fade = jnp.exp(old - top)
            m_row[h] = top
            l_row[h] = l_row[h] * fade + jnp.sum(prob, axis=0, keepdims=True)
            v_t = t0[64:128] if h == 0 else t12[(h - 1) * 64 : h * 64]
            o_acc[h] = o_acc[h] * fade + dot_nn(v_t, prob.astype(BF16))

    steps = 4 * (n - 1) + 2

    def at_step(t, at, jobs):
        @pl.when(t == at)
        def _():
            for job in jobs:
                job()

    def forward(m, side):
        limits = query_limits(border, prefix, m, c, rows)
        split_queries(m)
        m_row[...] = jnp.full(m_row.shape, NEG, F32)
        l_row[...] = jnp.zeros(l_row.shape, F32)
        o_acc[...] = jnp.zeros(o_acc.shape, F32)

        @pl.loop(0, steps)
        def _(t):
            own = t < 2
            s = jnp.where(own, 0, lax.div(t + 2, 4))
            b = jnp.where(own, t, lax.rem(lax.div(t, 2) + 1, 2))
            right = jnp.logical_and(jnp.logical_not(own), lax.rem(t, 2) == 0)
            left = jnp.logical_and(jnp.logical_not(own), lax.rem(t, 2) == 1)

            def arrive(way):
                kv_arrival(m, way, s, b).wait_recv()
                pl.when(sends(way, s))(lambda: kv_copy(m, way, s, b).start())
                if m == 0:
                    last = c if way == 0 else n - 1 - c
                    ready = jnp.logical_and(jnp.logical_and(s == last, b == 1), sends(way, 0))
                    pl.when(ready)(lambda: send_own(1, way))

            pl.when(jnp.logical_and(right, has(0, s)))(lambda: arrive(0))
            pl.when(jnp.logical_and(left, has(1, s)))(lambda: arrive(1))
            j = jnp.where(right, c - s, c + s)

            @pl.when(jnp.logical_and(j >= 0, j < n))
            def _():
                attend(m, j, b, limits)

            for at, jobs in side:
                at_step(t, at, jobs)

        flat = pl.ds(m * rows, rows)
        dq_t[128:192, :] = jnp.zeros((64, rows), F32)
        for h in range(3):
            norm = o_acc[h] / l_row[h]
            o_t[m, h] = norm
            lse[m, h : h + 1, :] = m_row[h] + jnp.log(l_row[h])
            at = 192 if h == 0 else (h - 1) * 64
            dq_t[at : at + 64, :] = norm
        heads[flat, :] = dq_t[...].T.astype(BF16)
        if m == 0:
            weight_wait(2)
        start_both(
            a_sums[m],
            lambda span: wide(wo, lambda w: dot_nn(heads[pl.ds(m * rows + span.start, size), :], w)),
        )

    def middle(m, i):
        return hid[m, tile(i), :].astype(F32) + BRANCH * attn[m, tile(i), :].astype(F32)

    def mlp_tiles(m, q):
        @pl.loop(0, 2)
        def _(core):
            i = q + (tiles // 2) * core
            flat = tile(i, m * rows)
            xhat, _ = normalize(middle(m, i))
            normed = (xhat * gain1 + shift1).astype(BF16)
            h2[flat, :] = normed
            up = dot_nn(normed, wu[...])
            active = gelu_value(up).astype(BF16)
            act[flat, :] = active
            down_grad = (BRANCH * cot[m, tile(i), :].astype(F32)).astype(BF16)
            d_mlp[flat, :] = down_grad
            d_up[flat, :] = (narrow(wd, down_grad) * gelu_slope(up)).astype(BF16)
            block[m, tile(i), :] = wide(wd, lambda w: dot_nn(active, w)).astype(BF16)

        n2_sums[m][q].start(
            lambda span: dot_nt(d_up[pl.ds(m * rows + span.start, size), :], wu[...])
        )

    def mlp_start(m):
        start_both(mlp_sums[m], lambda span: block[m, span, :])

    def middle_gradient(m, q):
        n2_sums[m][q].finish()

        @pl.loop(0, 2)
        def _(core):
            i = q + (tiles // 2) * core
            xhat, inv = normalize(middle(m, i))
            dn = n2_tot[m, tile(i), :].astype(F32)
            grad = cot[m, tile(i), :].astype(F32) + norm_back(dn, xhat, inv, gain1)
            grad_in[m, tile(i), :] = grad
            d_attn[tile(i, m * rows), :] = (BRANCH * grad).astype(BF16)
            stats[1:2, :] += column_sums(dn * xhat)
            stats[3:4, :] += column_sums(dn)

    def write_block(m):
        for piece in mlp_sums[m]:
            piece.finish()
            piece.drain()

        @pl.loop(0, tiles)
        def _(i):
            out = middle(m, i) + BRANCH * block[m, tile(i), :].astype(F32)
            block[m, tile(i), :] = out.astype(BF16)

    def down_gradient():
        @pl.loop(0, ff // 256)
        def _(i):
            to = pl.ds(pl.multiple_of(i * 256, 256), 256)
            left = act[:, to]
            for k in range(parts):
                grads[k, to, :] = dot_tn(left, d_mlp[:, k * cols : (k + 1) * cols]).astype(BF16)

    def up_gradient():
        for k in range(parts):
            @pl.loop(0, own_rows // 128)
            def _(i, k=k):
                value = dot_tn(h2[:, tile(i, k * own_rows)], d_up[...]).astype(BF16)
                for q in range(ff // cols):
                    grads[k, tile(i, ff + q * own_rows), :] = value[:, q * cols : (q + 1) * cols]

    def out_gradient():
        at = ff + own_rows * (ff // cols)
        for k in range(parts):
            grads[k, at : at + 256, :] = dot_tn(
                heads[...], d_attn[:, k * cols : (k + 1) * cols]
            ).astype(BF16)

    early, late, last = [], [], []
    if exchange:
        for i, (at, count) in enumerate(cuts_of(grads.shape[1], 512)):
            cut = pl.ds(at, count)
            early.append(GradSum(
                p, grads.at[1 - p.d, cut], grads.at[p.d, cut], ga.at[cut], a_fu.at[cut],
                a_fm.at[cut], gsend.at[i], grecv.at[i],
            ))
        for i, (at, count) in enumerate(cuts_of(640, 256)):
            cut, k = pl.ds(at, count), len(early) + i
            late.append(GradSum(
                p, gb_buf.at[1 - p.d, cut], gb_buf.at[p.d, cut], gb.at[cut], b_fu.at[cut],
                b_fm.at[cut], gsend.at[k], grecv.at[k],
            ))
        k = len(early) + len(late)
        last = [GradSum(
            p, gs_buf.at[1 - p.d], gs_buf.at[p.d], gs, s_fu, s_fm, gsend.at[k], grecv.at[k]
        )]

    def stage(group, name):
        return [getattr(piece, name) for piece in group]

    def dkv_message(m, way, j, b, to):
        return remote(
            sbuf.at[j, block_rows(b)], rbuf.at[m, j + 1 - way, block_rows(b)],
            kvs.at[m, way, j, b], kvr.at[m, way, j, b], ctx=to,
        )

    def dkv_copy(m, way, j, b):
        return dkv_message(m, way, j, b, c + 1 if way == 0 else c - 1)

    def dkv_landed(m, way, j, b):
        return dkv_message(m, way, j, b, c - 1 if way == 0 else c + 1)

    def upstream(way):
        return c > 0 if way == 0 else c < n - 1

    def attend_back(m, j, b, limits):
        span = block_rows(b)
        k01 = kv[m, j, span, 0:128]
        k2v0 = kv[m, j, span, 128:256]
        v12 = kv[m, j, span, 256:384]
        t01 = k01.T
        t2 = k2v0.T
        allowed = key_positions(border, 2 * j + b, half) <= limits
        sums = {}
        for h in range(3):
            scores = dot_nt(k2v0 if h == 2 else k01, qh[h])
            prob = jnp.exp(jnp.where(allowed, scores, NEG) - lse[m, h : h + 1, :])
            d_prob = dot_nt(k2v0 if h == 0 else v12, doh[h])
            d_scores = (prob * (d_prob - delta[h])).astype(BF16)
            dk = dot_nn(d_scores, qh[h])
            dv = dot_nn(prob.astype(BF16), doh[h])
            k_at, v_at = (1 if h == 2 else 0), (1 if h == 0 else 2)
            sums[k_at] = dk if k_at not in sums else sums[k_at] + dk
            sums[v_at] = dv if v_at not in sums else sums[v_at] + dv
            k_t = t2[0:64] if h == 2 else t01[h * 64 : (h + 1) * 64]
            dq_t[h * 64 : (h + 1) * 64, :] += dot_nn(k_t, d_scores)
        for k in range(3):
            acc[span, k * 128 : (k + 1) * 128] = sums[k]

    def backward(m, side):
        flat = pl.ds(m * rows, rows)
        limits = query_limits(border, prefix, m, c, rows)
        upper = d_attn[flat, :]
        d_heads = narrow(wo, upper).astype(BF16)
        doh[0] = d_heads[:, 128:256]
        doh[1], doh[2] = halves(d_heads[:, 0:128])
        share = wo.shape[2]
        d_heads_t = dot_nt(wo[0], upper[:, 0:share])
        for i in range(1, wo.shape[0]):
            d_heads_t += dot_nt(wo[i], upper[:, i * share : (i + 1) * share])
        for h in range(3):
            at = 192 if h == 0 else (h - 1) * 64
            delta[h] = jnp.sum(d_heads_t[at : at + 64] * o_t[m, h], axis=0, keepdims=True)
        split_queries(m)
        dq_t[...] = jnp.zeros(dq_t.shape, F32)

        @pl.loop(0, steps)
        def _(t):
            own = t >= steps - 2
            s = n - 1 - lax.div(t, 4)
            b = jnp.where(own, t - (steps - 2), lax.rem(lax.div(t, 2), 2))
            right = jnp.logical_and(lax.rem(t, 2) == 0, jnp.logical_not(own))
            left = jnp.logical_and(lax.rem(t, 2) == 1, jnp.logical_not(own))
            j = jnp.where(own, c, jnp.where(right, c + s, c - s))
            span = block_rows(b)

            for at, jobs in side:
                at_step(t, at, jobs)

            @pl.when(jnp.logical_and(j >= 0, j < n))
            def _():
                attend_back(m, j, b, limits)

                def pass_on(way):
                    if m > 0:
                        dkv_copy(m - 1, way, j, b).wait_send()

                    @pl.when(upstream(way))
                    def _():
                        dkv_landed(m, way, j, b).wait_recv()
                        sbuf[j, span, :] = (
                            acc[span, :] + rbuf[m, j + 1 - way, span, :].astype(F32)
                        ).astype(BF16)

                    @pl.when(jnp.logical_not(upstream(way)))
                    def _():
                        sbuf[j, span, :] = acc[span, :].astype(BF16)

                    dkv_copy(m, way, j, b).start()

                pl.when(right)(lambda: pass_on(0))
                pl.when(left)(lambda: pass_on(1))

        for way in range(2):
            @pl.when(upstream(way))
            def _(way=way):
                for b in range(2):
                    span = block_rows(b)
                    dkv_landed(m, way, c, b).wait_recv()
                    acc[span, :] += rbuf[m, c + 1 - way, span, :].astype(F32)

        d_pack[flat, 256:640] = acc[...].astype(BF16)
        d_pack[flat, 0:256] = (dq_t[...].T * HEAD_DIM ** (-0.5)).astype(BF16)
        start_both(
            n1_sums[m],
            lambda span: wide(wp, lambda w: dot_nn(d_pack[pl.ds(m * rows + span.start, size), :], w)),
        )

    def finish_rows(m, q):
        n1_sums[m][q].finish()

        @pl.loop(0, 2)
        def _(core):
            i = q + (tiles // 2) * core
            xhat, inv = normalize(hid[m, tile(i), :].astype(F32))
            dn = n2_tot[m, tile(i), :].astype(F32)
            grad_in[m, tile(i), :] += norm_back(dn, xhat, inv, gain0)
            stats[0:1, :] += column_sums(dn * xhat)
            stats[2:3, :] += column_sums(dn)

    def pack_tile(k, at, count):
        left = h1[:, pl.ds(pl.multiple_of(k * cols, 128), cols)]
        return dot_tn(d_pack[:, at : at + count], left)

    def do(jobs):
        for job in jobs:
            job()

    def each(group, name):
        return lambda: do(stage(group, name))

    def middle_ready(m):
        for q in range(2):
            middle_gradient(m, q)
        for piece in n2_sums[m]:
            piece.drain()

    def mlp_piece(m, q):
        a_sums[m][q].finish()
        mlp_tiles(m, q)

    def by_place(at_end, inside):
        return jnp.where(jnp.logical_or(c == 0, c == n - 1), at_end, inside)

    stats[...] = jnp.zeros(stats.shape, F32)
    (a0, a1), (x0, x1), (u0, u1), (y0, y1) = a_sums, n2_sums, mlp_sums, n1_sums
    forward(0, [])
    forward(1, [
        (0, [each(a0, "step2")]),
        (3, [a0[0].step3]),
        (5, [lambda: weight_wait(3, 4), lambda: mlp_piece(0, 0), a0[1].step3]),
        (7, [x0[0].step2, lambda: mlp_piece(0, 1)]),
        (9, [x0[1].step2]),
    ])
    do(stage(x0, "step3"))
    do(stage(a1, "step2"))
    middle_ready(0)
    spot = by_place(5, 0)
    backward(0, [
        (spot, [a1[0].step3, a1[1].step3, lambda: mlp_piece(1, 0), lambda: mlp_piece(1, 1)]),
        (spot + 2, [each(x1, "step2"), lambda: mlp_start(0)]),
        (spot + 4, [down_gradient, each(early[0:1], "s0")]),
        (spot + 6, [up_gradient, each(early[1:3], "s0"), each(u0, "step2"), each(x1, "step3")]),
        (steps - 1, [lambda: mlp_start(1)]),
    ])
    middle_ready(1)
    out_gradient()
    do(stage(early[3:], "s0"))
    backward(1, [
        (0, [each(y0, "step2"), each(u0, "step3")]),
        (by_place(0, steps - 1), [each(early[0:2], "s1")]),
        (steps - 3, [each(u1, "step2"), each(y0, "step3")]),
        (by_place(steps - 1, steps), [each(early[2:], "s1")]),
    ])
    if exchange:
        for piece, (at, count) in zip(late, cuts_of(640, 256)):
            gb_buf[1 - p.d, at : at + count, :] = pack_tile(1 - p.d, at, count).astype(BF16)
            piece.s0()
        do(stage(early[0:2], "s2"))
        for at, count in cuts_of(640, 256):
            gb_buf[p.d, at : at + count, :] = pack_tile(p.d, at, count).astype(BF16)
    else:
        for at, count in cuts_of(640, 128):
            gb[at : at + count, :] = pack_tile(0, at, count)
    do(stage(y1, "step2"))
    do(stage(u1, "step3"))
    for q in range(2):
        finish_rows(0, q)
    if exchange:
        @pl.when(by_place(0, 1) == 1)
        def _():
            do(stage(early[2:], "s1"))
    write_block(0)
    do(stage(late, "s1"))
    do(stage(early[2:], "s2"))
    do(stage(y1, "step3"))
    write_block(1)
    for q in range(2):
        finish_rows(1, q)
    if exchange:
        for k in range(2):
            cut = slice(k * cols, (k + 1) * cols)
            gs_buf[k] = jnp.concatenate([stats[:, cut], jnp.zeros((8, cols), F32)], axis=0).astype(BF16)
        do(stage(last, "s0"))
        do(stage(late, "s2"))
        do(stage(last, "s1"))
        do(stage(early, "s3"))
        do(stage(last, "s2"))
        do(stage(late, "s3"))
        do(stage(last, "s3"))
        for piece in early + late + last:
            piece.drain()
        for i in range(5):
            weight_copy(i).wait_send()
    else:
        gs[...] = stats[...]
    for b in range(2):
        for m in range(micro):
            for way in range(2):
                for s in range(n - 1):
                    pl.when(sends(way, s))(
                        lambda m=m, way=way, s=s, b=b: kv_copy(m, way, s, b).wait_send()
                    )
        for j in range(n):
            pl.when(c < j)(lambda j=j, b=b: dkv_copy(micro - 1, 0, j, b).wait_send())
            pl.when(c > j)(lambda j=j, b=b: dkv_copy(micro - 1, 1, j, b).wait_send())
    for piece in a0 + a1 + y0 + y1:
        piece.drain()


def run_block(n_ctx, exchange, prefix, border, hid, cot, weights, ff):
    micro, rows, width = hid.shape
    half = rows // 2
    total = micro * rows
    parts = 2 if exchange else 1
    cols = width // parts
    sds = jax.ShapeDtypeStruct
    vmem = pltpu.VMEM
    sems = pltpu.SemaphoreType.DMA
    grad_rows = ff + cols * (ff // cols) + 256
    outs = [sds((micro, rows, width), BF16), sds((micro, rows, width), F32)]
    scratch = []
    if exchange:
        outs += [sds((grad_rows, cols), BF16), sds((640, cols), BF16), sds((16, cols), BF16)]
        pieces = len(cuts_of(grad_rows, 512)) + len(cuts_of(640, 256)) + 1
        scratch += [
            vmem((2, 640, cols), BF16), vmem((2, 256, cols), BF16), vmem((width, ff), BF16),
            vmem((2, ff, cols), BF16), vmem((2, 8, cols), F32),
            vmem((2, grad_rows, cols), BF16), vmem((2, 640, cols), BF16), vmem((2, 16, cols), BF16),
            vmem((640, cols), BF16), vmem((640, cols), BF16),
            vmem((grad_rows, cols), BF16), vmem((grad_rows, cols), BF16),
            vmem((16, cols), BF16), vmem((16, cols), BF16),
            sems((5,)), sems((5,)), sems((pieces, 4)), sems((pieces, 4)),
        ]
    else:
        outs += [
            sds((1, grad_rows, cols), BF16), sds((640, width), F32), sds((8, width), F32)
        ]
    scratch += [
        vmem((micro, rows, width), BF16), vmem((total, 256), BF16), vmem((micro, 8, rows), F32),
        vmem((micro, 3, 64, rows), F32), vmem((micro, rows, 256), BF16),
        vmem((micro, n_ctx, rows, 384), BF16), vmem((total, width), BF16),
        vmem((3, 1, rows), F32), vmem((3, 1, rows), F32), vmem((3, 64, rows), F32),
        vmem((total, ff), BF16), vmem((total, width), BF16), vmem((total, ff), BF16),
        vmem((total, width), BF16), vmem((micro, rows, width), BF16), vmem((total, width), BF16),
        vmem((n_ctx, rows, 384), BF16), vmem((micro, n_ctx + 1, rows, 384), BF16),
        vmem((rows, 384), F32), vmem((3, rows, 128), BF16), vmem((3, rows, 128), BF16),
        vmem((256, rows), F32), vmem((3, 1, rows), F32), vmem((total, 640), BF16),
        vmem((8, width), F32),
        sems((micro, 2, n_ctx + 1, 2)), sems((micro, 2, n_ctx + 1, 2)),
        sems((micro, 2, n_ctx, 2)), sems((micro, 2, n_ctx, 2)),
    ]
    scratch += [vmem((16, half // 2, width), BF16)] * 4 + [sems((16, 3))] * 2
    smem = pl.BlockSpec(memory_space=pltpu.SMEM)
    return pl.pallas_call(
        functools.partial(block_kernel, n_ctx, exchange),
        out_shape=outs,
        in_specs=[smem, smem] + vmem_specs(2 + len(weights)),
        out_specs=vmem_specs(len(outs)),
        scratch_shapes=scratch,
        compiler_params=pltpu.CompilerParams(
            collective_id=0, has_side_effects=True, vmem_limit_bytes=67043328
        ),
        name="block_both_ways",
    )(prefix, border, hid, cot, *weights)


def unpack_kernel(ff, ga, gb, gs, qkv, out, up, down, gains, shifts):
    rows, cols = qkv.shape[2], ga.shape[1]
    down[...] = ga[0:ff, :].astype(F32)
    for k in range(ff // cols):
        up[:, k * cols : (k + 1) * cols] = ga[ff + k * rows : ff + (k + 1) * rows, :].astype(F32)
    at = ff + rows * (ff // cols)
    out[0:64, :] = ga[at + 192 : at + 256, :].astype(F32)
    out[64:192, :] = ga[at : at + 128, :].astype(F32)
    for i, at in enumerate((0, 256, 448)):
        qkv[i] = gb[at : at + 192, :].astype(F32)
    gains[...] = gs[...].astype(F32)[0:2]
    shifts[...] = gs[...].astype(F32)[2:4]


def body(
    hidden_in, prefix, block_order, qkv_weight, out_weight, up_weight, down_weight, ln_gains,
    ln_shifts, cotangent,
):
    micro, _, tokens, width = hidden_in.shape
    n_ctx = lax.axis_size("ctx")
    exchange = lax.axis_size("dp") == 2 and n_ctx % 2 == 0
    ff = up_weight.shape[1]
    params = (qkv_weight, out_weight, up_weight, down_weight, ln_gains, ln_shifts)
    turned = jnp.swapaxes(qkv_weight, 1, 2)
    weights = (turned,) + params[1:] if exchange else pack_weights(*params)
    hid, cot = hidden_in[:, 0], cotangent[:, 0]
    block, grad_in, ga, gb, gs = run_block(
        n_ctx, exchange, prefix[:, 0], block_order, hid, cot, weights, ff
    )
    if exchange:
        owned = pl.pallas_call(
            functools.partial(unpack_kernel, ff),
            out_shape=[jax.ShapeDtypeStruct(w.shape, F32) for w in (turned,) + params[1:]],
            in_specs=vmem_specs(3),
            out_specs=vmem_specs(6),
            name="unpack_gradients",
        )(ga, gb, gs)
        owned = [jnp.swapaxes(owned[0], 1, 2)] + list(owned[1:])
    else:
        ga = ga[0].astype(F32)
        g_out = ga[ff + width :]
        whole = lax.psum(
            (
                jnp.swapaxes(jnp.stack([gb[0:192], gb[256:448], gb[448:640]]), 1, 2),
                jnp.concatenate([g_out[192:], g_out[:128]], axis=0), ga[ff : ff + width], ga[:ff],
                gs[0:2], gs[2:4],
            ),
            "ctx",
        )
        owned = [
            lax.psum_scatter(v, "dp", scatter_dimension=d, tiled=True)
            for v, d in zip(whole, (1, 1, 0, 1, 1, 1))
        ]
    return (block[:, None], grad_in[:, None], *owned)


def solution(mesh):
    in_specs = (
        P(None, "dp", "ctx", None), P(None, "dp"), P(), P(None, "dp", "tp"), P("tp", "dp"),
        P("dp", "tp"), P("tp", "dp"), P(None, "dp"), P(None, "dp"), P(None, "dp", "ctx", None),
    )
    out_specs = (
        P(None, "dp", "ctx", None), P(None, "dp", "ctx", None), P(None, "dp", "tp"),
        P("tp", "dp"), P("dp", "tp"), P("tp", "dp"), P(None, "dp"), P(None, "dp"),
    )
    return jax.shard_map(body, mesh=mesh, in_specs=in_specs, out_specs=out_specs, check_vma=False)
```

```python
import functools

import jax
import jax.numpy as jnp
from jax import lax
from jax.experimental import pallas as pl
from jax.experimental.pallas import tpu as pltpu
from jax.sharding import PartitionSpec as P

HEAD_DIM = 64
DEPTH = 12
EPS = 1e-05
GELU_C = 0.7978845608028654
GELU_A = 0.044715
NEG = -1e30
BRANCH = DEPTH ** (-0.5)
MESH = pl.DeviceIdType.MESH
F32 = jnp.float32
BF16 = jnp.bfloat16


def gelu_value(u):
    return 0.5 * u * (1.0 + jnp.tanh(GELU_C * (u + GELU_A * u * u * u)))


def gelu_slope(u):
    inner = jnp.tanh(GELU_C * (u + GELU_A * u * u * u))
    return 0.5 * (1.0 + inner) + 0.5 * u * (1.0 - inner * inner) * GELU_C * (
        1.0 + 3.0 * GELU_A * u * u
    )


def normalize(x):
    centered = x - jnp.mean(x, axis=1, keepdims=True)
    inv = lax.rsqrt(jnp.mean(centered * centered, axis=1, keepdims=True) + EPS)
    return centered * inv, inv


def dot_nn(a, b):
    return lax.dot_general(a, b, (((1,), (0,)), ((), ())), preferred_element_type=F32)


def dot_nt(a, b):
    return lax.dot_general(a, b, (((1,), (1,)), ((), ())), preferred_element_type=F32)


def dot_tn(a, b):
    return lax.dot_general(a, b, (((0,), (0,)), ((), ())), preferred_element_type=F32)


def remote(src, dst, send, recv, **ids):
    return pltpu.make_async_remote_copy(
        src_ref=src, dst_ref=dst, send_sem=send, recv_sem=recv, device_id=ids, device_id_type=MESH
    )


class Place:
    def __init__(self, n_ctx):
        self.n = n_ctx
        self.c = lax.axis_index("ctx")
        self.d = lax.axis_index("dp")
        tp = lax.axis_index("tp")
        self.core = lax.rem(tp, 2)
        self.mate = tp + 1 - 2 * self.core
        chip = lax.div(tp, 2)
        self.across = (1 - chip) * 2 + self.core

    def barrier(self, dp, tp, ctx):
        sem = pltpu.get_barrier_semaphore()

        def hello(**ids):
            pl.semaphore_signal(sem, inc=1, device_id=ids, device_id_type=MESH)

        count = 0
        if dp:
            hello(dp=1 - self.d)
            count += 1
        if tp:
            hello(tp=self.mate)
            hello(tp=self.across)
            count += 2
        if ctx:
            pl.when(self.c > 0)(lambda: hello(ctx=self.c - 1))
            pl.when(self.c < self.n - 1)(lambda: hello(ctx=self.c + 1))
        if ctx:
            count = count + jnp.minimum(self.c, 1) + jnp.minimum(self.n - 1 - self.c, 1)
        pl.semaphore_wait(sem, count)


class TpSum:
    def __init__(self, place, half, first, size, mine, out_half, in_half, in_sum, total, send, recv):
        self.p, self.half, self.first, self.size = place, half, first, size
        self.mine, self.out_half, self.in_half = mine, out_half, in_half
        self.in_sum, self.total = in_sum, total
        self.send, self.recv = send, recv

    def rows(self, core):
        return pl.ds(pl.multiple_of(core * self.half + self.first, self.size), self.size)

    def c1(self):
        return remote(self.out_half, self.in_half, self.send.at[0], self.recv.at[0], tp=self.p.mate)

    def c2(self):
        return remote(self.mine, self.in_sum, self.send.at[1], self.recv.at[1], tp=self.p.across)

    def c3(self, core):
        part = self.total.at[self.rows(core)]
        return remote(part, part, self.send.at[2], self.recv.at[2], tp=self.p.mate)

    def start_other(self, partial):
        self.out_half[...] = partial(self.rows(1 - self.p.core)).astype(BF16)
        self.c1().start()

    def start_own(self, partial):
        self.mine[...] = partial(self.rows(self.p.core)).astype(BF16)

    def start(self, partial):
        self.start_other(partial)
        self.start_own(partial)

    def step2(self):
        self.c1().wait_recv()
        self.mine[...] = (self.mine[...].astype(F32) + self.in_half[...].astype(F32)).astype(BF16)
        self.c2().start()

    def step3(self):
        self.c2().wait_recv()
        both = self.mine[...].astype(F32) + self.in_sum[...].astype(F32)
        self.total[self.rows(self.p.core), :] = both.astype(BF16)
        self.c3(self.p.core).start()

    def finish(self):
        self.c3(1 - self.p.core).wait_recv()

    def drain(self):
        self.c1().wait_send()
        self.c2().wait_send()
        self.c3(self.p.core).wait_send()


def query_limits(border, prefix, m, c, rows):
    half = rows // 2
    lane = lax.broadcasted_iota(jnp.int32, (1, rows), 1)
    pos = jnp.where(lane < half, border[2 * c] * half + lane, border[2 * c + 1] * half + lane - half)
    return jnp.maximum(pos, prefix[m] - 1)


def key_positions(border, block, half):
    return border[block] * half + lax.broadcasted_iota(jnp.int32, (half, 1), 0)


def vmem_specs(k):
    return [pl.BlockSpec(memory_space=pltpu.VMEM)] * k


def pack_weights(qkv_weight, out_weight, up_weight, down_weight, ln_gains, ln_shifts):
    turned = jnp.swapaxes(qkv_weight, 1, 2)
    pad = jnp.zeros((64, turned.shape[2]), BF16)
    wp = jnp.concatenate([turned[0], pad, turned[1], turned[2]], axis=0)
    pad = jnp.zeros((64, out_weight.shape[1]), BF16)
    wo = jnp.concatenate([out_weight[64:], pad, out_weight[:64]], axis=0)
    ln = jnp.concatenate([ln_gains, ln_shifts], axis=0).astype(F32)
    ln = jnp.pad(ln, ((0, 4), (0, 0)))
    gather = functools.partial(lax.all_gather, axis_name="dp", tiled=True)
    return [
        gather(wp, axis=1)[None], gather(wo, axis=1)[None], gather(up_weight, axis=0),
        gather(down_weight, axis=1)[None], gather(ln, axis=1)[None],
    ]


def wide(ref_stack, fn):
    return jnp.concatenate([fn(ref_stack[i]) for i in range(ref_stack.shape[0])], axis=1)


def narrow(ref_stack, value, at=0, count=None):
    size = ref_stack.shape[2]
    span = pl.ds(at, ref_stack.shape[1] if count is None else count)
    total = dot_nt(value[:, 0:size], ref_stack[0, span, :])
    for i in range(1, ref_stack.shape[0]):
        total += dot_nt(value[:, i * size : (i + 1) * size], ref_stack[i, span, :])
    return total


def norm_back(dn, xhat, inv, gain):
    e = dn * gain
    return inv * (
        e - jnp.mean(e, axis=1, keepdims=True) - xhat * jnp.mean(e * xhat, axis=1, keepdims=True)
    )


def ln_row(ln, row):
    return jnp.concatenate([ln[i, row : row + 1, :] for i in range(ln.shape[0])], axis=1)


def column_sums(value):
    return jnp.sum(value, axis=0, keepdims=True)


class GradSum:
    def __init__(self, place, peer, own, out, from_up, from_mid, send, recv):
        self.p = place
        self.peer, self.own, self.from_dp, self.up = peer, own, out, own
        self.from_up, self.from_mid, self.out = from_up, from_mid, out
        self.send, self.recv = send, recv
        c, n = place.c, place.n
        low = c < n // 2
        self.toward = jnp.where(low, c + 1, c - 1)
        self.away = jnp.where(low, c - 1, c + 1)
        self.end = jnp.logical_or(c == 0, c == n - 1)
        self.inner = jnp.logical_or(c == n // 2 - 1, c == n // 2)

    def dp_copy(self):
        return remote(self.peer, self.from_dp, self.send.at[0], self.recv.at[0], dp=1 - self.p.d)

    def up_copy(self):
        return remote(self.up, self.from_up, self.send.at[1], self.recv.at[1], ctx=self.toward)

    def mid_copy(self):
        return remote(self.up, self.from_mid, self.send.at[2], self.recv.at[2], ctx=self.toward)

    def down_copy(self):
        return remote(self.out, self.out, self.send.at[3], self.recv.at[3], ctx=self.away)

    def s0(self):
        self.dp_copy().start()

    def s1(self):
        self.dp_copy().wait_recv()

        @pl.when(self.end)
        def _():
            self.up[...] = (self.own[...].astype(F32) + self.from_dp[...].astype(F32)).astype(BF16)

        @pl.when(jnp.logical_not(self.end))
        def _():
            self.up_copy().wait_recv()
            self.up[...] = (
                self.own[...].astype(F32) + self.from_dp[...].astype(F32)
                + self.from_up[...].astype(F32)
            ).astype(BF16)

        pl.when(self.inner)(lambda: self.mid_copy().start())
        pl.when(jnp.logical_not(self.inner))(lambda: self.up_copy().start())

    def s2(self):
        @pl.when(self.inner)
        def _():
            self.mid_copy().wait_recv()
            self.out[...] = (self.up[...].astype(F32) + self.from_mid[...].astype(F32)).astype(BF16)
            pl.when(jnp.logical_not(self.end))(lambda: self.down_copy().start())

    def s3(self):
        @pl.when(jnp.logical_not(self.inner))
        def _():
            self.down_copy().wait_recv()
            pl.when(jnp.logical_not(self.end))(lambda: self.down_copy().start())

    def drain(self):
        self.dp_copy().wait_send()
        pl.when(self.inner)(lambda: self.mid_copy().wait_send())
        pl.when(jnp.logical_not(self.inner))(lambda: self.up_copy().wait_send())
        pl.when(jnp.logical_not(self.end))(lambda: self.down_copy().wait_send())


EARLY_ROWS = 384
PACK_CUTS = ((0, 256, 0, 192), (256, 256, 192, 256), (512, 128, 448, 128))
A_SUM, N2_SUM, MLP_SUM, N1_SUM = 0, 2, 4, 6


def cuts_of(rows, most):
    at, cuts = 0, []
    while at < rows:
        size = min(most, rows - at)
        cuts.append((at, size))
        at += size
    return cuts


def block_kernel(n_ctx, exchange, prefix, border, hid, cot, *refs):
    if exchange:
        (qkv_s, out_s, up_s, down_s, gain_s, shift_s) = refs[:6]
        (block, grad_in, ga, gb, gs) = refs[6:11]
        (wp, wo, wu, wd, ln, grads, gb_buf, gs_buf, b_fu, b_fm, a_fu, a_fm, s_fu, s_fm,
         wsend, wrecv, gsend, grecv) = refs[11:29]
        refs = refs[29:]
    else:
        (wp, wo, wu, wd, ln) = refs[:5]
        (block, grad_in, grads, gb, gs) = refs[5:10]
        refs = refs[10:]
    (attn, heads, lse, o_t, qs, kv, h1, m_row, l_row, o_acc, act, d_mlp, d_up, h2, n2_tot, d_attn,
     sbuf, rbuf, q_all, do_all, st_all, qos, qor, acc, qh, doh, dq_t, delta, d_pack, stats, ks, kr, kvs, kvr,
     t_mine, t_out, t_in, t_sum, tsend, trecv) = refs
    p = Place(n_ctx)
    c, n = p.c, n_ctx
    micro, rows, width = hid.shape
    half = rows // 2
    ff = wu.shape[1]
    parts = 2 if exchange else 1
    cols = width // parts
    own_rows = width // parts
    tiles = rows // 128
    p.barrier(exchange, True, True)

    size = half // 2

    def tp_sums(kind, m, total):
        pieces = []
        for q in range(2):
            i = 2 * (kind + m) + q
            pieces.append(TpSum(
                p, half, q * size, size, t_mine.at[i], t_out.at[i], t_in.at[i], t_sum.at[i], total,
                tsend.at[i], trecv.at[i],
            ))
        return pieces

    a_sums = [tp_sums(A_SUM, m, attn.at[m]) for m in range(micro)]
    n2_sums = [tp_sums(N2_SUM, m, n2_tot.at[m]) for m in range(micro)]
    mlp_sums = [tp_sums(MLP_SUM, m, block.at[m]) for m in range(micro)]
    n1_sums = [tp_sums(N1_SUM, m, n2_tot.at[m]) for m in range(micro)]

    def start_both(group, partial):
        for piece in group:
            piece.start_other(partial)
        for piece in group:
            piece.start_own(partial)

    def tile(i, base=0):
        return pl.ds(pl.multiple_of(base + i * 128, 128), 128)

    if exchange:
        mine = pl.ds(pl.multiple_of(p.d * own_rows, own_rows), own_rows)
        kv_part, q_part = wp.at[p.d, pl.ds(256, 384)], wp.at[p.d, pl.ds(0, 192)]
        places = (ln.at[p.d], kv_part, q_part, wo.at[p.d], wu.at[mine], wd.at[p.d])
        sources = (ln.at[p.d], kv_part, q_part, wo.at[p.d], up_s, down_s)

        def weight_copy(i):
            return remote(sources[i], places[i], wsend.at[i], wrecv.at[i], dp=1 - p.d)

        ln[p.d] = jnp.concatenate(
            [gain_s[...].astype(F32), shift_s[...].astype(F32), jnp.zeros((4, cols), F32)], axis=0
        )
        weight_copy(0).start()
        wp[p.d, 256:448, :] = qkv_s[1]
        wp[p.d, 448:640, :] = qkv_s[2]
        weight_copy(1).start()
        wp[p.d, 0:192, :] = qkv_s[0]
        for k in range(2):
            wp[k, 192:256, :] = jnp.zeros((64, cols), BF16)
        wo[p.d, 0:128, :] = out_s[64:192, :]
        wo[p.d, 128:192, :] = jnp.zeros((64, cols), BF16)
        wo[p.d, 192:256, :] = out_s[0:64, :]
        wu[mine, :] = up_s[...]
        wd[p.d] = down_s[...]

    def weight_wait(*which):
        if exchange:
            for i in which:
                weight_copy(i).wait_recv()

    weight_wait(0)
    gain0, gain1, shift0, shift1 = (ln_row(ln, i) for i in range(4))
    for m in range(micro):
        @pl.loop(0, tiles)
        def _(i, m=m):
            xhat, _ = normalize(hid[m, tile(i), :].astype(F32))
            h1[tile(i, m * rows), :] = (xhat * gain0 + shift0).astype(BF16)

    def block_rows(b):
        return pl.ds(pl.multiple_of(b * half, half), half)

    def kv_copy(m, way, s, b):
        j, to = (c - s, c + 1) if way == 0 else (c + s, c - 1)
        piece = kv.at[m, j, block_rows(b)]
        return remote(piece, piece, ks.at[m, way, s, b], kr.at[m, way, s + 1, b], ctx=to)

    def kv_arrival(m, way, s, b):
        j, to = (c - s, c - 1) if way == 0 else (c + s, c + 1)
        piece = kv.at[m, j, block_rows(b)]
        return remote(piece, piece, ks.at[m, way, s, b], kr.at[m, way, s, b], ctx=to)

    def send_own(m, way):
        for b in range(2):
            kv_copy(m, way, 0, b).start()

    def has(way, s):
        return c - s >= 0 if way == 0 else c + s < n

    def sends(way, s):
        if way == 0:
            return jnp.logical_and(c - s >= 0, c + 1 < n)
        return jnp.logical_and(c + s < n, c - 1 >= 0)

    weight_wait(1)
    if exchange:
        weight_copy(2).start()
    for m in range(micro):
        @pl.loop(0, 2)
        def _(b, m=m):
            for i in range(tiles // 2):
                span = pl.ds(pl.multiple_of(b * half + i * 128, 128), 128)
                flat = pl.ds(pl.multiple_of(m * rows + b * half + i * 128, 128), 128)
                kv[m, c, span, :] = narrow(wp, h1[flat, :], 256, 384).astype(BF16)
            if m == 0:
                for way in range(2):
                    pl.when(sends(way, 0))(lambda way=way: kv_copy(0, way, 0, b).start())

    pl.when(c == 0)(lambda: send_own(1, 0))
    pl.when(c == n - 1)(lambda: send_own(1, 1))
    weight_wait(2)
    if exchange:
        for i in range(3, 6):
            weight_copy(i).start()
    for m in range(micro):
        @pl.loop(0, tiles)
        def _(i, m=m):
            q = narrow(wp, h1[tile(i, m * rows), :], 0, 256).astype(BF16).astype(F32)
            qs[m, tile(i), :] = (q * HEAD_DIM ** (-0.5)).astype(BF16)

    lanes = lax.broadcasted_iota(jnp.int32, (rows, 128), 1)

    def halves(value):
        zero = jnp.zeros_like(value)
        return jnp.where(lanes < 64, value, zero), jnp.where(lanes < 64, zero, value)

    def split_queries(m):
        qh[0], qh[1] = halves(qs[m, :, 0:128])
        qh[2] = qs[m, :, 128:256]

    def attend(m, j, b, limits):
        span = block_rows(b)
        k01 = kv[m, j, span, 0:128]
        k2v0 = kv[m, j, span, 128:256]
        t0 = k2v0.T
        t12 = kv[m, j, span, 256:384].T
        allowed = key_positions(border, 2 * j + b, half) <= limits
        for h in range(3):
            scores = dot_nt(k2v0 if h == 2 else k01, qh[h])
            scores = jnp.where(allowed, scores, NEG)
            old = m_row[h]
            top = jnp.maximum(old, jnp.max(scores, axis=0, keepdims=True))
            prob = jnp.exp(scores - top)
            fade = jnp.exp(old - top)
            m_row[h] = top
            l_row[h] = l_row[h] * fade + jnp.sum(prob, axis=0, keepdims=True)
            v_t = t0[64:128] if h == 0 else t12[(h - 1) * 64 : h * 64]
            o_acc[h] = o_acc[h] * fade + dot_nn(v_t, prob.astype(BF16))

    steps = 4 * (n - 1) + 2

    def at_step(t, at, jobs):
        @pl.when(t == at)
        def _():
            for job in jobs:
                job()

    def forward(m, side):
        limits = query_limits(border, prefix, m, c, rows)
        split_queries(m)
        m_row[...] = jnp.full(m_row.shape, NEG, F32)
        l_row[...] = jnp.zeros(l_row.shape, F32)
        o_acc[...] = jnp.zeros(o_acc.shape, F32)

        @pl.loop(0, steps)
        def _(t):
            own = t < 2
            s = jnp.where(own, 0, lax.div(t + 2, 4))
            b = jnp.where(own, t, lax.rem(lax.div(t, 2) + 1, 2))
            right = jnp.logical_and(jnp.logical_not(own), lax.rem(t, 2) == 0)
            left = jnp.logical_and(jnp.logical_not(own), lax.rem(t, 2) == 1)

            def arrive(way):
                kv_arrival(m, way, s, b).wait_recv()
                pl.when(sends(way, s))(lambda: kv_copy(m, way, s, b).start())
                if m == 0:
                    last = c if way == 0 else n - 1 - c
                    ready = jnp.logical_and(jnp.logical_and(s == last, b == 1), sends(way, 0))
                    pl.when(ready)(lambda: send_own(1, way))

            pl.when(jnp.logical_and(right, has(0, s)))(lambda: arrive(0))
            pl.when(jnp.logical_and(left, has(1, s)))(lambda: arrive(1))
            j = jnp.where(right, c - s, c + s)

            @pl.when(jnp.logical_and(j >= 0, j < n))
            def _():
                attend(m, j, b, limits)

            for at, jobs in side:
                at_step(t, at, jobs)

        flat = pl.ds(m * rows, rows)
        dq_t[128:192, :] = jnp.zeros((64, rows), F32)
        for h in range(3):
            norm = o_acc[h] / l_row[h]
            o_t[m, h] = norm
            lse[m, h : h + 1, :] = m_row[h] + jnp.log(l_row[h])
            at = 192 if h == 0 else (h - 1) * 64
            dq_t[at : at + 64, :] = norm
        heads[flat, :] = dq_t[...].T.astype(BF16)
        if m == 0:
            weight_wait(3)
        start_both(
            a_sums[m],
            lambda span: wide(wo, lambda w: dot_nn(heads[pl.ds(m * rows + span.start, size), :], w)),
        )

    def middle(m, i):
        return hid[m, tile(i), :].astype(F32) + BRANCH * attn[m, tile(i), :].astype(F32)

    def mlp_tiles(m, q):
        @pl.loop(0, 2)
        def _(core):
            i = q + (tiles // 2) * core
            flat = tile(i, m * rows)
            xhat, _ = normalize(middle(m, i))
            normed = (xhat * gain1 + shift1).astype(BF16)
            h2[flat, :] = normed
            up = dot_nn(normed, wu[...])
            active = gelu_value(up).astype(BF16)
            act[flat, :] = active
            down_grad = (BRANCH * cot[m, tile(i), :].astype(F32)).astype(BF16)
            d_mlp[flat, :] = down_grad
            d_up[flat, :] = (narrow(wd, down_grad) * gelu_slope(up)).astype(BF16)
            block[m, tile(i), :] = wide(wd, lambda w: dot_nn(active, w)).astype(BF16)

        n2_sums[m][q].start(
            lambda span: dot_nt(d_up[pl.ds(m * rows + span.start, size), :], wu[...])
        )

    def mlp_start(m):
        start_both(mlp_sums[m], lambda span: block[m, span, :])

    def middle_gradient(m, q):
        n2_sums[m][q].finish()

        @pl.loop(0, 2)
        def _(core):
            i = q + (tiles // 2) * core
            xhat, inv = normalize(middle(m, i))
            dn = n2_tot[m, tile(i), :].astype(F32)
            grad = cot[m, tile(i), :].astype(F32) + norm_back(dn, xhat, inv, gain1)
            grad_in[m, tile(i), :] = grad
            d_attn[tile(i, m * rows), :] = (BRANCH * grad).astype(BF16)
            stats[1:2, :] += column_sums(dn * xhat)
            stats[3:4, :] += column_sums(dn)

    def write_block(m):
        for piece in mlp_sums[m]:
            piece.finish()
            piece.drain()

        @pl.loop(0, tiles)
        def _(i):
            out = middle(m, i) + BRANCH * block[m, tile(i), :].astype(F32)
            block[m, tile(i), :] = out.astype(BF16)

    def down_gradient():
        @pl.loop(0, ff // 256)
        def _(i):
            to = pl.ds(pl.multiple_of(i * 256, 256), 256)
            left = act[:, to]
            for k in range(parts):
                grads[k, to, :] = dot_tn(left, d_mlp[:, k * cols : (k + 1) * cols]).astype(BF16)

    def up_gradient():
        for k in range(parts):
            @pl.loop(0, own_rows // 128)
            def _(i, k=k):
                value = dot_tn(h2[:, tile(i, k * own_rows)], d_up[...]).astype(BF16)
                for q in range(ff // cols):
                    grads[k, tile(i, ff + q * own_rows), :] = value[:, q * cols : (q + 1) * cols]

    def out_gradient():
        at = ff + own_rows * (ff // cols)
        for k in range(parts):
            value = dot_tn(heads[...], d_attn[:, k * cols : (k + 1) * cols]).astype(BF16)
            grads[k, at : at + 128, :] = value[0:128]
            grads[k, at + 128 : at + 192, :] = value[192:256]

    early, late, last = [], [], []
    if exchange:
        for i, (at, count) in enumerate(cuts_of(grads.shape[1], EARLY_ROWS)):
            cut = pl.ds(at, count)
            early.append(GradSum(
                p, grads.at[1 - p.d, cut], grads.at[p.d, cut], ga.at[cut], a_fu.at[cut],
                a_fm.at[cut], gsend.at[i], grecv.at[i],
            ))
        for i, (_, _, to, count) in enumerate(PACK_CUTS):
            cut, k = pl.ds(to, count), len(early) + i
            late.append(GradSum(
                p, gb_buf.at[1 - p.d, cut], gb_buf.at[p.d, cut], gb.at[cut], b_fu.at[cut],
                b_fm.at[cut], gsend.at[k], grecv.at[k],
            ))
        k = len(early) + len(late)
        last = [GradSum(
            p, gs_buf.at[1 - p.d], gs_buf.at[p.d], gs, s_fu, s_fm, gsend.at[k], grecv.at[k]
        )]

    def stage(group, name):
        return [getattr(piece, name) for piece in group]

    def dkv_message(way, j, b, to):
        return remote(
            sbuf.at[j, block_rows(b)], rbuf.at[j + 1 - way, block_rows(b)],
            kvs.at[way, j, b], kvr.at[way, j, b], ctx=to,
        )

    def dkv_copy(way, j, b):
        return dkv_message(way, j, b, c + 1 if way == 0 else c - 1)

    def dkv_landed(way, j, b):
        return dkv_message(way, j, b, c - 1 if way == 0 else c + 1)

    gathered = (q_all, do_all, st_all)

    def qo_copy(kind, way, s):
        j, to = (c - s, c + 1) if way == 0 else (c + s, c - 1)
        piece = gathered[kind].at[j]
        return remote(piece, piece, qos.at[kind, way, s], qor.at[kind, way, s + 1], ctx=to)

    def qo_arrival(kind, way, s):
        j, to = (c - s, c - 1) if way == 0 else (c + s, c + 1)
        piece = gathered[kind].at[j]
        return remote(piece, piece, qos.at[kind, way, s], qor.at[kind, way, s], ctx=to)

    def qo_send(kind):
        for way in range(2):
            pl.when(sends(way, 0))(lambda way=way: qo_copy(kind, way, 0).start())

    def qo_step(kind, way, s):
        @pl.when(has(way, s))
        def _():
            qo_arrival(kind, way, s).wait_recv()
            pl.when(sends(way, s))(lambda: qo_copy(kind, way, s).start())

    def qo_steps(kind, s):
        for way in range(2):
            qo_step(kind, way, s)

    def send_queries(m):
        q_all[c] = qs[m].T[0:192]
        qo_send(0)

    def upstream(way):
        return c > 0 if way == 0 else c < n - 1

    def attend_back(m, j, b, limits, keys_too=True):
        span = block_rows(b)
        k01 = kv[m, j, span, 0:128]
        k2v0 = kv[m, j, span, 128:256]
        v12 = kv[m, j, span, 256:384]
        t01 = k01.T
        t2 = k2v0.T
        allowed = key_positions(border, 2 * j + b, half) <= limits
        sums = {}
        for h in range(3):
            scores = dot_nt(k2v0 if h == 2 else k01, qh[h])
            prob = jnp.exp(jnp.where(allowed, scores, NEG) - lse[m, h : h + 1, :])
            d_prob = dot_nt(k2v0 if h == 0 else v12, doh[h])
            d_scores = (prob * (d_prob - delta[h])).astype(BF16)
            k_t = t2[0:64] if h == 2 else t01[h * 64 : (h + 1) * 64]
            dq_t[h * 64 : (h + 1) * 64, :] += dot_nn(k_t, d_scores)
            if keys_too:
                dk = dot_nn(d_scores, qh[h])
                dv = dot_nn(prob.astype(BF16), doh[h])
                k_at, v_at = (1 if h == 2 else 0), (1 if h == 0 else 2)
                sums[k_at] = dk if k_at not in sums else sums[k_at] + dk
                sums[v_at] = dv if v_at not in sums else sums[v_at] + dv
        for k in sums:
            acc[span, k * 128 : (k + 1) * 128] = sums[k]

    def attend_keys(m, j, b):
        span = block_rows(b)
        k01 = kv[m, c, span, 0:128]
        k2v0 = kv[m, c, span, 128:256]
        v12 = kv[m, c, span, 256:384]
        limits = query_limits(border, prefix, m, j, rows)
        allowed = key_positions(border, 2 * c + b, half) <= limits
        zero = jnp.zeros((64, rows), BF16)
        for h in range(3):
            q_h = q_all[j, h * 64 : (h + 1) * 64, :]
            q_h = jnp.concatenate([zero, q_h] if h == 1 else [q_h, zero], axis=0)
            do_h = do_all[j, h * 64 : (h + 1) * 64, :]
            do_h = jnp.concatenate([do_h, zero] if h == 1 else [zero, do_h], axis=0)
            scores = dot_nn(k2v0 if h == 2 else k01, q_h)
            prob = jnp.exp(jnp.where(allowed, scores, NEG) - st_all[j, h : h + 1, :])
            d_prob = dot_nn(k2v0 if h == 0 else v12, do_h)
            d_scores = (prob * (d_prob - st_all[j, 3 + h : 4 + h, :])).astype(BF16)
            k_at, v_at = (128 if h == 2 else 0), (128 if h == 0 else 256)
            acc[span, k_at : k_at + 128] += dot_nt(d_scores, q_h)
            acc[span, v_at : v_at + 128] += dot_nt(prob.astype(BF16), do_h)

    def head_gradients(m):
        upper = d_attn[pl.ds(m * rows, rows), :]
        share = wo.shape[2]
        d_heads_t = dot_nt(wo[0], upper[:, 0:share])
        for i in range(1, wo.shape[0]):
            d_heads_t += dot_nt(wo[i], upper[:, i * share : (i + 1) * share])
        for h in range(3):
            at = 192 if h == 0 else (h - 1) * 64
            delta[h] = jnp.sum(d_heads_t[at : at + 64] * o_t[m, h], axis=0, keepdims=True)
            if m > 0:
                do_all[c, h * 64 : (h + 1) * 64, :] = d_heads_t[at : at + 64].astype(BF16)
                st_all[c, h : h + 1, :] = lse[m, h : h + 1, :]
                st_all[c, 3 + h : 4 + h, :] = delta[h]
        if m > 0:
            st_all[c, 6:8, :] = jnp.zeros((2, rows), F32)
            qo_send(2)
            qo_send(1)
        d_heads = narrow(wo, upper).astype(BF16)
        doh[0] = d_heads[:, 128:256]
        doh[1], doh[2] = halves(d_heads[:, 0:128])
        split_queries(m)
        dq_t[...] = jnp.zeros(dq_t.shape, F32)

    def backward_end(m):
        flat = pl.ds(m * rows, rows)
        d_pack[flat, 256:640] = acc[...].astype(BF16)
        d_pack[flat, 0:256] = (dq_t[...].T * HEAD_DIM ** (-0.5)).astype(BF16)
        start_both(
            n1_sums[m],
            lambda span: wide(wp, lambda w: dot_nn(d_pack[pl.ds(m * rows + span.start, size), :], w)),
        )

    def backward(m, side):
        limits = query_limits(border, prefix, m, c, rows)
        head_gradients(m)

        @pl.loop(0, steps)
        def _(t):
            own = t >= steps - 2
            s = n - 1 - lax.div(t, 4)
            b = jnp.where(own, t - (steps - 2), lax.rem(lax.div(t, 2), 2))
            right = jnp.logical_and(lax.rem(t, 2) == 0, jnp.logical_not(own))
            left = jnp.logical_and(lax.rem(t, 2) == 1, jnp.logical_not(own))
            j = jnp.where(own, c, jnp.where(right, c + s, c - s))
            span = block_rows(b)

            for at, jobs in side:
                at_step(t, at, jobs)

            @pl.when(jnp.logical_and(j >= 0, j < n))
            def _():
                attend_back(m, j, b, limits)

                def pass_on(way):
                    @pl.when(upstream(way))
                    def _():
                        dkv_landed(way, j, b).wait_recv()
                        sbuf[j, span, :] = (
                            acc[span, :] + rbuf[j + 1 - way, span, :].astype(F32)
                        ).astype(BF16)

                    @pl.when(jnp.logical_not(upstream(way)))
                    def _():
                        sbuf[j, span, :] = acc[span, :].astype(BF16)

                    dkv_copy(way, j, b).start()

                pl.when(right)(lambda: pass_on(0))
                pl.when(left)(lambda: pass_on(1))

        for way in range(2):
            @pl.when(upstream(way))
            def _(way=way):
                for b in range(2):
                    span = block_rows(b)
                    dkv_landed(way, c, b).wait_recv()
                    acc[span, :] += rbuf[c + 1 - way, span, :].astype(F32)

        backward_end(m)

    def backward_last(m, side, side_keys):
        limits = query_limits(border, prefix, m, c, rows)
        head_gradients(m)

        @pl.loop(0, 2)
        def _(b):
            attend_back(m, c, b, limits)

        @pl.loop(0, 2 * (n - 1))
        def _(t):
            j = lax.rem(c + 1 + lax.div(t, 2), n)
            attend_back(m, j, lax.rem(t, 2), limits, keys_too=False)
            for at, jobs in side:
                at_step(t, at, jobs)

        @pl.loop(0, 2 * (n - 1))
        def _(t):
            s = 1 + lax.div(t, 2)
            for way in range(2):
                @pl.when(jnp.logical_and(lax.rem(t, 2) == way, has(way, s)))
                def _(way=way):
                    pl.when(s > 2)(lambda: qo_step(2, way, s))
                    pl.when(s > 2)(lambda: qo_step(1, way, s))
                    for b in range(2):
                        attend_keys(m, c - s if way == 0 else c + s, b)
            for at, jobs in side_keys:
                at_step(t, at, jobs)

        backward_end(m)

    def finish_rows(m, q):
        n1_sums[m][q].finish()

        @pl.loop(0, 2)
        def _(core):
            i = q + (tiles // 2) * core
            xhat, inv = normalize(hid[m, tile(i), :].astype(F32))
            dn = n2_tot[m, tile(i), :].astype(F32)
            grad_in[m, tile(i), :] += norm_back(dn, xhat, inv, gain0)
            stats[0:1, :] += column_sums(dn * xhat)
            stats[2:3, :] += column_sums(dn)

    def pack_part(to, k, at, count, first, kept):
        left = h1[:, pl.ds(pl.multiple_of(k * cols, 128), cols)]
        value = dot_tn(d_pack[:, at : at + count], left)
        to[first : first + kept, :] = value[0:kept].astype(to.dtype)

    def do(jobs):
        for job in jobs:
            job()

    def each(group, name):
        return lambda: do(stage(group, name))

    def middle_ready(m):
        for q in range(2):
            middle_gradient(m, q)
        for piece in n2_sums[m]:
            piece.drain()

    def mlp_piece(m, q):
        a_sums[m][q].finish()
        mlp_tiles(m, q)

    def by_place(at_end, inside):
        return jnp.where(jnp.logical_or(c == 0, c == n - 1), at_end, inside)

    stats[...] = jnp.zeros(stats.shape, F32)
    (a0, a1), (x0, x1), (u0, u1), (y0, y1) = a_sums, n2_sums, mlp_sums, n1_sums
    forward(0, [])
    forward(1, [
        (0, [each(a0, "step2")]),
        (3, [a0[0].step3]),
        (4, [
            lambda: weight_wait(4, 5), lambda: mlp_piece(0, 0), a0[1].step3, x0[0].step2,
            lambda: mlp_piece(0, 1),
        ]),
        (6, [x0[1].step2]),
    ])
    do(stage(x0, "step3"))
    do(stage(a1, "step2"))
    middle_ready(0)
    spot = by_place(5, 0)
    send_queries(1)
    backward(0, [
        (2, [lambda: qo_steps(0, 1)]),
        (spot, [a1[0].step3, a1[1].step3, lambda: mlp_piece(1, 0), lambda: mlp_piece(1, 1)]),
        (6, [lambda: qo_steps(0, 2)]),
        (spot + 2, [each(x1, "step2"), lambda: mlp_start(0)]),
        (spot + 4, [down_gradient, each(early[0:2], "s0")]),
        (spot + 6, [up_gradient, each(early[2:-1], "s0"), each(u0, "step2"), each(x1, "step3")]),
        (steps - 1, [lambda: mlp_start(1)] + [lambda s=s: qo_steps(0, s) for s in range(3, n)]),
    ])
    middle_ready(1)
    backward_last(1, [
        (0, [out_gradient, each(early[-1:], "s0"), each(y0, "step2")]),
        (by_place(0, 5), [each(early[0:1], "s1")]),
        (by_place(1, 6), [each(early[1:2], "s1")]),
        (2, [lambda: qo_steps(2, 1), lambda: qo_steps(1, 1)]),
        (5, [lambda: qo_steps(2, 2), lambda: qo_steps(1, 2)]),
    ], [
        (by_place(0, 2), [each(early[2:3], "s1")]),
        (by_place(6, 0), [each(early[1:2], "s1")]),
        (1, [each(y0, "step3"), each(u0, "step3")]),
        (2, [each(early[0:1], "s2")]),
        (by_place(2, 5), [each(early[3:4], "s1")]),
        (3, [each(u1, "step2")]),
        (4, [each(early[1:2], "s2")]),
        (by_place(5, 6), [each(early[4:5], "s1")]),
    ])
    if exchange:
        for piece, cut in zip(late, PACK_CUTS):
            pack_part(gb_buf.at[1 - p.d], 1 - p.d, *cut)
            piece.s0()
        for cut in PACK_CUTS:
            pack_part(gb_buf.at[p.d], p.d, *cut)
    else:
        for cut in PACK_CUTS:
            pack_part(gb, 0, *cut)
    do(stage(y1, "step2"))
    for q in range(2):
        finish_rows(0, q)
    if exchange:
        @pl.when(by_place(0, 1) == 1)
        def _():
            early[4].s1()

        early[2].s2()
    do(stage(u1, "step3"))
    write_block(0)
    if exchange:
        early[3].s2()
    do(stage(y1, "step3"))
    write_block(1)
    for q in range(2):
        finish_rows(1, q)
    if exchange:
        for k in range(2):
            cut = slice(k * cols, (k + 1) * cols)
            gs_buf[k] = jnp.concatenate([stats[:, cut], jnp.zeros((8, cols), F32)], axis=0).astype(BF16)
        do(stage(last, "s0"))

        chain = early + late + last
        for i in range(5, len(chain) + 1):
            if i < len(chain):
                chain[i].s1()
            chain[i - 1].s2()
        for piece in early + late + last:
            piece.s3()
        for piece in early + late + last:
            piece.drain()
        for i in range(6):
            weight_copy(i).wait_send()
    else:
        gs[...] = stats[...]
    for b in range(2):
        for m in range(micro):
            for way in range(2):
                for s in range(n - 1):
                    pl.when(sends(way, s))(
                        lambda m=m, way=way, s=s, b=b: kv_copy(m, way, s, b).wait_send()
                    )
        for j in range(n):
            pl.when(c < j)(lambda j=j, b=b: dkv_copy(0, j, b).wait_send())
            pl.when(c > j)(lambda j=j, b=b: dkv_copy(1, j, b).wait_send())
    for kind in range(3):
        for way in range(2):
            for s in range(n - 1):
                pl.when(sends(way, s))(
                    lambda kind=kind, way=way, s=s: qo_copy(kind, way, s).wait_send()
                )
    for piece in a0 + a1 + y0 + y1:
        piece.drain()


def run_block(n_ctx, exchange, prefix, border, hid, cot, weights, ff):
    micro, rows, width = hid.shape
    half = rows // 2
    total = micro * rows
    parts = 2 if exchange else 1
    cols = width // parts
    sds = jax.ShapeDtypeStruct
    vmem = pltpu.VMEM
    sems = pltpu.SemaphoreType.DMA
    grad_rows = ff + cols * (ff // cols) + 192
    outs = [sds((micro, rows, width), BF16), sds((micro, rows, width), F32)]
    scratch = []
    if exchange:
        outs += [sds((grad_rows, cols), BF16), sds((576, cols), BF16), sds((16, cols), BF16)]
        pieces = len(cuts_of(grad_rows, EARLY_ROWS)) + len(PACK_CUTS) + 1
        scratch += [
            vmem((2, 640, cols), BF16), vmem((2, 256, cols), BF16), vmem((width, ff), BF16),
            vmem((2, ff, cols), BF16), vmem((2, 8, cols), F32),
            vmem((2, grad_rows, cols), BF16), vmem((2, 576, cols), BF16), vmem((2, 16, cols), BF16),
            vmem((576, cols), BF16), vmem((576, cols), BF16),
            vmem((grad_rows, cols), BF16), vmem((grad_rows, cols), BF16),
            vmem((16, cols), BF16), vmem((16, cols), BF16),
            sems((6,)), sems((6,)), sems((pieces, 4)), sems((pieces, 4)),
        ]
    else:
        outs += [
            sds((1, grad_rows, cols), BF16), sds((576, width), F32), sds((8, width), F32)
        ]
    scratch += [
        vmem((micro, rows, width), BF16), vmem((total, 256), BF16), vmem((micro, 8, rows), F32),
        vmem((micro, 3, 64, rows), F32), vmem((micro, rows, 256), BF16),
        vmem((micro, n_ctx, rows, 384), BF16), vmem((total, width), BF16),
        vmem((3, 1, rows), F32), vmem((3, 1, rows), F32), vmem((3, 64, rows), F32),
        vmem((total, ff), BF16), vmem((total, width), BF16), vmem((total, ff), BF16),
        vmem((total, width), BF16), vmem((micro, rows, width), BF16), vmem((total, width), BF16),
        vmem((n_ctx, rows, 384), BF16), vmem((n_ctx + 1, rows, 384), BF16),
        vmem((n_ctx, 192, rows), BF16), vmem((n_ctx, 192, rows), BF16), vmem((n_ctx, 8, rows), F32),
        sems((3, 2, n_ctx + 1)), sems((3, 2, n_ctx + 1)),
        vmem((rows, 384), F32), vmem((3, rows, 128), BF16), vmem((3, rows, 128), BF16),
        vmem((256, rows), F32), vmem((3, 1, rows), F32), vmem((total, 640), BF16),
        vmem((8, width), F32),
        sems((micro, 2, n_ctx + 1, 2)), sems((micro, 2, n_ctx + 1, 2)),
        sems((2, n_ctx, 2)), sems((2, n_ctx, 2)),
    ]
    scratch += [vmem((16, half // 2, width), BF16)] * 4 + [sems((16, 3))] * 2
    smem = pl.BlockSpec(memory_space=pltpu.SMEM)
    return pl.pallas_call(
        functools.partial(block_kernel, n_ctx, exchange),
        out_shape=outs,
        in_specs=[smem, smem] + vmem_specs(2 + len(weights)),
        out_specs=vmem_specs(len(outs)),
        scratch_shapes=scratch,
        compiler_params=pltpu.CompilerParams(
            collective_id=0, has_side_effects=True, vmem_limit_bytes=67043328
        ),
        name="block_both_ways",
    )(prefix, border, hid, cot, *weights)


def unpack_kernel(ff, ga, gb, gs, qkv, out, up, down, gains, shifts):
    rows, cols = qkv.shape[2], ga.shape[1]
    down[...] = ga[0:ff, :].astype(F32)
    for k in range(ff // cols):
        up[:, k * cols : (k + 1) * cols] = ga[ff + k * rows : ff + (k + 1) * rows, :].astype(F32)
    at = ff + rows * (ff // cols)
    out[0:64, :] = ga[at + 128 : at + 192, :].astype(F32)
    out[64:192, :] = ga[at : at + 128, :].astype(F32)
    for i, at in enumerate((0, 192, 384)):
        qkv[i] = gb[at : at + 192, :].astype(F32)
    gains[...] = gs[...].astype(F32)[0:2]
    shifts[...] = gs[...].astype(F32)[2:4]


def body(
    hidden_in, prefix, block_order, qkv_weight, out_weight, up_weight, down_weight, ln_gains,
    ln_shifts, cotangent,
):
    micro, _, tokens, width = hidden_in.shape
    n_ctx = lax.axis_size("ctx")
    exchange = lax.axis_size("dp") == 2 and n_ctx % 2 == 0
    ff = up_weight.shape[1]
    params = (qkv_weight, out_weight, up_weight, down_weight, ln_gains, ln_shifts)
    turned = jnp.swapaxes(qkv_weight, 1, 2)
    weights = (turned,) + params[1:] if exchange else pack_weights(*params)
    hid, cot = hidden_in[:, 0], cotangent[:, 0]
    block, grad_in, ga, gb, gs = run_block(
        n_ctx, exchange, prefix[:, 0], block_order, hid, cot, weights, ff
    )
    if exchange:
        owned = pl.pallas_call(
            functools.partial(unpack_kernel, ff),
            out_shape=[jax.ShapeDtypeStruct(w.shape, F32) for w in (turned,) + params[1:]],
            in_specs=vmem_specs(3),
            out_specs=vmem_specs(6),
            name="unpack_gradients",
        )(ga, gb, gs)
        owned = [jnp.swapaxes(owned[0], 1, 2)] + list(owned[1:])
    else:
        ga = ga[0].astype(F32)
        g_out = ga[ff + width :]
        whole = lax.psum(
            (
                jnp.swapaxes(gb.reshape(3, 192, -1), 1, 2),
                jnp.concatenate([g_out[128:], g_out[:128]], axis=0), ga[ff : ff + width], ga[:ff],
                gs[0:2], gs[2:4],
            ),
            "ctx",
        )
        owned = [
            lax.psum_scatter(v, "dp", scatter_dimension=d, tiled=True)
            for v, d in zip(whole, (1, 1, 0, 1, 1, 1))
        ]
    return (block[:, None], grad_in[:, None], *owned)


def solution(mesh):
    in_specs = (
        P(None, "dp", "ctx", None), P(None, "dp"), P(), P(None, "dp", "tp"), P("tp", "dp"),
        P("dp", "tp"), P("tp", "dp"), P(None, "dp"), P(None, "dp"), P(None, "dp", "ctx", None),
    )
    out_specs = (
        P(None, "dp", "ctx", None), P(None, "dp", "ctx", None), P(None, "dp", "tp"),
        P("tp", "dp"), P("dp", "tp"), P("tp", "dp"), P(None, "dp"), P(None, "dp"),
    )
    return jax.shard_map(body, mesh=mesh, in_specs=in_specs, out_specs=out_specs, check_vma=False)
```

```python
import functools

import jax
import jax.numpy as jnp
from jax import lax
from jax.experimental import pallas as pl
from jax.experimental.pallas import tpu as pltpu
from jax.sharding import PartitionSpec as P

HEAD_DIM = 64
DEPTH = 12
EPS = 1e-05
GELU_C = 0.7978845608028654
GELU_A = 0.044715
NEG = -1e30
BRANCH = DEPTH ** (-0.5)
MESH = pl.DeviceIdType.MESH
F32 = jnp.float32
BF16 = jnp.bfloat16


def gelu_value(u):
    return 0.5 * u * (1.0 + jnp.tanh(GELU_C * (u + GELU_A * u * u * u)))


def gelu_slope(u):
    inner = jnp.tanh(GELU_C * (u + GELU_A * u * u * u))
    return 0.5 * (1.0 + inner) + 0.5 * u * (1.0 - inner * inner) * GELU_C * (
        1.0 + 3.0 * GELU_A * u * u
    )


def normalize(x):
    centered = x - jnp.mean(x, axis=1, keepdims=True)
    inv = lax.rsqrt(jnp.mean(centered * centered, axis=1, keepdims=True) + EPS)
    return centered * inv, inv


def dot_nn(a, b):
    return lax.dot_general(a, b, (((1,), (0,)), ((), ())), preferred_element_type=F32)


def dot_nt(a, b):
    return lax.dot_general(a, b, (((1,), (1,)), ((), ())), preferred_element_type=F32)


def dot_tn(a, b):
    return lax.dot_general(a, b, (((0,), (0,)), ((), ())), preferred_element_type=F32)


def remote(src, dst, send, recv, **ids):
    return pltpu.make_async_remote_copy(
        src_ref=src, dst_ref=dst, send_sem=send, recv_sem=recv, device_id=ids, device_id_type=MESH
    )


class Place:
    def __init__(self, n_ctx):
        self.n = n_ctx
        self.c = lax.axis_index("ctx")
        self.d = lax.axis_index("dp")
        tp = lax.axis_index("tp")
        self.core = lax.rem(tp, 2)
        self.mate = tp + 1 - 2 * self.core
        chip = lax.div(tp, 2)
        self.across = (1 - chip) * 2 + self.core

    def barrier(self, dp, tp, ctx):
        sem = pltpu.get_barrier_semaphore()

        def hello(**ids):
            pl.semaphore_signal(sem, inc=1, device_id=ids, device_id_type=MESH)

        count = 0
        if dp:
            hello(dp=1 - self.d)
            count += 1
        if tp:
            hello(tp=self.mate)
            hello(tp=self.across)
            count += 2
        if ctx:
            for j in range(1, self.n):
                hello(ctx=lax.rem(self.c + j, self.n))
            count += self.n - 1
        pl.semaphore_wait(sem, count)


class TpSum:
    def __init__(self, place, half, first, size, mine, out_half, in_half, in_sum, total, send, recv):
        self.p, self.half, self.first, self.size = place, half, first, size
        self.mine, self.out_half, self.in_half = mine, out_half, in_half
        self.in_sum, self.total = in_sum, total
        self.send, self.recv = send, recv

    def rows(self, core):
        return pl.ds(pl.multiple_of(core * self.half + self.first, self.size), self.size)

    def c1(self):
        return remote(self.out_half, self.in_half, self.send.at[0], self.recv.at[0], tp=self.p.mate)

    def c2(self):
        return remote(self.mine, self.in_sum, self.send.at[1], self.recv.at[1], tp=self.p.across)

    def c3(self, core):
        part = self.total.at[self.rows(core)]
        return remote(part, part, self.send.at[2], self.recv.at[2], tp=self.p.mate)

    def start_other(self, partial):
        self.out_half[...] = partial(self.rows(1 - self.p.core)).astype(BF16)
        self.c1().start()

    def start_own(self, partial):
        self.mine[...] = partial(self.rows(self.p.core)).astype(BF16)

    def start(self, partial):
        self.start_other(partial)
        self.start_own(partial)

    def step2(self):
        self.c1().wait_recv()
        self.mine[...] = (self.mine[...].astype(F32) + self.in_half[...].astype(F32)).astype(BF16)
        self.c2().start()

    def step3(self):
        self.c2().wait_recv()
        both = self.mine[...].astype(F32) + self.in_sum[...].astype(F32)
        self.total[self.rows(self.p.core), :] = both.astype(BF16)
        self.c3(self.p.core).start()

    def finish(self):
        self.c3(1 - self.p.core).wait_recv()

    def drain(self):
        self.c1().wait_send()
        self.c2().wait_send()
        self.c3(self.p.core).wait_send()


def query_limits(border, prefix, m, c, rows):
    half = rows // 2
    lane = lax.broadcasted_iota(jnp.int32, (1, rows), 1)
    pos = jnp.where(lane < half, border[2 * c] * half + lane, border[2 * c + 1] * half + lane - half)
    return jnp.maximum(pos, prefix[m] - 1)


def key_positions(border, block, half):
    return border[block] * half + lax.broadcasted_iota(jnp.int32, (half, 1), 0)


def vmem_specs(k):
    return [pl.BlockSpec(memory_space=pltpu.VMEM)] * k


def pack_weights(qkv_weight, out_weight, up_weight, down_weight, ln_gains, ln_shifts):
    turned = jnp.swapaxes(qkv_weight, 1, 2)
    pad = jnp.zeros((64, turned.shape[2]), BF16)
    wp = jnp.concatenate([turned[0], pad, turned[1], turned[2]], axis=0)
    pad = jnp.zeros((64, out_weight.shape[1]), BF16)
    wo = jnp.concatenate([out_weight[64:], pad, out_weight[:64]], axis=0)
    ln = jnp.concatenate([ln_gains, ln_shifts], axis=0).astype(F32)
    ln = jnp.pad(ln, ((0, 4), (0, 0)))
    gather = functools.partial(lax.all_gather, axis_name="dp", tiled=True)
    return [
        gather(wp, axis=1)[None], gather(wo, axis=1)[None], gather(up_weight, axis=0),
        gather(down_weight, axis=1)[None], gather(ln, axis=1)[None],
    ]


def wide(ref_stack, fn):
    return jnp.concatenate([fn(ref_stack[i]) for i in range(ref_stack.shape[0])], axis=1)


def narrow(ref_stack, value, at=0, count=None):
    size = ref_stack.shape[2]
    span = pl.ds(at, ref_stack.shape[1] if count is None else count)
    total = dot_nt(value[:, 0:size], ref_stack[0, span, :])
    for i in range(1, ref_stack.shape[0]):
        total += dot_nt(value[:, i * size : (i + 1) * size], ref_stack[i, span, :])
    return total


def norm_back(dn, xhat, inv, gain):
    e = dn * gain
    return inv * (
        e - jnp.mean(e, axis=1, keepdims=True) - xhat * jnp.mean(e * xhat, axis=1, keepdims=True)
    )


def ln_row(ln, row):
    return jnp.concatenate([ln[i, row : row + 1, :] for i in range(ln.shape[0])], axis=1)


def column_sums(value):
    return jnp.sum(value, axis=0, keepdims=True)


class GradSum:
    def __init__(self, place, peer, own, out, from_up, from_mid, send, recv):
        self.p = place
        self.peer, self.own, self.from_dp, self.up = peer, own, out, own
        self.from_up, self.from_mid, self.out = from_up, from_mid, out
        self.send, self.recv = send, recv
        c, n = place.c, place.n
        low = c < n // 2
        self.toward = jnp.where(low, c + 1, c - 1)
        self.away = jnp.where(low, c - 1, c + 1)
        self.end = jnp.logical_or(c == 0, c == n - 1)
        self.inner = jnp.logical_or(c == n // 2 - 1, c == n // 2)

    def dp_copy(self):
        return remote(self.peer, self.from_dp, self.send.at[0], self.recv.at[0], dp=1 - self.p.d)

    def up_copy(self):
        return remote(self.up, self.from_up, self.send.at[1], self.recv.at[1], ctx=self.toward)

    def mid_copy(self):
        return remote(self.up, self.from_mid, self.send.at[2], self.recv.at[2], ctx=self.toward)

    def down_copy(self):
        return remote(self.out, self.out, self.send.at[3], self.recv.at[3], ctx=self.away)

    def s0(self):
        self.dp_copy().start()

    def s1(self):
        self.dp_copy().wait_recv()

        @pl.when(self.end)
        def _():
            self.up[...] = (self.own[...].astype(F32) + self.from_dp[...].astype(F32)).astype(BF16)

        @pl.when(jnp.logical_not(self.end))
        def _():
            self.up_copy().wait_recv()
            self.up[...] = (
                self.own[...].astype(F32) + self.from_dp[...].astype(F32)
                + self.from_up[...].astype(F32)
            ).astype(BF16)

        pl.when(self.inner)(lambda: self.mid_copy().start())
        pl.when(jnp.logical_not(self.inner))(lambda: self.up_copy().start())

    def s2(self):
        @pl.when(self.inner)
        def _():
            self.mid_copy().wait_recv()
            self.out[...] = (self.up[...].astype(F32) + self.from_mid[...].astype(F32)).astype(BF16)
            pl.when(jnp.logical_not(self.end))(lambda: self.down_copy().start())

    def s3(self):
        @pl.when(jnp.logical_not(self.inner))
        def _():
            self.down_copy().wait_recv()
            pl.when(jnp.logical_not(self.end))(lambda: self.down_copy().start())

    def drain(self):
        self.dp_copy().wait_send()
        pl.when(self.inner)(lambda: self.mid_copy().wait_send())
        pl.when(jnp.logical_not(self.inner))(lambda: self.up_copy().wait_send())
        pl.when(jnp.logical_not(self.end))(lambda: self.down_copy().wait_send())


class StatSum:
    def __init__(self, place, parts, from_dp, every, out, send, recv):
        self.p, self.parts, self.from_dp, self.every, self.out = place, parts, from_dp, every, out
        self.send, self.recv = send, recv

    def dp_copy(self):
        return remote(
            self.parts.at[1 - self.p.d], self.from_dp, self.send.at[0], self.recv.at[0],
            dp=1 - self.p.d,
        )

    def copy(self, owner, k):
        piece = self.every.at[owner]
        return remote(
            piece, piece, self.send.at[k], self.recv.at[k], ctx=lax.rem(self.p.c + k, self.p.n)
        )

    def s0(self):
        self.dp_copy().start()

    def s1(self):
        self.dp_copy().wait_recv()
        both = self.parts[self.p.d].astype(F32) + self.from_dp[...].astype(F32)
        self.every[self.p.c] = both.astype(BF16)
        for k in range(1, self.p.n):
            self.copy(self.p.c, k).start()

    def s2(self):
        for k in range(1, self.p.n):
            self.copy(lax.rem(self.p.c + self.p.n - k, self.p.n), k).wait_recv()
        total = self.every[0].astype(F32)
        for j in range(1, self.p.n):
            total += self.every[j].astype(F32)
        self.out[...] = total

    def drain(self):
        self.dp_copy().wait_send()
        for k in range(1, self.p.n):
            self.copy(self.p.c, k).wait_send()


EARLY_ROWS = 384
PACK_CUTS = ((0, 256, 0, 192), (256, 128, 192, 128), (384, 128, 320, 128), (512, 128, 448, 128))
A_SUM, N2_SUM, MLP_SUM, N1_SUM = 0, 2, 4, 6


def cuts_of(rows, most):
    at, cuts = 0, []
    while at < rows:
        size = min(most, rows - at)
        cuts.append((at, size))
        at += size
    return cuts


def block_kernel(n_ctx, exchange, prefix, border, hid_in, cot_in, *refs):
    if exchange:
        (qkv_s, out_s, up_s, down_s, gain_s, shift_s) = refs[:6]
        (block_out, grad_out, ga_out, gb_out, gs) = refs[6:11]
        (wp, wo, wu, wd, ln, grads, gb_buf, gs_buf, b_fu, b_fm, a_fu, a_fm, s_dp, s_all,
         hid, cot, block, grad_in, ga, gb, load, keep, wsend, wrecv, gsend, grecv, ssend,
         srecv) = refs[11:39]
        refs = refs[39:]
    else:
        hid, cot = hid_in, cot_in
        (wp, wo, wu, wd, ln) = refs[:5]
        (block, grad_in, grads, gb, gs) = refs[5:10]
        refs = refs[10:]
    (attn, heads, lse, o_t, qs, kv, h1, m_row, l_row, o_acc, act, d_mlp, d_up, h2, n2_tot, d_attn,
     sbuf, rbuf, q_all, do_all, st_all, qos, qor, acc, qh, doh, dq_t, delta, d_pack, stats, ks, kr, kvs, kvr,
     t_mine, t_out, t_in, t_sum, tsend, trecv) = refs
    p = Place(n_ctx)
    c, n = p.c, n_ctx
    micro, rows, width = hid.shape
    half = rows // 2
    ff = wu.shape[1]
    parts = 2 if exchange else 1
    cols = width // parts
    own_rows = width // parts
    tiles = rows // 128
    loads = []
    if exchange:
        spot = pl.ds(pl.multiple_of(p.d * cols, cols), cols)
        pairs = ((hid_in, hid), (cot_in, cot), (up_s, wu.at[spot]), (down_s, wd.at[p.d]))
        loads = [pltpu.make_async_copy(a, b, load.at[i]) for i, (a, b) in enumerate(pairs)]
        loads[0].start()
    p.barrier(exchange, True, True)

    size = half // 2

    def tp_sums(kind, m, total):
        pieces = []
        for q in range(2):
            i = 2 * (kind + m) + q
            pieces.append(TpSum(
                p, half, q * size, size, t_mine.at[i], t_out.at[i], t_in.at[i], t_sum.at[i], total,
                tsend.at[i], trecv.at[i],
            ))
        return pieces

    a_sums = [tp_sums(A_SUM, m, attn.at[m]) for m in range(micro)]
    n2_sums = [tp_sums(N2_SUM, m, n2_tot.at[m]) for m in range(micro)]
    mlp_sums = [tp_sums(MLP_SUM, m, block.at[m]) for m in range(micro)]
    n1_sums = [tp_sums(N1_SUM, m, n2_tot.at[m]) for m in range(micro)]

    def start_both(group, partial):
        for piece in group:
            piece.start_other(partial)
        for piece in group:
            piece.start_own(partial)

    def tile(i, base=0):
        return pl.ds(pl.multiple_of(base + i * 128, 128), 128)

    if exchange:
        mine = pl.ds(pl.multiple_of(p.d * own_rows, own_rows), own_rows)
        kv_part, q_part = wp.at[p.d, pl.ds(256, 384)], wp.at[p.d, pl.ds(0, 192)]
        places = (ln.at[p.d], kv_part, q_part, wo.at[p.d], wu.at[mine], wd.at[p.d])
        sources = (ln.at[p.d], kv_part, q_part, wo.at[p.d], up_s, down_s)

        def weight_copy(i):
            return remote(sources[i], places[i], wsend.at[i], wrecv.at[i], dp=1 - p.d)

        ln[p.d] = jnp.concatenate(
            [gain_s[...].astype(F32), shift_s[...].astype(F32), jnp.zeros((4, cols), F32)], axis=0
        )
        weight_copy(0).start()
        wp[p.d, 256:448, :] = qkv_s[1]
        wp[p.d, 448:640, :] = qkv_s[2]
        weight_copy(1).start()
        wp[p.d, 0:192, :] = qkv_s[0]
        for k in range(2):
            wp[k, 192:256, :] = jnp.zeros((64, cols), BF16)
        wo[p.d, 0:128, :] = out_s[64:192, :]
        wo[p.d, 128:192, :] = jnp.zeros((64, cols), BF16)
        wo[p.d, 192:256, :] = out_s[0:64, :]
        for piece in loads[1:]:
            piece.start()
        loads[0].wait()

    def weight_wait(*which):
        if exchange:
            for i in which:
                weight_copy(i).wait_recv()

    weight_wait(0)
    gain0, gain1, shift0, shift1 = (ln_row(ln, i) for i in range(4))
    for m in range(micro):
        @pl.loop(0, tiles)
        def _(i, m=m):
            xhat, _ = normalize(hid[m, tile(i), :].astype(F32))
            h1[tile(i, m * rows), :] = (xhat * gain0 + shift0).astype(BF16)

    def block_rows(b):
        return pl.ds(pl.multiple_of(b * half, half), half)

    def kv_copy(m, way, s, b):
        j, to = (c - s, c + 1) if way == 0 else (c + s, c - 1)
        piece = kv.at[m, j, block_rows(b)]
        return remote(piece, piece, ks.at[m, way, s, b], kr.at[m, way, s + 1, b], ctx=to)

    def kv_arrival(m, way, s, b):
        j, to = (c - s, c - 1) if way == 0 else (c + s, c + 1)
        piece = kv.at[m, j, block_rows(b)]
        return remote(piece, piece, ks.at[m, way, s, b], kr.at[m, way, s, b], ctx=to)

    def send_own(m, way):
        for b in range(2):
            kv_copy(m, way, 0, b).start()

    def has(way, s):
        return c - s >= 0 if way == 0 else c + s < n

    def sends(way, s):
        if way == 0:
            return jnp.logical_and(c - s >= 0, c + 1 < n)
        return jnp.logical_and(c + s < n, c - 1 >= 0)

    weight_wait(1)
    if exchange:
        weight_copy(2).start()
    for m in range(micro):
        @pl.loop(0, 2)
        def _(b, m=m):
            for i in range(tiles // 2):
                span = pl.ds(pl.multiple_of(b * half + i * 128, 128), 128)
                flat = pl.ds(pl.multiple_of(m * rows + b * half + i * 128, 128), 128)
                kv[m, c, span, :] = narrow(wp, h1[flat, :], 256, 384).astype(BF16)
            if m == 0:
                for way in range(2):
                    pl.when(sends(way, 0))(lambda way=way: kv_copy(0, way, 0, b).start())

    pl.when(c == 0)(lambda: send_own(1, 0))
    pl.when(c == n - 1)(lambda: send_own(1, 1))
    weight_wait(2)
    for piece in loads[1:]:
        piece.wait()
    if exchange:
        for i in range(3, 6):
            weight_copy(i).start()
    for m in range(micro):
        @pl.loop(0, tiles)
        def _(i, m=m):
            q = narrow(wp, h1[tile(i, m * rows), :], 0, 256).astype(BF16).astype(F32)
            qs[m, tile(i), :] = (q * HEAD_DIM ** (-0.5)).astype(BF16)

    lanes = lax.broadcasted_iota(jnp.int32, (rows, 128), 1)

    def halves(value):
        zero = jnp.zeros_like(value)
        return jnp.where(lanes < 64, value, zero), jnp.where(lanes < 64, zero, value)

    def split_queries(m):
        qh[0], qh[1] = halves(qs[m, :, 0:128])
        qh[2] = qs[m, :, 128:256]

    def attend(m, j, b, limits):
        span = block_rows(b)
        k01 = kv[m, j, span, 0:128]
        k2v0 = kv[m, j, span, 128:256]
        t0 = k2v0.T
        t12 = kv[m, j, span, 256:384].T
        allowed = key_positions(border, 2 * j + b, half) <= limits
        for h in range(3):
            scores = dot_nt(k2v0 if h == 2 else k01, qh[h])
            scores = jnp.where(allowed, scores, NEG)
            old = m_row[h]
            top = jnp.maximum(old, jnp.max(scores, axis=0, keepdims=True))
            prob = jnp.exp(scores - top)
            fade = jnp.exp(old - top)
            m_row[h] = top
            l_row[h] = l_row[h] * fade + jnp.sum(prob, axis=0, keepdims=True)
            v_t = t0[64:128] if h == 0 else t12[(h - 1) * 64 : h * 64]
            o_acc[h] = o_acc[h] * fade + dot_nn(v_t, prob.astype(BF16))

    steps = 4 * (n - 1) + 2

    def at_step(t, at, jobs):
        @pl.when(t == at)
        def _():
            for job in jobs:
                job()

    def forward(m, side):
        limits = query_limits(border, prefix, m, c, rows)
        split_queries(m)
        m_row[...] = jnp.full(m_row.shape, NEG, F32)
        l_row[...] = jnp.zeros(l_row.shape, F32)
        o_acc[...] = jnp.zeros(o_acc.shape, F32)

        @pl.loop(0, steps)
        def _(t):
            own = t < 2
            s = jnp.where(own, 0, lax.div(t + 2, 4))
            b = jnp.where(own, t, lax.rem(lax.div(t, 2) + 1, 2))
            right = jnp.logical_and(jnp.logical_not(own), lax.rem(t, 2) == 0)
            left = jnp.logical_and(jnp.logical_not(own), lax.rem(t, 2) == 1)

            def arrive(way):
                kv_arrival(m, way, s, b).wait_recv()
                pl.when(sends(way, s))(lambda: kv_copy(m, way, s, b).start())
                if m == 0:
                    last = c if way == 0 else n - 1 - c
                    ready = jnp.logical_and(jnp.logical_and(s == last, b == 1), sends(way, 0))
                    pl.when(ready)(lambda: send_own(1, way))

            pl.when(jnp.logical_and(right, has(0, s)))(lambda: arrive(0))
            pl.when(jnp.logical_and(left, has(1, s)))(lambda: arrive(1))
            j = jnp.where(right, c - s, c + s)

            @pl.when(jnp.logical_and(j >= 0, j < n))
            def _():
                attend(m, j, b, limits)

            for at, jobs in side:
                at_step(t, at, jobs)

        flat = pl.ds(m * rows, rows)
        dq_t[128:192, :] = jnp.zeros((64, rows), F32)
        for h in range(3):
            norm = o_acc[h] / l_row[h]
            o_t[m, h] = norm
            lse[m, h : h + 1, :] = m_row[h] + jnp.log(l_row[h])
            at = 192 if h == 0 else (h - 1) * 64
            dq_t[at : at + 64, :] = norm
        heads[flat, :] = dq_t[...].T.astype(BF16)
        if m == 0:
            weight_wait(3)
        start_both(
            a_sums[m],
            lambda span: wide(wo, lambda w: dot_nn(heads[pl.ds(m * rows + span.start, size), :], w)),
        )

    def middle(m, i):
        return hid[m, tile(i), :].astype(F32) + BRANCH * attn[m, tile(i), :].astype(F32)

    def mlp_tiles(m, q):
        @pl.loop(0, 2)
        def _(core):
            i = q + (tiles // 2) * core
            flat = tile(i, m * rows)
            xhat, _ = normalize(middle(m, i))
            normed = (xhat * gain1 + shift1).astype(BF16)
            h2[flat, :] = normed
            up = dot_nn(normed, wu[...])
            active = gelu_value(up).astype(BF16)
            act[flat, :] = active
            down_grad = (BRANCH * cot[m, tile(i), :].astype(F32)).astype(BF16)
            d_mlp[flat, :] = down_grad
            d_up[flat, :] = (narrow(wd, down_grad) * gelu_slope(up)).astype(BF16)
            block[m, tile(i), :] = wide(wd, lambda w: dot_nn(active, w)).astype(BF16)

        n2_sums[m][q].start(
            lambda span: dot_nt(d_up[pl.ds(m * rows + span.start, size), :], wu[...])
        )

    def mlp_start(m):
        start_both(mlp_sums[m], lambda span: block[m, span, :])

    def middle_gradient(m, q):
        n2_sums[m][q].finish()

        @pl.loop(0, 2)
        def _(core):
            i = q + (tiles // 2) * core
            xhat, inv = normalize(middle(m, i))
            dn = n2_tot[m, tile(i), :].astype(F32)
            grad = cot[m, tile(i), :].astype(F32) + norm_back(dn, xhat, inv, gain1)
            grad_in[m, tile(i), :] = grad
            d_attn[tile(i, m * rows), :] = (BRANCH * grad).astype(BF16)
            stats[1:2, :] += column_sums(dn * xhat)
            stats[3:4, :] += column_sums(dn)

    def write_block(m):
        for piece in mlp_sums[m]:
            piece.finish()
            piece.drain()

        @pl.loop(0, tiles)
        def _(i):
            out = middle(m, i) + BRANCH * block[m, tile(i), :].astype(F32)
            block[m, tile(i), :] = out.astype(BF16)

    def down_gradient():
        @pl.loop(0, ff // 256)
        def _(i):
            to = pl.ds(pl.multiple_of(i * 256, 256), 256)
            left = act[:, to]
            for k in range(parts):
                grads[k, to, :] = dot_tn(left, d_mlp[:, k * cols : (k + 1) * cols]).astype(BF16)

    def up_gradient():
        for k in range(parts):
            @pl.loop(0, own_rows // 128)
            def _(i, k=k):
                value = dot_tn(h2[:, tile(i, k * own_rows)], d_up[...]).astype(BF16)
                for q in range(ff // cols):
                    grads[k, tile(i, ff + q * own_rows), :] = value[:, q * cols : (q + 1) * cols]

    def out_gradient():
        at = ff + own_rows * (ff // cols)
        for k in range(parts):
            value = dot_tn(heads[...], d_attn[:, k * cols : (k + 1) * cols]).astype(BF16)
            grads[k, at : at + 128, :] = value[0:128]
            grads[k, at + 128 : at + 192, :] = value[192:256]

    early, late, norms = [], [], None
    stores = []

    def store(source, to, *index):
        if exchange:
            piece = pltpu.make_async_copy(source.at[index], to.at[index], keep.at[len(stores)])
            piece.start()
            stores.append(piece)

    if exchange:
        for i, (at, count) in enumerate(cuts_of(grads.shape[1], EARLY_ROWS)):
            cut = pl.ds(at, count)
            early.append(GradSum(
                p, grads.at[1 - p.d, cut], grads.at[p.d, cut], ga.at[cut], a_fu.at[cut],
                a_fm.at[cut], gsend.at[i], grecv.at[i],
            ))
        for i, (_, _, to, count) in enumerate(PACK_CUTS):
            cut, k = pl.ds(to, count), len(early) + i
            late.append(GradSum(
                p, gb_buf.at[1 - p.d, cut], gb_buf.at[p.d, cut], gb.at[cut], b_fu.at[cut],
                b_fm.at[cut], gsend.at[k], grecv.at[k],
            ))
        norms = StatSum(p, gs_buf, s_dp, s_all, gs, ssend, srecv)

    def stage(group, name):
        return [getattr(piece, name) for piece in group]

    def dkv_message(way, j, b, to):
        return remote(
            sbuf.at[j, block_rows(b)], rbuf.at[j + 1 - way, block_rows(b)],
            kvs.at[way, j, b], kvr.at[way, j, b], ctx=to,
        )

    def dkv_copy(way, j, b):
        return dkv_message(way, j, b, c + 1 if way == 0 else c - 1)

    def dkv_landed(way, j, b):
        return dkv_message(way, j, b, c - 1 if way == 0 else c + 1)

    gathered = (q_all, do_all, st_all)

    def qo_copy(kind, way, s):
        j, to = (c - s, c + 1) if way == 0 else (c + s, c - 1)
        piece = gathered[kind].at[j]
        return remote(piece, piece, qos.at[kind, way, s], qor.at[kind, way, s + 1], ctx=to)

    def qo_arrival(kind, way, s):
        j, to = (c - s, c - 1) if way == 0 else (c + s, c + 1)
        piece = gathered[kind].at[j]
        return remote(piece, piece, qos.at[kind, way, s], qor.at[kind, way, s], ctx=to)

    def qo_send(kind):
        for way in range(2):
            pl.when(sends(way, 0))(lambda way=way: qo_copy(kind, way, 0).start())

    def qo_step(kind, way, s):
        @pl.when(has(way, s))
        def _():
            qo_arrival(kind, way, s).wait_recv()
            pl.when(sends(way, s))(lambda: qo_copy(kind, way, s).start())

    def qo_steps(kind, s):
        for way in range(2):
            qo_step(kind, way, s)

    def send_queries(m):
        q_all[c] = qs[m].T[0:192]
        qo_send(0)

    def upstream(way):
        return c > 0 if way == 0 else c < n - 1

    def attend_back(m, j, b, limits, keys_too=True):
        span = block_rows(b)
        k01 = kv[m, j, span, 0:128]
        k2v0 = kv[m, j, span, 128:256]
        v12 = kv[m, j, span, 256:384]
        t01 = k01.T
        t2 = k2v0.T
        allowed = key_positions(border, 2 * j + b, half) <= limits
        sums = {}
        for h in range(3):
            scores = dot_nt(k2v0 if h == 2 else k01, qh[h])
            prob = jnp.exp(jnp.where(allowed, scores, NEG) - lse[m, h : h + 1, :])
            d_prob = dot_nt(k2v0 if h == 0 else v12, doh[h])
            d_scores = (prob * (d_prob - delta[h])).astype(BF16)
            k_t = t2[0:64] if h == 2 else t01[h * 64 : (h + 1) * 64]
            dq_t[h * 64 : (h + 1) * 64, :] += dot_nn(k_t, d_scores)
            if keys_too:
                dk = dot_nn(d_scores, qh[h])
                dv = dot_nn(prob.astype(BF16), doh[h])
                k_at, v_at = (1 if h == 2 else 0), (1 if h == 0 else 2)
                sums[k_at] = dk if k_at not in sums else sums[k_at] + dk
                sums[v_at] = dv if v_at not in sums else sums[v_at] + dv
        for k in sums:
            acc[span, k * 128 : (k + 1) * 128] = sums[k]

    def attend_keys(m, j, b):
        span = block_rows(b)
        k01 = kv[m, c, span, 0:128]
        k2v0 = kv[m, c, span, 128:256]
        v12 = kv[m, c, span, 256:384]
        limits = query_limits(border, prefix, m, j, rows)
        allowed = key_positions(border, 2 * c + b, half) <= limits
        zero = jnp.zeros((64, rows), BF16)
        for h in range(3):
            q_h = q_all[j, h * 64 : (h + 1) * 64, :]
            q_h = jnp.concatenate([zero, q_h] if h == 1 else [q_h, zero], axis=0)
            do_h = do_all[j, h * 64 : (h + 1) * 64, :]
            do_h = jnp.concatenate([do_h, zero] if h == 1 else [zero, do_h], axis=0)
            scores = dot_nn(k2v0 if h == 2 else k01, q_h)
            prob = jnp.exp(jnp.where(allowed, scores, NEG) - st_all[j, h : h + 1, :])
            d_prob = dot_nn(k2v0 if h == 0 else v12, do_h)
            d_scores = (prob * (d_prob - st_all[j, 3 + h : 4 + h, :])).astype(BF16)
            k_at, v_at = (128 if h == 2 else 0), (128 if h == 0 else 256)
            acc[span, k_at : k_at + 128] += dot_nt(d_scores, q_h)
            acc[span, v_at : v_at + 128] += dot_nt(prob.astype(BF16), do_h)

    def head_gradients(m):
        upper = d_attn[pl.ds(m * rows, rows), :]
        share = wo.shape[2]
        d_heads_t = dot_nt(wo[0], upper[:, 0:share])
        for i in range(1, wo.shape[0]):
            d_heads_t += dot_nt(wo[i], upper[:, i * share : (i + 1) * share])
        for h in range(3):
            at = 192 if h == 0 else (h - 1) * 64
            delta[h] = jnp.sum(d_heads_t[at : at + 64] * o_t[m, h], axis=0, keepdims=True)
            if m > 0:
                do_all[c, h * 64 : (h + 1) * 64, :] = d_heads_t[at : at + 64].astype(BF16)
                st_all[c, h : h + 1, :] = lse[m, h : h + 1, :]
                st_all[c, 3 + h : 4 + h, :] = delta[h]
        if m > 0:
            st_all[c, 6:8, :] = jnp.zeros((2, rows), F32)
            qo_send(2)
            qo_send(1)
        d_heads = narrow(wo, upper).astype(BF16)
        doh[0] = d_heads[:, 128:256]
        doh[1], doh[2] = halves(d_heads[:, 0:128])
        split_queries(m)
        dq_t[...] = jnp.zeros(dq_t.shape, F32)

    def query_gradient(m):
        flat = pl.ds(m * rows, rows)
        d_pack[flat, 0:256] = (dq_t[...].T * HEAD_DIM ** (-0.5)).astype(BF16)

    def backward_end(m):
        d_pack[pl.ds(m * rows, rows), 256:640] = acc[...].astype(BF16)
        start_both(
            n1_sums[m],
            lambda span: wide(wp, lambda w: dot_nn(d_pack[pl.ds(m * rows + span.start, size), :], w)),
        )

    def backward(m, side):
        limits = query_limits(border, prefix, m, c, rows)
        head_gradients(m)

        @pl.loop(0, steps)
        def _(t):
            own = t >= steps - 2
            s = n - 1 - lax.div(t, 4)
            b = jnp.where(own, t - (steps - 2), lax.rem(lax.div(t, 2), 2))
            right = jnp.logical_and(lax.rem(t, 2) == 0, jnp.logical_not(own))
            left = jnp.logical_and(lax.rem(t, 2) == 1, jnp.logical_not(own))
            j = jnp.where(own, c, jnp.where(right, c + s, c - s))
            span = block_rows(b)

            for at, jobs in side:
                at_step(t, at, jobs)

            @pl.when(jnp.logical_and(j >= 0, j < n))
            def _():
                attend_back(m, j, b, limits)

                def pass_on(way):
                    @pl.when(upstream(way))
                    def _():
                        dkv_landed(way, j, b).wait_recv()
                        sbuf[j, span, :] = (
                            acc[span, :] + rbuf[j + 1 - way, span, :].astype(F32)
                        ).astype(BF16)

                    @pl.when(jnp.logical_not(upstream(way)))
                    def _():
                        sbuf[j, span, :] = acc[span, :].astype(BF16)

                    dkv_copy(way, j, b).start()

                pl.when(right)(lambda: pass_on(0))
                pl.when(left)(lambda: pass_on(1))

        for way in range(2):
            @pl.when(upstream(way))
            def _(way=way):
                for b in range(2):
                    span = block_rows(b)
                    dkv_landed(way, c, b).wait_recv()
                    acc[span, :] += rbuf[c + 1 - way, span, :].astype(F32)

        query_gradient(m)
        backward_end(m)

    def backward_last(m, side, between, side_keys):
        limits = query_limits(border, prefix, m, c, rows)
        head_gradients(m)

        @pl.loop(0, 2)
        def _(b):
            attend_back(m, c, b, limits)

        @pl.loop(0, 2 * (n - 1))
        def _(t):
            j = lax.rem(c + 1 + lax.div(t, 2), n)
            attend_back(m, j, lax.rem(t, 2), limits, keys_too=False)
            for at, jobs in side:
                at_step(t, at, jobs)

        query_gradient(m)
        do(between)

        @pl.loop(0, 2 * (n - 1))
        def _(t):
            s = 1 + lax.div(t, 2)
            for way in range(2):
                @pl.when(jnp.logical_and(lax.rem(t, 2) == way, has(way, s)))
                def _(way=way):
                    pl.when(s > 2)(lambda: qo_step(2, way, s))
                    pl.when(s > 2)(lambda: qo_step(1, way, s))
                    for b in range(2):
                        attend_keys(m, c - s if way == 0 else c + s, b)
            for at, jobs in side_keys:
                at_step(t, at, jobs)

        backward_end(m)

    def finish_rows(m, q):
        n1_sums[m][q].finish()

        @pl.loop(0, 2)
        def _(core):
            i = q + (tiles // 2) * core
            xhat, inv = normalize(hid[m, tile(i), :].astype(F32))
            dn = n2_tot[m, tile(i), :].astype(F32)
            grad_in[m, tile(i), :] += norm_back(dn, xhat, inv, gain0)
            stats[0:1, :] += column_sums(dn * xhat)
            stats[2:3, :] += column_sums(dn)

    def pack_part(to, k, at, count, first, kept):
        left = h1[:, pl.ds(pl.multiple_of(k * cols, 128), cols)]
        value = dot_tn(d_pack[:, at : at + count], left)
        to[first : first + kept, :] = value[0:kept].astype(to.dtype)

    def do(jobs):
        for job in jobs:
            job()

    def each(group, name):
        return lambda: do(stage(group, name))

    def middle_ready(m):
        for q in range(2):
            middle_gradient(m, q)
        for piece in n2_sums[m]:
            piece.drain()

    def mlp_piece(m, q):
        a_sums[m][q].finish()
        mlp_tiles(m, q)

    def by_place(at_end, inside):
        return jnp.where(jnp.logical_or(c == 0, c == n - 1), at_end, inside)

    stats[...] = jnp.zeros(stats.shape, F32)
    (a0, a1), (x0, x1), (u0, u1), (y0, y1) = a_sums, n2_sums, mlp_sums, n1_sums
    forward(0, [])
    forward(1, [
        (0, [each(a0, "step2")]),
        (3, [a0[0].step3]),
        (4, [
            lambda: weight_wait(4, 5), lambda: mlp_piece(0, 0), a0[1].step3, x0[0].step2,
            lambda: mlp_piece(0, 1),
        ]),
        (5, [x0[1].step2]),
    ])
    do(stage(x0, "step3"))
    do(stage(a1, "step2"))
    middle_ready(0)
    spot = by_place(5, 0)
    send_queries(1)
    backward(0, [
        (2, [lambda: qo_steps(0, 1)]),
        (spot, [a1[0].step3, a1[1].step3, lambda: mlp_piece(1, 0), lambda: mlp_piece(1, 1)]),
        (6, [lambda: qo_steps(0, 2)]),
        (spot + 2, [each(x1, "step2"), lambda: mlp_start(0)]),
        (spot + 4, [down_gradient, each(early[0:2], "s0")]),
        (spot + 6, [up_gradient, each(early[2:-1], "s0"), each(u0, "step2"), each(x1, "step3")]),
        (steps - 1, [lambda: mlp_start(1)] + [lambda s=s: qo_steps(0, s) for s in range(3, n)]),
    ])
    def at_place(ends, jobs):
        @pl.when(by_place(1, 0) == ends)
        def _():
            do(jobs)

    at_place(1, stage(early[0:1], "s1"))
    middle_ready(1)
    query_pieces = []
    if exchange:
        def query_piece():
            pack_part(gb_buf.at[1 - p.d], 1 - p.d, *PACK_CUTS[0])
            late[0].s0()
            pack_part(gb_buf.at[p.d], p.d, *PACK_CUTS[0])

        query_pieces = [query_piece]
    backward_last(1, [
        (0, [out_gradient, each(early[-1:], "s0"), each(y0, "step2")]),
        (by_place(0, 5), [each(early[1:2], "s1")]),
        (2, [lambda: qo_steps(2, 1), lambda: qo_steps(1, 1)]),
        (by_place(9, 3), [each(early[0:1], "s1")]),
        (5, [lambda: qo_steps(2, 2), lambda: qo_steps(1, 2)]),
        (by_place(4, 9), [each(early[2:3], "s1")]),
    ], query_pieces, [
        (by_place(0, 9), [each(early[3:4], "s1")]),
        (0, [each(early[0:1], "s2")]),
        (1, [each(y0, "step3"), each(u0, "step3")]),
        (by_place(9, 2), [each(early[2:3], "s1")]),
        (by_place(2, 9), [each(early[4:5], "s1")]),
        (3, [each(u1, "step2"), each(early[1:2], "s2")]),
        (by_place(9, 5), [each(early[3:4], "s1")]),
    ])
    if exchange:
        for piece, cut in zip(late[1:], PACK_CUTS[1:]):
            pack_part(gb_buf.at[1 - p.d], 1 - p.d, *cut)
            piece.s0()
        for cut in PACK_CUTS[1:]:
            pack_part(gb_buf.at[p.d], p.d, *cut)
    else:
        for cut in PACK_CUTS:
            pack_part(gb, 0, *cut)
    do(stage(y1, "step2"))
    if exchange:
        at_place(1, stage(late[0:1], "s1"))
        at_place(0, stage(early[2:3], "s2"))
    for q in range(2):
        finish_rows(0, q)
    store(grad_in, grad_out if exchange else None, 0)
    if exchange:
        at_place(1, stage(late[1:3], "s1"))
        at_place(0, stage(early[4:5] + late[0:1], "s1"))
    do(stage(u1, "step3"))
    write_block(0)
    store(block, block_out if exchange else None, 0)
    if exchange:
        at_place(1, stage(late[3:], "s1"))
        at_place(0, stage(late[1:2], "s1") + stage(early[3:4], "s2"))
    for q in range(2):
        y1[q].step3()
    for q in range(2):
        finish_rows(1, q)
    store(grad_in, grad_out if exchange else None, 1)
    if exchange:
        for k in range(2):
            cut = slice(k * cols, (k + 1) * cols)
            gs_buf[k] = jnp.concatenate([stats[:, cut], jnp.zeros((8, cols), F32)], axis=0).astype(BF16)
        norms.s0()
        at_place(0, stage(early[4:5], "s2") + stage(late[2:], "s1") + stage(late[0:1], "s2"))
    write_block(1)
    store(block, block_out if exchange else None, 1)
    if exchange:
        norms.s1()
        at_place(0, stage(late[1:], "s2"))
        for group, held, to, cuts in (
            (early, ga, ga_out, cuts_of(ga.shape[0], EARLY_ROWS)),
            (late, gb, gb_out, [cut[2:] for cut in PACK_CUTS]),
        ):
            for piece, (at, count) in zip(group, cuts):
                piece.s3()
                store(held, to, pl.ds(at, count))
        norms.s2()
        for piece in early + late + [norms]:
            piece.drain()
        for piece in stores:
            piece.wait()
        for i in range(6):
            weight_copy(i).wait_send()
    else:
        gs[...] = stats[...]
    for b in range(2):
        for m in range(micro):
            for way in range(2):
                for s in range(n - 1):
                    pl.when(sends(way, s))(
                        lambda m=m, way=way, s=s, b=b: kv_copy(m, way, s, b).wait_send()
                    )
        for j in range(n):
            pl.when(c < j)(lambda j=j, b=b: dkv_copy(0, j, b).wait_send())
            pl.when(c > j)(lambda j=j, b=b: dkv_copy(1, j, b).wait_send())
    for kind in range(3):
        for way in range(2):
            for s in range(n - 1):
                pl.when(sends(way, s))(
                    lambda kind=kind, way=way, s=s: qo_copy(kind, way, s).wait_send()
                )
    for piece in a0 + a1 + y0 + y1:
        piece.drain()


def run_block(n_ctx, exchange, prefix, border, hid, cot, weights, ff):
    micro, rows, width = hid.shape
    half = rows // 2
    total = micro * rows
    parts = 2 if exchange else 1
    cols = width // parts
    sds = jax.ShapeDtypeStruct
    vmem = pltpu.VMEM
    sems = pltpu.SemaphoreType.DMA
    grad_rows = ff + cols * (ff // cols) + 192
    outs = [sds((micro, rows, width), BF16), sds((micro, rows, width), F32)]
    scratch = []
    if exchange:
        outs += [sds((grad_rows, cols), BF16), sds((576, cols), BF16), sds((16, cols), F32)]
        pieces = len(cuts_of(grad_rows, EARLY_ROWS)) + len(PACK_CUTS)
        scratch += [
            vmem((2, 640, cols), BF16), vmem((2, 256, cols), BF16), vmem((width, ff), BF16),
            vmem((2, ff, cols), BF16), vmem((2, 8, cols), F32),
            vmem((2, grad_rows, cols), BF16), vmem((2, 576, cols), BF16), vmem((2, 16, cols), BF16),
            vmem((576, cols), BF16), vmem((576, cols), BF16),
            vmem((grad_rows, cols), BF16), vmem((grad_rows, cols), BF16),
            vmem((16, cols), BF16), vmem((n_ctx, 16, cols), BF16),
            vmem(hid.shape, BF16), vmem(hid.shape, BF16), vmem(hid.shape, BF16), vmem(hid.shape, F32),
            vmem((grad_rows, cols), BF16), vmem((576, cols), BF16), sems((4,)),
            sems((2 * micro + pieces,)),
            sems((6,)), sems((6,)), sems((pieces, 4)), sems((pieces, 4)),
            sems((n_ctx,)), sems((n_ctx,)),
        ]
    else:
        outs += [
            sds((1, grad_rows, cols), BF16), sds((576, width), F32), sds((8, width), F32)
        ]
    scratch += [
        vmem((micro, rows, width), BF16), vmem((total, 256), BF16), vmem((micro, 8, rows), F32),
        vmem((micro, 3, 64, rows), F32), vmem((micro, rows, 256), BF16),
        vmem((micro, n_ctx, rows, 384), BF16), vmem((total, width), BF16),
        vmem((3, 1, rows), F32), vmem((3, 1, rows), F32), vmem((3, 64, rows), F32),
        vmem((total, ff), BF16), vmem((total, width), BF16), vmem((total, ff), BF16),
        vmem((total, width), BF16), vmem((micro, rows, width), BF16), vmem((total, width), BF16),
        vmem((n_ctx, rows, 384), BF16), vmem((n_ctx + 1, rows, 384), BF16),
        vmem((n_ctx, 192, rows), BF16), vmem((n_ctx, 192, rows), BF16), vmem((n_ctx, 8, rows), F32),
        sems((3, 2, n_ctx + 1)), sems((3, 2, n_ctx + 1)),
        vmem((rows, 384), F32), vmem((3, rows, 128), BF16), vmem((3, rows, 128), BF16),
        vmem((256, rows), F32), vmem((3, 1, rows), F32), vmem((total, 640), BF16),
        vmem((8, width), F32),
        sems((micro, 2, n_ctx + 1, 2)), sems((micro, 2, n_ctx + 1, 2)),
        sems((2, n_ctx, 2)), sems((2, n_ctx, 2)),
    ]
    scratch += [vmem((16, half // 2, width), BF16)] * 4 + [sems((16, 3))] * 2
    smem = pl.BlockSpec(memory_space=pltpu.SMEM)
    stay = pl.BlockSpec(memory_space=pl.ANY)
    specs = vmem_specs(2 + len(weights))
    if exchange:
        specs = [stay, stay] + vmem_specs(2) + [stay, stay] + vmem_specs(2)
    return pl.pallas_call(
        functools.partial(block_kernel, n_ctx, exchange),
        out_shape=outs,
        in_specs=[smem, smem] + specs,
        out_specs=([stay] * 4 + vmem_specs(1)) if exchange else vmem_specs(len(outs)),
        scratch_shapes=scratch,
        compiler_params=pltpu.CompilerParams(
            collective_id=0, has_side_effects=True, vmem_limit_bytes=67043328
        ),
        name="block_both_ways",
    )(prefix, border, hid, cot, *weights)


def unpack_kernel(
    block_in, grad_in, down_in, left_in, right_in, out_in, qkv_in, gs,
    block, grad, down, up, qkv, out, gains, shifts,
):
    cols = down_in.shape[1]
    block[...] = block_in[...]
    grad[...] = grad_in[...]
    down[...] = down_in[...].astype(F32)
    up[:, 0:cols] = left_in[...].astype(F32)
    up[:, cols : 2 * cols] = right_in[...].astype(F32)
    qkv[...] = qkv_in[...].astype(F32)

    @pl.when(pl.program_id(0) == 0)
    def _():
        out[0:64, :] = out_in[128:192, :].astype(F32)
        out[64:192, :] = out_in[0:128, :].astype(F32)
        gains[...] = gs[0:2]
        shifts[...] = gs[2:4]


UNPACK_STEPS = 4


def unpack(block, grad_in, ga, gb, gs, ff):
    cols = ga.shape[1]
    d, u, q = ff // UNPACK_STEPS, cols // UNPACK_STEPS, gb.shape[0] // UNPACK_STEPS
    total, width = block.shape
    r = total // UNPACK_STEPS
    sds = jax.ShapeDtypeStruct

    def rows(count, wide_by, first=0):
        return pl.BlockSpec((count, wide_by), lambda i: (first + i, 0))

    def whole(*shape, at=0):
        return pl.BlockSpec(shape, lambda i: (at, 0))

    return pl.pallas_call(
        unpack_kernel,
        grid=(UNPACK_STEPS,),
        out_shape=[
            sds((total, width), BF16), sds((total, width), F32), sds((ff, cols), F32),
            sds((cols, 2 * cols), F32), sds(gb.shape, F32), sds((192, cols), F32),
            sds((2, cols), F32), sds((2, cols), F32),
        ],
        in_specs=[
            rows(r, width), rows(r, width), rows(d, cols), rows(u, cols, ff // u),
            rows(u, cols, (ff + cols) // u), whole(192, cols, at=(ff + 2 * cols) // 192), rows(q, cols),
            whole(*gs.shape),
        ],
        out_specs=[
            rows(r, width), rows(r, width), rows(d, cols), rows(u, 2 * cols), rows(q, cols),
            whole(192, cols), whole(2, cols), whole(2, cols),
        ],
        name="unpack_outputs",
    )(block, grad_in, ga, ga, ga, ga, gb, gs)


def body(
    hidden_in, prefix, block_order, qkv_weight, out_weight, up_weight, down_weight, ln_gains,
    ln_shifts, cotangent,
):
    micro, _, tokens, width = hidden_in.shape
    n_ctx = lax.axis_size("ctx")
    exchange = lax.axis_size("dp") == 2 and n_ctx % 2 == 0
    ff = up_weight.shape[1]
    params = (qkv_weight, out_weight, up_weight, down_weight, ln_gains, ln_shifts)
    turned = jnp.swapaxes(qkv_weight, 1, 2)
    weights = (turned,) + params[1:] if exchange else pack_weights(*params)
    hid, cot = hidden_in[:, 0], cotangent[:, 0]
    block, grad_in, ga, gb, gs = run_block(
        n_ctx, exchange, prefix[:, 0], block_order, hid, cot, weights, ff
    )
    if exchange:
        total = micro * tokens
        block, grad_in, g_down, g_up, g_qkv, g_out, g_gains, g_shifts = unpack(
            block.reshape(total, width), grad_in.reshape(total, width), ga, gb, gs, ff
        )
        shape = (micro, 1, tokens, width)
        g_qkv = jnp.swapaxes(g_qkv.reshape(turned.shape), 1, 2)
        return (
            block.reshape(shape), grad_in.reshape(shape), g_qkv, g_out, g_up, g_down, g_gains,
            g_shifts,
        )
    ga = ga[0].astype(F32)
    g_out = ga[ff + width :]
    whole = lax.psum(
        (
            jnp.swapaxes(gb.reshape(3, 192, -1), 1, 2),
            jnp.concatenate([g_out[128:], g_out[:128]], axis=0), ga[ff : ff + width], ga[:ff],
            gs[0:2], gs[2:4],
        ),
        "ctx",
    )
    owned = [
        lax.psum_scatter(v, "dp", scatter_dimension=d, tiled=True)
        for v, d in zip(whole, (1, 1, 0, 1, 1, 1))
    ]
    return (block[:, None], grad_in[:, None], *owned)


def solution(mesh):
    in_specs = (
        P(None, "dp", "ctx", None), P(None, "dp"), P(), P(None, "dp", "tp"), P("tp", "dp"),
        P("dp", "tp"), P("tp", "dp"), P(None, "dp"), P(None, "dp"), P(None, "dp", "ctx", None),
    )
    out_specs = (
        P(None, "dp", "ctx", None), P(None, "dp", "ctx", None), P(None, "dp", "tp"),
        P("tp", "dp"), P("dp", "tp"), P("tp", "dp"), P(None, "dp"), P(None, "dp"),
    )
    return jax.shard_map(body, mesh=mesh, in_specs=in_specs, out_specs=out_specs, check_vma=False)
```

```python
import functools

import jax
import jax.numpy as jnp
from jax import lax
from jax.experimental import pallas as pl
from jax.experimental.pallas import tpu as pltpu
from jax.sharding import PartitionSpec as P

HEAD_DIM = 64
DEPTH = 12
EPS = 1e-05
GELU_C = 0.7978845608028654
GELU_A = 0.044715
NEG = -1e30
BRANCH = DEPTH ** (-0.5)
MESH = pl.DeviceIdType.MESH
F32 = jnp.float32
BF16 = jnp.bfloat16


def gelu_value(u):
    return 0.5 * u * (1.0 + jnp.tanh(GELU_C * (u + GELU_A * u * u * u)))


def gelu_slope(u):
    inner = jnp.tanh(GELU_C * (u + GELU_A * u * u * u))
    return 0.5 * (1.0 + inner) + 0.5 * u * (1.0 - inner * inner) * GELU_C * (
        1.0 + 3.0 * GELU_A * u * u
    )


def normalize(x):
    centered = x - jnp.mean(x, axis=1, keepdims=True)
    inv = lax.rsqrt(jnp.mean(centered * centered, axis=1, keepdims=True) + EPS)
    return centered * inv, inv


def dot_nn(a, b):
    return lax.dot_general(a, b, (((1,), (0,)), ((), ())), preferred_element_type=F32)


def dot_nt(a, b):
    return lax.dot_general(a, b, (((1,), (1,)), ((), ())), preferred_element_type=F32)


def dot_tn(a, b):
    return lax.dot_general(a, b, (((0,), (0,)), ((), ())), preferred_element_type=F32)


def remote(src, dst, send, recv, **ids):
    return pltpu.make_async_remote_copy(
        src_ref=src, dst_ref=dst, send_sem=send, recv_sem=recv, device_id=ids, device_id_type=MESH
    )


class Place:
    def __init__(self, n_ctx):
        self.n = n_ctx
        self.c = lax.axis_index("ctx")
        self.d = lax.axis_index("dp")
        tp = lax.axis_index("tp")
        self.core = lax.rem(tp, 2)
        self.mate = tp + 1 - 2 * self.core
        chip = lax.div(tp, 2)
        self.across = (1 - chip) * 2 + self.core

    def barrier(self, dp, tp, ctx):
        sem = pltpu.get_barrier_semaphore()

        def hello(**ids):
            pl.semaphore_signal(sem, inc=1, device_id=ids, device_id_type=MESH)

        count = 0
        if dp:
            hello(dp=1 - self.d)
            count += 1
        if tp:
            hello(tp=self.mate)
            hello(tp=self.across)
            count += 2
        if ctx:
            for j in range(1, self.n):
                hello(ctx=lax.rem(self.c + j, self.n))
            count += self.n - 1
        pl.semaphore_wait(sem, count)


class TpSum:
    def __init__(self, place, half, first, size, mine, out_half, in_half, in_sum, total, send, recv):
        self.p, self.half, self.first, self.size = place, half, first, size
        self.mine, self.out_half, self.in_half = mine, out_half, in_half
        self.in_sum, self.total = in_sum, total
        self.send, self.recv = send, recv

    def rows(self, core):
        return pl.ds(pl.multiple_of(core * self.half + self.first, self.size), self.size)

    def c1(self):
        return remote(self.out_half, self.in_half, self.send.at[0], self.recv.at[0], tp=self.p.mate)

    def c2(self):
        return remote(self.mine, self.in_sum, self.send.at[1], self.recv.at[1], tp=self.p.across)

    def c3(self, core):
        part = self.total.at[self.rows(core)]
        return remote(part, part, self.send.at[2], self.recv.at[2], tp=self.p.mate)

    def start_other(self, partial):
        self.out_half[...] = partial(self.rows(1 - self.p.core)).astype(BF16)
        self.c1().start()

    def start_own(self, partial):
        self.mine[...] = partial(self.rows(self.p.core)).astype(BF16)

    def start(self, partial):
        self.start_other(partial)
        self.start_own(partial)

    def step2(self):
        self.c1().wait_recv()
        self.mine[...] = (self.mine[...].astype(F32) + self.in_half[...].astype(F32)).astype(BF16)
        self.c2().start()

    def step3(self):
        self.c2().wait_recv()
        both = self.mine[...].astype(F32) + self.in_sum[...].astype(F32)
        self.total[self.rows(self.p.core), :] = both.astype(BF16)
        self.c3(self.p.core).start()

    def finish(self):
        self.c3(1 - self.p.core).wait_recv()

    def drain(self):
        self.c1().wait_send()
        self.c2().wait_send()
        self.c3(self.p.core).wait_send()


def query_limits(border, prefix, m, c, rows):
    half = rows // 2
    lane = lax.broadcasted_iota(jnp.int32, (1, rows), 1)
    pos = jnp.where(lane < half, border[2 * c] * half + lane, border[2 * c + 1] * half + lane - half)
    return jnp.maximum(pos, prefix[m] - 1)


def key_positions(border, block, half):
    return border[block] * half + lax.broadcasted_iota(jnp.int32, (half, 1), 0)


def vmem_specs(k):
    return [pl.BlockSpec(memory_space=pltpu.VMEM)] * k


def pack_weights(qkv_weight, out_weight, up_weight, down_weight, ln_gains, ln_shifts):
    turned = jnp.swapaxes(qkv_weight, 1, 2)
    pad = jnp.zeros((64, turned.shape[2]), BF16)
    wp = jnp.concatenate([turned[0], pad, turned[1], turned[2]], axis=0)
    pad = jnp.zeros((64, out_weight.shape[1]), BF16)
    wo = jnp.concatenate([out_weight[64:], pad, out_weight[:64]], axis=0)
    ln = jnp.concatenate([ln_gains, ln_shifts], axis=0).astype(F32)
    ln = jnp.pad(ln, ((0, 4), (0, 0)))
    gather = functools.partial(lax.all_gather, axis_name="dp", tiled=True)
    return [
        gather(wp, axis=1)[None], gather(wo, axis=1)[None], gather(up_weight, axis=0),
        gather(down_weight, axis=1)[None], gather(ln, axis=1)[None],
    ]


def wide(ref_stack, fn):
    return jnp.concatenate([fn(ref_stack[i]) for i in range(ref_stack.shape[0])], axis=1)


def narrow(ref_stack, value, at=0, count=None):
    size = ref_stack.shape[2]
    span = pl.ds(at, ref_stack.shape[1] if count is None else count)
    total = dot_nt(value[:, 0:size], ref_stack[0, span, :])
    for i in range(1, ref_stack.shape[0]):
        total += dot_nt(value[:, i * size : (i + 1) * size], ref_stack[i, span, :])
    return total


def norm_back(dn, xhat, inv, gain):
    e = dn * gain
    return inv * (
        e - jnp.mean(e, axis=1, keepdims=True) - xhat * jnp.mean(e * xhat, axis=1, keepdims=True)
    )


def ln_row(ln, row):
    return jnp.concatenate([ln[i, row : row + 1, :] for i in range(ln.shape[0])], axis=1)


def column_sums(value):
    return jnp.sum(value, axis=0, keepdims=True)


class GradSum:
    def __init__(self, place, peer, own, out, from_up, from_mid, send, recv):
        self.p = place
        self.peer, self.own, self.from_dp, self.up = peer, own, out, own
        self.from_up, self.from_mid, self.out = from_up, from_mid, out
        self.send, self.recv = send, recv
        c, n = place.c, place.n
        low = c < n // 2
        self.toward = jnp.where(low, c + 1, c - 1)
        self.away = jnp.where(low, c - 1, c + 1)
        self.end = jnp.logical_or(c == 0, c == n - 1)
        self.inner = jnp.logical_or(c == n // 2 - 1, c == n // 2)

    def dp_copy(self):
        return remote(self.peer, self.from_dp, self.send.at[0], self.recv.at[0], dp=1 - self.p.d)

    def up_copy(self):
        return remote(self.up, self.from_up, self.send.at[1], self.recv.at[1], ctx=self.toward)

    def mid_copy(self):
        return remote(self.up, self.from_mid, self.send.at[2], self.recv.at[2], ctx=self.toward)

    def down_copy(self):
        return remote(self.out, self.out, self.send.at[3], self.recv.at[3], ctx=self.away)

    def s0(self):
        self.dp_copy().start()

    def s1(self):
        self.dp_copy().wait_recv()

        @pl.when(self.end)
        def _():
            self.up[...] = (self.own[...].astype(F32) + self.from_dp[...].astype(F32)).astype(BF16)

        @pl.when(jnp.logical_not(self.end))
        def _():
            self.up_copy().wait_recv()
            self.up[...] = (
                self.own[...].astype(F32) + self.from_dp[...].astype(F32)
                + self.from_up[...].astype(F32)
            ).astype(BF16)

        pl.when(self.inner)(lambda: self.mid_copy().start())
        pl.when(jnp.logical_not(self.inner))(lambda: self.up_copy().start())

    def s2(self):
        @pl.when(self.inner)
        def _():
            self.mid_copy().wait_recv()
            self.out[...] = (self.up[...].astype(F32) + self.from_mid[...].astype(F32)).astype(BF16)
            pl.when(jnp.logical_not(self.end))(lambda: self.down_copy().start())

    def s3(self):
        @pl.when(jnp.logical_not(self.inner))
        def _():
            self.down_copy().wait_recv()
            pl.when(jnp.logical_not(self.end))(lambda: self.down_copy().start())

    def drain(self):
        self.dp_copy().wait_send()
        pl.when(self.inner)(lambda: self.mid_copy().wait_send())
        pl.when(jnp.logical_not(self.inner))(lambda: self.up_copy().wait_send())
        pl.when(jnp.logical_not(self.end))(lambda: self.down_copy().wait_send())


class StatSum:
    def __init__(self, place, parts, from_dp, every, out, send, recv):
        self.p, self.parts, self.from_dp, self.every, self.out = place, parts, from_dp, every, out
        self.send, self.recv = send, recv

    def dp_copy(self):
        return remote(
            self.parts.at[1 - self.p.d], self.from_dp, self.send.at[0], self.recv.at[0],
            dp=1 - self.p.d,
        )

    def copy(self, owner, k):
        piece = self.every.at[owner]
        return remote(
            piece, piece, self.send.at[k], self.recv.at[k], ctx=lax.rem(self.p.c + k, self.p.n)
        )

    def s0(self):
        self.dp_copy().start()

    def s1(self):
        self.dp_copy().wait_recv()
        both = self.parts[self.p.d].astype(F32) + self.from_dp[...].astype(F32)
        self.every[self.p.c] = both.astype(BF16)
        for k in range(1, self.p.n):
            self.copy(self.p.c, k).start()

    def s2(self):
        for k in range(1, self.p.n):
            self.copy(lax.rem(self.p.c + self.p.n - k, self.p.n), k).wait_recv()
        total = self.every[0].astype(F32)
        for j in range(1, self.p.n):
            total += self.every[j].astype(F32)
        self.out[...] = total

    def drain(self):
        self.dp_copy().wait_send()
        for k in range(1, self.p.n):
            self.copy(self.p.c, k).wait_send()


EARLY_ROWS = 384
PACK_CUTS = ((0, 256, 0, 192), (256, 128, 192, 128), (384, 128, 320, 128), (512, 128, 448, 128))
A_SUM, N2_SUM, MLP_SUM, N1_SUM = 0, 2, 4, 6


def cuts_of(rows, most):
    at, cuts = 0, []
    while at < rows:
        size = min(most, rows - at)
        cuts.append((at, size))
        at += size
    return cuts


def block_kernel(n_ctx, exchange, prefix, border, hid_in, cot_in, *refs):
    if exchange:
        (qkv_s, out_s, up_s, down_s, gain_s, shift_s) = refs[:6]
        (block_out, grad_out, ga_out, gb_out, gs) = refs[6:11]
        (wp, wo, wu, wd, ln, grads, gb_buf, gs_buf, b_fu, b_fm, a_fu, a_fm, s_dp, s_all,
         hid, cot, block, grad_in, ga, gb, load, keep, wsend, wrecv, gsend, grecv, ssend,
         srecv) = refs[11:39]
        refs = refs[39:]
    else:
        hid, cot = hid_in, cot_in
        (wp, wo, wu, wd, ln) = refs[:5]
        (block, grad_in, grads, gb, gs) = refs[5:10]
        refs = refs[10:]
    (attn, heads, lse, o_t, qs, kv, h1, m_row, l_row, o_acc, act, d_mlp, d_up, h2, n2_tot, d_attn,
     sbuf, rbuf, q_all, do_all, st_all, qos, qor, acc, qh, doh, dq_t, delta, d_pack, stats, ks, kr, kvs, kvr,
     t_mine, t_out, t_in, t_sum, tsend, trecv) = refs
    p = Place(n_ctx)
    c, n = p.c, n_ctx
    micro, rows, width = hid.shape
    half = rows // 2
    ff = wu.shape[1]
    parts = 2 if exchange else 1
    cols = width // parts
    own_rows = width // parts
    tiles = rows // 128
    loads = []
    if exchange:
        spot = pl.ds(pl.multiple_of(p.d * cols, cols), cols)
        pairs = ((hid_in, hid), (cot_in, cot), (up_s, wu.at[spot]), (down_s, wd.at[p.d]))
        loads = [pltpu.make_async_copy(a, b, load.at[i]) for i, (a, b) in enumerate(pairs)]
        loads[0].start()
    p.barrier(exchange, True, True)

    size = half // 2

    def tp_piece(kind, m, q, total):
        i = 2 * (kind + m) + q
        return TpSum(
            p, half, q * size, size, t_mine.at[i], t_out.at[i], t_in.at[i], t_sum.at[i], total,
            tsend.at[i], trecv.at[i],
        )

    def tp_sums(kind, m, total):
        return [tp_piece(kind, m, q, total) for q in range(2)]

    a_sums = [tp_sums(A_SUM, m, attn.at[m]) for m in range(micro)]
    n2_sums = [tp_sums(N2_SUM, m, n2_tot.at[m]) for m in range(micro)]
    mlp_sums = [tp_sums(MLP_SUM, m, block.at[m]) for m in range(micro)]
    n1_sums = [tp_sums(N1_SUM, m, n2_tot.at[m]) for m in range(micro)]

    def start_both(group, partial):
        for piece in group:
            piece.start_other(partial)
        for piece in group:
            piece.start_own(partial)

    def tile(i, base=0):
        return pl.ds(pl.multiple_of(base + i * 128, 128), 128)

    if exchange:
        mine = pl.ds(pl.multiple_of(p.d * own_rows, own_rows), own_rows)
        kv_part, q_part = wp.at[p.d, pl.ds(256, 384)], wp.at[p.d, pl.ds(0, 192)]
        places = (ln.at[p.d], kv_part, q_part, wo.at[p.d], wu.at[mine], wd.at[p.d])
        sources = (ln.at[p.d], kv_part, q_part, wo.at[p.d], up_s, down_s)

        def weight_copy(i):
            return remote(sources[i], places[i], wsend.at[i], wrecv.at[i], dp=1 - p.d)

        ln[p.d] = jnp.concatenate(
            [gain_s[...].astype(F32), shift_s[...].astype(F32), jnp.zeros((4, cols), F32)], axis=0
        )
        weight_copy(0).start()
        wp[p.d, 256:448, :] = qkv_s[1]
        wp[p.d, 448:640, :] = qkv_s[2]
        weight_copy(1).start()
        wp[p.d, 0:192, :] = qkv_s[0]
        for k in range(2):
            wp[k, 192:256, :] = jnp.zeros((64, cols), BF16)
        wo[p.d, 0:128, :] = out_s[64:192, :]
        wo[p.d, 128:192, :] = jnp.zeros((64, cols), BF16)
        wo[p.d, 192:256, :] = out_s[0:64, :]
        for piece in loads[1:]:
            piece.start()
        loads[0].wait()

    def weight_wait(*which):
        if exchange:
            for i in which:
                weight_copy(i).wait_recv()

    weight_wait(0)
    gain0, gain1, shift0, shift1 = (ln_row(ln, i) for i in range(4))
    for m in range(micro):
        @pl.loop(0, tiles)
        def _(i, m=m):
            xhat, _ = normalize(hid[m, tile(i), :].astype(F32))
            h1[tile(i, m * rows), :] = (xhat * gain0 + shift0).astype(BF16)

    def block_rows(b):
        return pl.ds(pl.multiple_of(b * half, half), half)

    def kv_copy(m, way, s, b):
        j, to = (c - s, c + 1) if way == 0 else (c + s, c - 1)
        piece = kv.at[m, j, block_rows(b)]
        return remote(piece, piece, ks.at[m, way, s, b], kr.at[m, way, s + 1, b], ctx=to)

    def kv_arrival(m, way, s, b):
        j, to = (c - s, c - 1) if way == 0 else (c + s, c + 1)
        piece = kv.at[m, j, block_rows(b)]
        return remote(piece, piece, ks.at[m, way, s, b], kr.at[m, way, s, b], ctx=to)

    def send_own(m, way):
        for b in range(2):
            kv_copy(m, way, 0, b).start()

    def has(way, s):
        return c - s >= 0 if way == 0 else c + s < n

    def sends(way, s):
        if way == 0:
            return jnp.logical_and(c - s >= 0, c + 1 < n)
        return jnp.logical_and(c + s < n, c - 1 >= 0)

    weight_wait(1)
    if exchange:
        weight_copy(2).start()
    for m in range(micro):
        @pl.loop(0, 2)
        def _(b, m=m):
            flat = pl.ds(pl.multiple_of(m * rows + b * half, half), half)
            kv[m, c, block_rows(b), :] = narrow(wp, h1[flat, :], 256, 384).astype(BF16)
            if m == 0:
                for way in range(2):
                    pl.when(sends(way, 0))(lambda way=way: kv_copy(0, way, 0, b).start())

    pl.when(c == 0)(lambda: send_own(1, 0))
    pl.when(c == n - 1)(lambda: send_own(1, 1))
    weight_wait(2)
    for piece in loads[1:]:
        piece.wait()
    if exchange:
        for i in range(3, 6):
            weight_copy(i).start()
    for m in range(micro):
        @pl.loop(0, 2)
        def _(b, m=m):
            flat = pl.ds(pl.multiple_of(m * rows + b * half, half), half)
            q = narrow(wp, h1[flat, :], 0, 256).astype(BF16).astype(F32)
            qs[m, block_rows(b), :] = (q * HEAD_DIM ** (-0.5)).astype(BF16)

    lanes = lax.broadcasted_iota(jnp.int32, (rows, 128), 1)

    def halves(value):
        zero = jnp.zeros_like(value)
        return jnp.where(lanes < 64, value, zero), jnp.where(lanes < 64, zero, value)

    def split_queries(m):
        qh[0], qh[1] = halves(qs[m, :, 0:128])
        qh[2] = qs[m, :, 128:256]

    def attend(m, j, b, limits):
        span = block_rows(b)
        k01 = kv[m, j, span, 0:128]
        k2v0 = kv[m, j, span, 128:256]
        t0 = k2v0.T
        t12 = kv[m, j, span, 256:384].T
        allowed = key_positions(border, 2 * j + b, half) <= limits
        for h in range(3):
            scores = dot_nt(k2v0 if h == 2 else k01, qh[h])
            scores = jnp.where(allowed, scores, NEG)
            old = m_row[h]
            top = jnp.maximum(old, jnp.max(scores, axis=0, keepdims=True))
            prob = jnp.exp(scores - top)
            fade = jnp.exp(old - top)
            m_row[h] = top
            l_row[h] = l_row[h] * fade + jnp.sum(prob, axis=0, keepdims=True)
            v_t = t0[64:128] if h == 0 else t12[(h - 1) * 64 : h * 64]
            o_acc[h] = o_acc[h] * fade + dot_nn(v_t, prob.astype(BF16))

    steps = 4 * (n - 1) + 2

    def at_step(t, at, jobs):
        @pl.when(t == at)
        def _():
            for job in jobs:
                job()

    def forward(m, side):
        limits = query_limits(border, prefix, m, c, rows)
        split_queries(m)
        m_row[...] = jnp.full(m_row.shape, NEG, F32)
        l_row[...] = jnp.zeros(l_row.shape, F32)
        o_acc[...] = jnp.zeros(o_acc.shape, F32)

        @pl.loop(0, steps)
        def _(t):
            own = t < 2
            s = jnp.where(own, 0, lax.div(t + 2, 4))
            b = jnp.where(own, t, lax.rem(lax.div(t, 2) + 1, 2))
            right = jnp.logical_and(jnp.logical_not(own), lax.rem(t, 2) == 0)
            left = jnp.logical_and(jnp.logical_not(own), lax.rem(t, 2) == 1)

            def arrive(way):
                kv_arrival(m, way, s, b).wait_recv()
                pl.when(sends(way, s))(lambda: kv_copy(m, way, s, b).start())
                if m == 0:
                    last = c if way == 0 else n - 1 - c
                    ready = jnp.logical_and(jnp.logical_and(s == last, b == 1), sends(way, 0))
                    pl.when(ready)(lambda: send_own(1, way))

            pl.when(jnp.logical_and(right, has(0, s)))(lambda: arrive(0))
            pl.when(jnp.logical_and(left, has(1, s)))(lambda: arrive(1))
            j = jnp.where(right, c - s, c + s)

            @pl.when(jnp.logical_and(j >= 0, j < n))
            def _():
                attend(m, j, b, limits)

            for at, jobs in side:
                at_step(t, at, jobs)

        flat = pl.ds(m * rows, rows)
        dq_t[128:192, :] = jnp.zeros((64, rows), F32)
        for h in range(3):
            norm = o_acc[h] / l_row[h]
            o_t[m, h] = norm
            lse[m, h : h + 1, :] = m_row[h] + jnp.log(l_row[h])
            at = 192 if h == 0 else (h - 1) * 64
            dq_t[at : at + 64, :] = norm
        heads[flat, :] = dq_t[...].T.astype(BF16)
        if m == 0:
            weight_wait(3)
        start_both(
            a_sums[m],
            lambda span: wide(wo, lambda w: dot_nn(heads[pl.ds(m * rows + span.start, size), :], w)),
        )

    def middle(m, i):
        return hid[m, tile(i), :].astype(F32) + BRANCH * attn[m, tile(i), :].astype(F32)

    def mlp_tiles(m, q):
        order = (q, q + tiles // 2)

        def rows_of(read):
            return jnp.concatenate([read(i) for i in order], axis=0)

        def keep_rows(ref, value, base=0):
            for k, i in enumerate(order):
                ref[tile(i, base), :] = value[k * 128 : (k + 1) * 128]

        xhat, _ = normalize(rows_of(lambda i: middle(m, i)))
        normed = (xhat * gain1 + shift1).astype(BF16)
        keep_rows(h2, normed, m * rows)
        up = dot_nn(normed, wu[...])
        active = gelu_value(up).astype(BF16)
        keep_rows(act, active, m * rows)
        down_grad = (BRANCH * rows_of(lambda i: cot[m, tile(i), :].astype(F32))).astype(BF16)
        keep_rows(d_mlp, down_grad, m * rows)
        keep_rows(d_up, (narrow(wd, down_grad) * gelu_slope(up)).astype(BF16), m * rows)
        keep_rows(block.at[m], wide(wd, lambda w: dot_nn(active, w)).astype(BF16))
        tp_piece(N2_SUM, m, q, n2_tot.at[m]).start(
            lambda span: dot_nt(d_up[pl.ds(m * rows + span.start, size), :], wu[...])
        )

    def mlp_start(m):
        start_both(mlp_sums[m], lambda span: block[m, span, :])

    def middle_gradient(m, q):
        n2_sums[m][q].finish()

        @pl.loop(0, 2)
        def _(core):
            i = q + (tiles // 2) * core
            xhat, inv = normalize(middle(m, i))
            dn = n2_tot[m, tile(i), :].astype(F32)
            grad = cot[m, tile(i), :].astype(F32) + norm_back(dn, xhat, inv, gain1)
            grad_in[m, tile(i), :] = grad
            d_attn[tile(i, m * rows), :] = (BRANCH * grad).astype(BF16)
            stats[1:2, :] += column_sums(dn * xhat)
            stats[3:4, :] += column_sums(dn)

    def write_block(m):
        for piece in mlp_sums[m]:
            piece.finish()
            piece.drain()

        @pl.loop(0, tiles)
        def _(i):
            out = middle(m, i) + BRANCH * block[m, tile(i), :].astype(F32)
            block[m, tile(i), :] = out.astype(BF16)

    def down_gradient():
        @pl.loop(0, ff // 256)
        def _(i):
            to = pl.ds(pl.multiple_of(i * 256, 256), 256)
            left = act[:, to]
            for k in range(parts):
                grads[k, to, :] = dot_tn(left, d_mlp[:, k * cols : (k + 1) * cols]).astype(BF16)

    def up_gradient():
        for k in range(parts):
            @pl.loop(0, own_rows // 128)
            def _(i, k=k):
                value = dot_tn(h2[:, tile(i, k * own_rows)], d_up[...]).astype(BF16)
                for q in range(ff // cols):
                    grads[k, tile(i, ff + q * own_rows), :] = value[:, q * cols : (q + 1) * cols]

    def out_gradient():
        at = ff + own_rows * (ff // cols)
        for k in range(parts):
            value = dot_tn(heads[...], d_attn[:, k * cols : (k + 1) * cols]).astype(BF16)
            grads[k, at : at + 128, :] = value[0:128]
            grads[k, at + 128 : at + 192, :] = value[192:256]

    early, late, norms = [], [], None
    stores = []

    def store(source, to, *index):
        if exchange:
            piece = pltpu.make_async_copy(source.at[index], to.at[index], keep.at[len(stores)])
            piece.start()
            stores.append(piece)

    if exchange:
        for i, (at, count) in enumerate(cuts_of(grads.shape[1], EARLY_ROWS)):
            cut = pl.ds(at, count)
            early.append(GradSum(
                p, grads.at[1 - p.d, cut], grads.at[p.d, cut], ga.at[cut], a_fu.at[cut],
                a_fm.at[cut], gsend.at[i], grecv.at[i],
            ))
        for i, (_, _, to, count) in enumerate(PACK_CUTS):
            cut, k = pl.ds(to, count), len(early) + i
            late.append(GradSum(
                p, gb_buf.at[1 - p.d, cut], gb_buf.at[p.d, cut], gb.at[cut], b_fu.at[cut],
                b_fm.at[cut], gsend.at[k], grecv.at[k],
            ))
        norms = StatSum(p, gs_buf, s_dp, s_all, gs, ssend, srecv)

    def stage(group, name):
        return [getattr(piece, name) for piece in group]

    def dkv_message(way, j, b, to):
        return remote(
            sbuf.at[j, block_rows(b)], rbuf.at[j + 1 - way, block_rows(b)],
            kvs.at[way, j, b], kvr.at[way, j, b], ctx=to,
        )

    def dkv_copy(way, j, b):
        return dkv_message(way, j, b, c + 1 if way == 0 else c - 1)

    def dkv_landed(way, j, b):
        return dkv_message(way, j, b, c - 1 if way == 0 else c + 1)

    gathered = (q_all, do_all, st_all)

    def qo_copy(kind, way, s):
        j, to = (c - s, c + 1) if way == 0 else (c + s, c - 1)
        piece = gathered[kind].at[j]
        return remote(piece, piece, qos.at[kind, way, s], qor.at[kind, way, s + 1], ctx=to)

    def qo_arrival(kind, way, s):
        j, to = (c - s, c - 1) if way == 0 else (c + s, c + 1)
        piece = gathered[kind].at[j]
        return remote(piece, piece, qos.at[kind, way, s], qor.at[kind, way, s], ctx=to)

    def qo_send(kind):
        for way in range(2):
            pl.when(sends(way, 0))(lambda way=way: qo_copy(kind, way, 0).start())

    def qo_step(kind, way, s):
        @pl.when(has(way, s))
        def _():
            qo_arrival(kind, way, s).wait_recv()
            pl.when(sends(way, s))(lambda: qo_copy(kind, way, s).start())

    def qo_steps(kind, s):
        for way in range(2):
            qo_step(kind, way, s)

    def send_queries(m):
        q_all[c] = qs[m].T[0:192]
        qo_send(0)

    def upstream(way):
        return c > 0 if way == 0 else c < n - 1

    def attend_back(m, j, b, limits, keys_too=True):
        span = block_rows(b)
        k01 = kv[m, j, span, 0:128]
        k2v0 = kv[m, j, span, 128:256]
        v12 = kv[m, j, span, 256:384]
        t01 = k01.T
        t2 = k2v0.T
        allowed = key_positions(border, 2 * j + b, half) <= limits
        sums = {}
        for h in range(3):
            scores = dot_nt(k2v0 if h == 2 else k01, qh[h])
            prob = jnp.exp(jnp.where(allowed, scores, NEG) - lse[m, h : h + 1, :])
            d_prob = dot_nt(k2v0 if h == 0 else v12, doh[h])
            d_scores = (prob * (d_prob - delta[h])).astype(BF16)
            k_t = t2[0:64] if h == 2 else t01[h * 64 : (h + 1) * 64]
            dq_t[h * 64 : (h + 1) * 64, :] += dot_nn(k_t, d_scores)
            if keys_too:
                dk = dot_nn(d_scores, qh[h])
                dv = dot_nn(prob.astype(BF16), doh[h])
                k_at, v_at = (1 if h == 2 else 0), (1 if h == 0 else 2)
                sums[k_at] = dk if k_at not in sums else sums[k_at] + dk
                sums[v_at] = dv if v_at not in sums else sums[v_at] + dv
        for k in sums:
            acc[span, k * 128 : (k + 1) * 128] = sums[k]

    def attend_keys(m, j, b):
        span = block_rows(b)
        k01 = kv[m, c, span, 0:128]
        k2v0 = kv[m, c, span, 128:256]
        v12 = kv[m, c, span, 256:384]
        limits = query_limits(border, prefix, m, j, rows)
        allowed = key_positions(border, 2 * c + b, half) <= limits
        zero = jnp.zeros((64, rows), BF16)
        for h in range(3):
            q_h = q_all[j, h * 64 : (h + 1) * 64, :]
            q_h = jnp.concatenate([zero, q_h] if h == 1 else [q_h, zero], axis=0)
            do_h = do_all[j, h * 64 : (h + 1) * 64, :]
            do_h = jnp.concatenate([do_h, zero] if h == 1 else [zero, do_h], axis=0)
            scores = dot_nn(k2v0 if h == 2 else k01, q_h)
            prob = jnp.exp(jnp.where(allowed, scores, NEG) - st_all[j, h : h + 1, :])
            d_prob = dot_nn(k2v0 if h == 0 else v12, do_h)
            d_scores = (prob * (d_prob - st_all[j, 3 + h : 4 + h, :])).astype(BF16)
            k_at, v_at = (128 if h == 2 else 0), (128 if h == 0 else 256)
            acc[span, k_at : k_at + 128] += dot_nt(d_scores, q_h)
            acc[span, v_at : v_at + 128] += dot_nt(prob.astype(BF16), do_h)

    def head_gradients(m):
        upper = d_attn[pl.ds(m * rows, rows), :]
        share = wo.shape[2]
        d_heads_t = dot_nt(wo[0], upper[:, 0:share])
        for i in range(1, wo.shape[0]):
            d_heads_t += dot_nt(wo[i], upper[:, i * share : (i + 1) * share])
        for h in range(3):
            at = 192 if h == 0 else (h - 1) * 64
            delta[h] = jnp.sum(d_heads_t[at : at + 64] * o_t[m, h], axis=0, keepdims=True)
            if m > 0:
                do_all[c, h * 64 : (h + 1) * 64, :] = d_heads_t[at : at + 64].astype(BF16)
                st_all[c, h : h + 1, :] = lse[m, h : h + 1, :]
                st_all[c, 3 + h : 4 + h, :] = delta[h]
        if m > 0:
            st_all[c, 6:8, :] = jnp.zeros((2, rows), F32)
            qo_send(2)
            qo_send(1)
        d_heads = narrow(wo, upper).astype(BF16)
        doh[0] = d_heads[:, 128:256]
        doh[1], doh[2] = halves(d_heads[:, 0:128])
        split_queries(m)
        dq_t[...] = jnp.zeros(dq_t.shape, F32)

    def query_gradient(m):
        flat = pl.ds(m * rows, rows)
        d_pack[flat, 0:256] = (dq_t[...].T * HEAD_DIM ** (-0.5)).astype(BF16)

    def backward_end(m):
        d_pack[pl.ds(m * rows, rows), 256:640] = acc[...].astype(BF16)
        start_both(
            n1_sums[m],
            lambda span: wide(wp, lambda w: dot_nn(d_pack[pl.ds(m * rows + span.start, size), :], w)),
        )

    def backward(m, side):
        limits = query_limits(border, prefix, m, c, rows)
        head_gradients(m)

        @pl.loop(0, steps)
        def _(t):
            own = t >= steps - 2
            s = n - 1 - lax.div(t, 4)
            b = jnp.where(own, t - (steps - 2), lax.rem(lax.div(t, 2), 2))
            right = jnp.logical_and(lax.rem(t, 2) == 0, jnp.logical_not(own))
            left = jnp.logical_and(lax.rem(t, 2) == 1, jnp.logical_not(own))
            j = jnp.where(own, c, jnp.where(right, c + s, c - s))
            span = block_rows(b)

            for at, jobs in side:
                at_step(t, at, jobs)

            @pl.when(jnp.logical_and(j >= 0, j < n))
            def _():
                attend_back(m, j, b, limits)

                def pass_on(way):
                    @pl.when(upstream(way))
                    def _():
                        dkv_landed(way, j, b).wait_recv()
                        sbuf[j, span, :] = (
                            acc[span, :] + rbuf[j + 1 - way, span, :].astype(F32)
                        ).astype(BF16)

                    @pl.when(jnp.logical_not(upstream(way)))
                    def _():
                        sbuf[j, span, :] = acc[span, :].astype(BF16)

                    dkv_copy(way, j, b).start()

                pl.when(right)(lambda: pass_on(0))
                pl.when(left)(lambda: pass_on(1))

        for way in range(2):
            @pl.when(upstream(way))
            def _(way=way):
                for b in range(2):
                    span = block_rows(b)
                    dkv_landed(way, c, b).wait_recv()
                    acc[span, :] += rbuf[c + 1 - way, span, :].astype(F32)

        query_gradient(m)
        backward_end(m)

    def backward_last(m, side, between, side_keys):
        limits = query_limits(border, prefix, m, c, rows)
        head_gradients(m)

        @pl.loop(0, 2)
        def _(b):
            attend_back(m, c, b, limits)

        @pl.loop(0, 2 * (n - 1))
        def _(t):
            j = lax.rem(c + 1 + lax.div(t, 2), n)
            attend_back(m, j, lax.rem(t, 2), limits, keys_too=False)
            for at, jobs in side:
                at_step(t, at, jobs)

        query_gradient(m)
        do(between)

        @pl.loop(0, 2 * (n - 1))
        def _(t):
            s = 1 + lax.div(t, 2)
            for way in range(2):
                @pl.when(jnp.logical_and(lax.rem(t, 2) == way, has(way, s)))
                def _(way=way):
                    pl.when(s > 2)(lambda: qo_step(2, way, s))
                    pl.when(s > 2)(lambda: qo_step(1, way, s))
                    for b in range(2):
                        attend_keys(m, c - s if way == 0 else c + s, b)
            for at, jobs in side_keys:
                at_step(t, at, jobs)

        backward_end(m)

    def finish_rows(m, q):
        n1_sums[m][q].finish()

        @pl.loop(0, 2)
        def _(core):
            i = q + (tiles // 2) * core
            xhat, inv = normalize(hid[m, tile(i), :].astype(F32))
            dn = n2_tot[m, tile(i), :].astype(F32)
            grad_in[m, tile(i), :] += norm_back(dn, xhat, inv, gain0)
            stats[0:1, :] += column_sums(dn * xhat)
            stats[2:3, :] += column_sums(dn)

    def pack_part(to, k, at, count, first, kept):
        left = h1[:, pl.ds(pl.multiple_of(k * cols, 128), cols)]
        value = dot_tn(d_pack[:, at : at + count], left)
        to[first : first + kept, :] = value[0:kept].astype(to.dtype)

    def do(jobs):
        for job in jobs:
            job()

    def each(group, name):
        return lambda: do(stage(group, name))

    def middle_ready(m):
        for q in range(2):
            middle_gradient(m, q)
        for piece in n2_sums[m]:
            piece.drain()

    def mlp_piece(m, q):
        tp_piece(A_SUM, m, q, attn.at[m]).finish()
        mlp_tiles(m, q)

    def mlp_pieces(m):
        @pl.loop(0, 2)
        def _(q):
            mlp_piece(m, q)

    def by_place(at_end, inside):
        return jnp.where(jnp.logical_or(c == 0, c == n - 1), at_end, inside)

    stats[...] = jnp.zeros(stats.shape, F32)
    (a0, a1), (x0, x1), (u0, u1), (y0, y1) = a_sums, n2_sums, mlp_sums, n1_sums
    forward(0, [])
    forward(1, [
        (0, [each(a0, "step2")]),
        (3, [a0[0].step3]),
        (4, [
            lambda: weight_wait(4, 5), lambda: mlp_piece(0, 0), a0[1].step3, x0[0].step2,
            lambda: mlp_piece(0, 1),
        ]),
        (5, [x0[1].step2]),
    ])
    do(stage(x0, "step3"))
    do(stage(a1, "step2"))
    middle_ready(0)
    spot = by_place(5, 0)
    send_queries(1)
    backward(0, [
        (2, [lambda: qo_steps(0, 1)]),
        (spot, [a1[0].step3, a1[1].step3, lambda: mlp_pieces(1)]),
        (6, [lambda: qo_steps(0, 2)]),
        (spot + 2, [each(x1, "step2"), lambda: mlp_start(0)]),
        (spot + 4, [down_gradient, each(early[0:2], "s0")]),
        (spot + 6, [up_gradient, each(early[2:-1], "s0"), each(u0, "step2"), each(x1, "step3")]),
        (steps - 1, [lambda: mlp_start(1)] + [lambda s=s: qo_steps(0, s) for s in range(3, n)]),
    ])
    def at_place(ends, jobs):
        @pl.when(by_place(1, 0) == ends)
        def _():
            do(jobs)

    at_place(1, stage(early[0:1], "s1"))
    middle_ready(1)
    query_pieces = []

    def pack_pieces(first, end):
        @pl.loop(0, 2)
        def _(i):
            k = lax.rem(p.d + 1 + i, 2)
            for piece, cut in list(zip(late, PACK_CUTS))[first:end]:
                pack_part(gb_buf.at[k], k, *cut)
                pl.when(i == 0)(piece.s0)

    if exchange:
        query_pieces = [lambda: pack_pieces(0, 1)]
    backward_last(1, [
        (0, [out_gradient, each(early[-1:], "s0"), each(y0, "step2")]),
        (by_place(0, 5), [each(early[1:2], "s1")]),
        (2, [lambda: qo_steps(2, 1), lambda: qo_steps(1, 1)]),
        (by_place(9, 3), [each(early[0:1], "s1")]),
        (5, [lambda: qo_steps(2, 2), lambda: qo_steps(1, 2)]),
        (by_place(4, 9), [each(early[2:3], "s1")]),
    ], query_pieces, [
        (by_place(0, 9), [each(early[3:4], "s1")]),
        (0, [each(early[0:1], "s2")]),
        (1, [each(y0, "step3"), each(u0, "step3")]),
        (by_place(9, 2), [each(early[2:3], "s1")]),
        (by_place(2, 9), [each(early[4:5], "s1")]),
        (3, [each(u1, "step2"), each(early[1:2], "s2")]),
        (by_place(9, 5), [each(early[3:4], "s1")]),
    ])
    if exchange:
        pack_pieces(1, len(late))
    else:
        for cut in PACK_CUTS:
            pack_part(gb, 0, *cut)
    do(stage(y1, "step2"))
    if exchange:
        at_place(1, stage(late[0:1], "s1"))
        at_place(0, stage(early[2:3], "s2"))
    for q in range(2):
        finish_rows(0, q)
    store(grad_in, grad_out if exchange else None, 0)
    if exchange:
        at_place(1, stage(late[1:3], "s1"))
        at_place(0, stage(early[4:5] + late[0:1], "s1"))
    do(stage(u1, "step3"))
    write_block(0)
    store(block, block_out if exchange else None, 0)
    if exchange:
        at_place(1, stage(late[3:], "s1"))
        at_place(0, stage(late[1:2], "s1") + stage(early[3:4], "s2"))
    for q in range(2):
        y1[q].step3()
    for q in range(2):
        finish_rows(1, q)
    store(grad_in, grad_out if exchange else None, 1)
    if exchange:
        for k in range(2):
            cut = slice(k * cols, (k + 1) * cols)
            gs_buf[k] = jnp.concatenate([stats[:, cut], jnp.zeros((8, cols), F32)], axis=0).astype(BF16)
        norms.s0()
        at_place(0, stage(early[4:5], "s2") + stage(late[2:], "s1") + stage(late[0:1], "s2"))
    write_block(1)
    store(block, block_out if exchange else None, 1)
    if exchange:
        norms.s1()
        at_place(0, stage(late[1:], "s2"))
        for group, held, to, cuts in (
            (early, ga, ga_out, cuts_of(ga.shape[0], EARLY_ROWS)),
            (late, gb, gb_out, [cut[2:] for cut in PACK_CUTS]),
        ):
            for piece, (at, count) in zip(group, cuts):
                piece.s3()
                store(held, to, pl.ds(at, count))
        norms.s2()
        for piece in early + late + [norms]:
            piece.drain()
        for piece in stores:
            piece.wait()
        for i in range(6):
            weight_copy(i).wait_send()
    else:
        gs[...] = stats[...]
    for b in range(2):
        for m in range(micro):
            for way in range(2):
                for s in range(n - 1):
                    pl.when(sends(way, s))(
                        lambda m=m, way=way, s=s, b=b: kv_copy(m, way, s, b).wait_send()
                    )
        for j in range(n):
            pl.when(c < j)(lambda j=j, b=b: dkv_copy(0, j, b).wait_send())
            pl.when(c > j)(lambda j=j, b=b: dkv_copy(1, j, b).wait_send())
    for kind in range(3):
        for way in range(2):
            for s in range(n - 1):
                pl.when(sends(way, s))(
                    lambda kind=kind, way=way, s=s: qo_copy(kind, way, s).wait_send()
                )
    for piece in a0 + a1 + y0 + y1:
        piece.drain()


def run_block(n_ctx, exchange, prefix, border, hid, cot, weights, ff):
    micro, rows, width = hid.shape
    half = rows // 2
    total = micro * rows
    parts = 2 if exchange else 1
    cols = width // parts
    sds = jax.ShapeDtypeStruct
    vmem = pltpu.VMEM
    sems = pltpu.SemaphoreType.DMA
    grad_rows = ff + cols * (ff // cols) + 192
    outs = [sds((micro, rows, width), BF16), sds((micro, rows, width), F32)]
    scratch = []
    if exchange:
        outs += [sds((grad_rows, cols), BF16), sds((576, cols), BF16), sds((16, cols), F32)]
        pieces = len(cuts_of(grad_rows, EARLY_ROWS)) + len(PACK_CUTS)
        scratch += [
            vmem((2, 640, cols), BF16), vmem((2, 256, cols), BF16), vmem((width, ff), BF16),
            vmem((2, ff, cols), BF16), vmem((2, 8, cols), F32),
            vmem((2, grad_rows, cols), BF16), vmem((2, 576, cols), BF16), vmem((2, 16, cols), BF16),
            vmem((576, cols), BF16), vmem((576, cols), BF16),
            vmem((grad_rows, cols), BF16), vmem((grad_rows, cols), BF16),
            vmem((16, cols), BF16), vmem((n_ctx, 16, cols), BF16),
            vmem(hid.shape, BF16), vmem(hid.shape, BF16), vmem(hid.shape, BF16), vmem(hid.shape, F32),
            vmem((grad_rows, cols), BF16), vmem((576, cols), BF16), sems((4,)),
            sems((2 * micro + pieces,)),
            sems((6,)), sems((6,)), sems((pieces, 4)), sems((pieces, 4)),
            sems((n_ctx,)), sems((n_ctx,)),
        ]
    else:
        outs += [
            sds((1, grad_rows, cols), BF16), sds((576, width), F32), sds((8, width), F32)
        ]
    scratch += [
        vmem((micro, rows, width), BF16), vmem((total, 256), BF16), vmem((micro, 8, rows), F32),
        vmem((micro, 3, 64, rows), F32), vmem((micro, rows, 256), BF16),
        vmem((micro, n_ctx, rows, 384), BF16), vmem((total, width), BF16),
        vmem((3, 1, rows), F32), vmem((3, 1, rows), F32), vmem((3, 64, rows), F32),
        vmem((total, ff), BF16), vmem((total, width), BF16), vmem((total, ff), BF16),
        vmem((total, width), BF16), vmem((micro, rows, width), BF16), vmem((total, width), BF16),
        vmem((n_ctx, rows, 384), BF16), vmem((n_ctx + 1, rows, 384), BF16),
        vmem((n_ctx, 192, rows), BF16), vmem((n_ctx, 192, rows), BF16), vmem((n_ctx, 8, rows), F32),
        sems((3, 2, n_ctx + 1)), sems((3, 2, n_ctx + 1)),
        vmem((rows, 384), F32), vmem((3, rows, 128), BF16), vmem((3, rows, 128), BF16),
        vmem((256, rows), F32), vmem((3, 1, rows), F32), vmem((total, 640), BF16),
        vmem((8, width), F32),
        sems((micro, 2, n_ctx + 1, 2)), sems((micro, 2, n_ctx + 1, 2)),
        sems((2, n_ctx, 2)), sems((2, n_ctx, 2)),
    ]
    scratch += [vmem((16, half // 2, width), BF16)] * 4 + [sems((16, 3))] * 2
    smem = pl.BlockSpec(memory_space=pltpu.SMEM)
    stay = pl.BlockSpec(memory_space=pl.ANY)
    specs = vmem_specs(2 + len(weights))
    if exchange:
        specs = [stay, stay] + vmem_specs(2) + [stay, stay] + vmem_specs(2)
    return pl.pallas_call(
        functools.partial(block_kernel, n_ctx, exchange),
        out_shape=outs,
        in_specs=[smem, smem] + specs,
        out_specs=([stay] * 4 + vmem_specs(1)) if exchange else vmem_specs(len(outs)),
        scratch_shapes=scratch,
        compiler_params=pltpu.CompilerParams(
            collective_id=0, has_side_effects=True, vmem_limit_bytes=67043328
        ),
        name="block_both_ways",
    )(prefix, border, hid, cot, *weights)


def unpack_kernel(
    block_in, grad_in, down_in, left_in, right_in, out_in, qkv_in, gs,
    block, grad, down, up, qkv, out, gains, shifts,
):
    cols = down_in.shape[1]
    block[...] = block_in[...]
    grad[...] = grad_in[...]
    down[...] = down_in[...].astype(F32)
    up[:, 0:cols] = left_in[...].astype(F32)
    up[:, cols : 2 * cols] = right_in[...].astype(F32)
    qkv[...] = qkv_in[...].astype(F32)

    @pl.when(pl.program_id(0) == 0)
    def _():
        out[0:64, :] = out_in[128:192, :].astype(F32)
        out[64:192, :] = out_in[0:128, :].astype(F32)
        gains[...] = gs[0:2]
        shifts[...] = gs[2:4]


UNPACK_STEPS = 2


def unpack(block, grad_in, ga, gb, gs, ff):
    cols = ga.shape[1]
    d, u, q = ff // UNPACK_STEPS, cols // UNPACK_STEPS, gb.shape[0] // UNPACK_STEPS
    total, width = block.shape
    r = total // UNPACK_STEPS
    sds = jax.ShapeDtypeStruct

    def rows(count, wide_by, first=0):
        return pl.BlockSpec((count, wide_by), lambda i: (first + i, 0))

    def whole(*shape, at=0):
        return pl.BlockSpec(shape, lambda i: (at, 0))

    return pl.pallas_call(
        unpack_kernel,
        grid=(UNPACK_STEPS,),
        out_shape=[
            sds((total, width), BF16), sds((total, width), F32), sds((ff, cols), F32),
            sds((cols, 2 * cols), F32), sds(gb.shape, F32), sds((192, cols), F32),
            sds((2, cols), F32), sds((2, cols), F32),
        ],
        in_specs=[
            rows(r, width), rows(r, width), rows(d, cols), rows(u, cols, ff // u),
            rows(u, cols, (ff + cols) // u), whole(192, cols, at=(ff + 2 * cols) // 192), rows(q, cols),
            whole(*gs.shape),
        ],
        out_specs=[
            rows(r, width), rows(r, width), rows(d, cols), rows(u, 2 * cols), rows(q, cols),
            whole(192, cols), whole(2, cols), whole(2, cols),
        ],
        name="unpack_outputs",
    )(block, grad_in, ga, ga, ga, ga, gb, gs)


def body(
    hidden_in, prefix, block_order, qkv_weight, out_weight, up_weight, down_weight, ln_gains,
    ln_shifts, cotangent,
):
    micro, _, tokens, width = hidden_in.shape
    n_ctx = lax.axis_size("ctx")
    exchange = lax.axis_size("dp") == 2 and n_ctx % 2 == 0
    ff = up_weight.shape[1]
    params = (qkv_weight, out_weight, up_weight, down_weight, ln_gains, ln_shifts)
    turned = jnp.swapaxes(qkv_weight, 1, 2)
    weights = (turned,) + params[1:] if exchange else pack_weights(*params)
    hid, cot = hidden_in[:, 0], cotangent[:, 0]
    block, grad_in, ga, gb, gs = run_block(
        n_ctx, exchange, prefix[:, 0], block_order, hid, cot, weights, ff
    )
    if exchange:
        total = micro * tokens
        block, grad_in, g_down, g_up, g_qkv, g_out, g_gains, g_shifts = unpack(
            block.reshape(total, width), grad_in.reshape(total, width), ga, gb, gs, ff
        )
        shape = (micro, 1, tokens, width)
        g_qkv = jnp.swapaxes(g_qkv.reshape(turned.shape), 1, 2)
        return (
            block.reshape(shape), grad_in.reshape(shape), g_qkv, g_out, g_up, g_down, g_gains,
            g_shifts,
        )
    ga = ga[0].astype(F32)
    g_out = ga[ff + width :]
    whole = lax.psum(
        (
            jnp.swapaxes(gb.reshape(3, 192, -1), 1, 2),
            jnp.concatenate([g_out[128:], g_out[:128]], axis=0), ga[ff : ff + width], ga[:ff],
            gs[0:2], gs[2:4],
        ),
        "ctx",
    )
    owned = [
        lax.psum_scatter(v, "dp", scatter_dimension=d, tiled=True)
        for v, d in zip(whole, (1, 1, 0, 1, 1, 1))
    ]
    return (block[:, None], grad_in[:, None], *owned)


def solution(mesh):
    in_specs = (
        P(None, "dp", "ctx", None), P(None, "dp"), P(), P(None, "dp", "tp"), P("tp", "dp"),
        P("dp", "tp"), P("tp", "dp"), P(None, "dp"), P(None, "dp"), P(None, "dp", "ctx", None),
    )
    out_specs = (
        P(None, "dp", "ctx", None), P(None, "dp", "ctx", None), P(None, "dp", "tp"),
        P("tp", "dp"), P("dp", "tp"), P("tp", "dp"), P(None, "dp"), P(None, "dp"),
    )
    return jax.shard_map(body, mesh=mesh, in_specs=in_specs, out_specs=out_specs, check_vma=False)
```
